512 devices in a mesh: gz: 64 (over z_lo, x, y), gy: 8 (over z_hi, core).
Axes of the slice: x: 4, y: 4, z: 16 (z_hi: 4, z_lo: 4; z = z_hi * 4 + z_lo), core: 2. Of those that a mesh axis runs over, the one named last changes fastest.
Arguments:
- levels: float32 [4, 256, 64, 512], P(None, 'gz', 'gy'), may hold values from -20 to 20
- ct_image: float32 [256, 64, 512], P('gz', 'gy'), may hold values from -4 to 4
- region_means: float32 [16], replicated, may hold values from -1.5 to 1.5
Outputs:
- evolved: float32 [4, 256, 64, 512], P(None, 'gz', 'gy')
- regularized: float32 [4, 256, 64, 512], P(None, 'gz', 'gy')
The draws below stay inside these ranges and needn't reach their ends.
All inputs are finite; a program needn't handle non-finite values.
Results may differ from the reference program's by a relative error of at most 0.000022.
Values sent between devices are 32-bit elements; how exact they have to be, the bound alone decides.
A program may use at most 64 MiB of HBM per device.

```python
import math
import jax
import jax.numpy as jnp
from jax import lax

LEVELS = 4
PHASES = 16
UPDATES = 2
KERNEL = 200
NX = 512
NZ = 256
NY = 64


def step_profile(key):
    subkeys = jax.random.split(key, 2)
    edge_low = 0.05 * NX
    edge_high = max(edge_low, min(0.45 * NX, NX - KERNEL - 0.1 * NX))
    fraction = jax.random.uniform(subkeys[0], (LEVELS,), jnp.float32, 0.0, 1.0)
    edge = edge_low + fraction * (edge_high - edge_low)
    direction = jax.random.randint(subkeys[1], (LEVELS,), 0, 2)
    position = jnp.arange(NX, dtype=jnp.float32)
    mirrored = jnp.where(direction[:, None] == 1, NX - 1.0 - position[None, :], position[None, :])
    return -4.5 + 11.5 * jnp.tanh((mirrored - edge[:, None]) / 1.5)


def draw_levels(key, part):
    subkeys = jax.random.split(key, 4)
    full_shape = (LEVELS, NZ, NY, NX)
    profile = step_profile(subkeys[3])[:, None, None, :]
    rough_part = jnp.clip(1.5 * jax.random.normal(subkeys[0], full_shape, jnp.float32), -6.0, 6.0)
    return jnp.clip(rough_part + profile, -19.8, 19.8)


def steps_of(stream_key, shape, cuts, smallest, top_value):
    gain, own = 1.0, jax.random.fold_in(stream_key, 6)
    for axis_at, shards_of in cuts:
        draws = jnp.exp(jax.random.uniform(jax.random.fold_in(own, axis_at), (shards_of,), jnp.float32, smallest / len(cuts), top_value / len(cuts)))
        gain = gain * jnp.repeat(draws, shape[axis_at] // shards_of).reshape([-1 if axis == axis_at else 1 for axis in range(len(shape))])
    return gain


def scatter_about(key, extent, spread, reach, cuts=(), kind=jnp.bfloat16):
    factor_of = steps_of(key, extent, cuts, -0.22, 0.18) if cuts else 1.0
    entries = jax.random.normal(key, extent, jnp.float32) * spread * factor_of
    return jnp.minimum(jnp.maximum(entries, -reach), reach).astype(kind)


def setup_inputs(seed: int = 0) -> dict:
    key_list = jax.random.split(jax.random.key(seed), 4)
    return {
        "levels": draw_levels(jax.random.fold_in(key_list[3], 71), 0),
        "ct_image": scatter_about(key_list[1], (NZ, NY, NX), 1.0, 4.0, ((0, 64), (1, 8)), jnp.float32),
        "region_means": jnp.clip(jax.random.uniform(key_list[2], (PHASES,), jnp.float32, -1.5, 1.5), -1.5, 1.5),
    }


PENALTY = 0.0005
STEP_SIZE = 0.5


def evolve(level_pad, picture, region_means):
    interior = level_pad[:, 1:-1, 1:-1, :]
    side_x = jnp.pad(interior, ((0, 0), (0, 0), (0, 0), (1, 1)))
    laplace = level_pad[:, 2:, 1:-1, :] + level_pad[:, :-2, 1:-1, :]
    laplace = laplace + level_pad[:, 1:-1, 2:, :] + level_pad[:, 1:-1, :-2, :]
    laplace = laplace + side_x[..., 2:] + side_x[..., :-2] - 6.0 * interior
    heaviside = 0.5 + jnp.arctan(interior) / math.pi
    delta_term = 1.0 / (math.pi * (1.0 + interior * interior))
    forces = [jnp.zeros_like(interior[0]) for level_id in range(LEVELS)]
    for phase_id in range(PHASES):
        differ = picture - region_means[phase_id]
        energy = differ * differ
        factors = []
        for level_id in range(LEVELS):
            if (phase_id >> level_id) & 1:
                factors.append(heaviside[level_id])
            else:
                factors.append(1.0 - heaviside[level_id])
        for level_id in range(LEVELS):
            sign_value = 1.0 if (phase_id >> level_id) & 1 else -1.0
            others = energy
            for other_id in range(LEVELS):
                if other_id != level_id:
                    others = others * factors[other_id]
            forces[level_id] = forces[level_id] + sign_value * others
    force_all = jnp.stack(forces, axis=0)
    return interior + STEP_SIZE * delta_term * (laplace - force_all)


def minplus_lines(field_in, line_axis, kernel_reach):
    moved_field = jnp.moveaxis(field_in, line_axis, -1)
    line_shape = moved_field.shape
    line_len = line_shape[-1]
    line_rows = moved_field.reshape(-1, line_len)
    row_count = line_rows.shape[0]
    positions = jnp.arange(line_len, dtype=jnp.float32)
    distance = positions[:, None] - positions[None, :]
    penalty_table = jnp.where(jnp.abs(distance) <= kernel_reach, PENALTY * (distance * distance), jnp.inf).astype(line_rows.dtype)
    row_limit = max(1, 4194304 // (line_len * line_len))
    row_block = 1
    while row_block * 2 <= row_limit and row_count % (row_block * 2) == 0:
        row_block = row_block * 2
    grouped = line_rows.reshape(row_count // row_block, row_block, line_len)

    def block_min(block_rows):
        return jnp.min(block_rows[:, None, :] + penalty_table[None, :, :], axis=2)

    result_rows = lax.map(block_min, grouped)
    return jnp.moveaxis(result_rows.reshape(line_shape), -1, line_axis)


def reference(levels, ct_image, region_means):
    current = levels
    for update_round in range(UPDATES):
        padded = jnp.pad(current, ((0, 0), (1, 1), (1, 1), (0, 0)))
        current = evolve(padded, ct_image, region_means)
    smoothed = minplus_lines(current, 3, KERNEL)
    smoothed = minplus_lines(smoothed, 1, KERNEL)
    smoothed = minplus_lines(smoothed, 2, KERNEL)
    return current, smoothed
```

```python
import math

import jax
import jax.numpy as jnp
from jax import lax
from jax.experimental import pallas as pl
from jax.experimental.pallas import tpu as pltpu
from jax.sharding import PartitionSpec as P

LEVELS = 4
PHASES = 16
UPDATES = 2
KERNEL = 200


PENALTY = 0.0005
STEP_SIZE = 0.5


def arctan(x):
    ax = jnp.abs(x)
    big = ax > 2.414213562373095
    mid = ax > 0.4142135623730950
    z_big = -1.0 / jnp.where(big, ax, 1.0)
    z_mid = (ax - 1.0) / (ax + 1.0)
    z = jnp.where(big, z_big, jnp.where(mid, z_mid, ax))
    base = jnp.where(big, math.pi / 2, jnp.where(mid, math.pi / 4, 0.0))
    zz = z * z
    poly = (((8.05374449538e-2 * zz - 1.38776856032e-1) * zz + 1.99777106478e-1) * zz
            - 3.33329491539e-1) * zz * z + z
    r = base + poly
    return jnp.where(x < 0, -r, r)


def evolve_kernel(means_ref, cur_ref, zlo_ref, zhi_ref, ylo_ref, yhi_ref, ct_ref, out_ref):
    nz, ny, nx = cur_ref.shape[1], cur_ref.shape[2], cur_ref.shape[3]
    shape = (ny, nx)
    xi = lax.broadcasted_iota(jnp.int32, shape, 1)
    yi = lax.broadcasted_iota(jnp.int32, shape, 0)
    xa = pltpu.roll(xi, 1, 1)
    xb = pltpu.roll(xi, nx - 1, 1)
    xa_ok = jnp.abs(xa - xi) == 1
    xb_ok = jnp.abs(xb - xi) == 1
    ya = pltpu.roll(yi, 1, 0)
    yb = pltpu.roll(yi, ny - 1, 0)
    ya_ok = jnp.abs(ya - yi) == 1
    yb_ok = jnp.abs(yb - yi) == 1
    low_row = yi == 0
    means = [means_ref[p] for p in range(PHASES)]
    for z in range(nz):
        picture = ct_ref[z]
        energy = []
        for p in range(PHASES):
            differ = picture - means[p]
            energy.append(differ * differ)
        phis, lap, g1, g0, dl = [], [], [], [], []
        for k in range(LEVELS):
            c = cur_ref[k, z]
            zm = zlo_ref[k, 0] if z == 0 else cur_ref[k, z - 1]
            zp = zhi_ref[k, 0] if z == nz - 1 else cur_ref[k, z + 1]
            edge = jnp.where(low_row, ylo_ref[k, z], yhi_ref[k, z])
            ym = jnp.where(ya_ok, pltpu.roll(c, 1, 0), edge)
            yp = jnp.where(yb_ok, pltpu.roll(c, ny - 1, 0), edge)
            xm = jnp.where(xa_ok, pltpu.roll(c, 1, 1), 0.0)
            xp = jnp.where(xb_ok, pltpu.roll(c, nx - 1, 1), 0.0)
            lap.append(zm + zp + ym + yp + xm + xp - 6.0 * c)
            h = 0.5 + arctan(c) / math.pi
            g1.append(h)
            g0.append(1.0 - h)
            dl.append(1.0 / (math.pi * (1.0 + c * c)))
            phis.append(c)
        g = (g0, g1)
        pair_lo = {(a, b): g[a][0] * g[b][1] for a in (0, 1) for b in (0, 1)}
        pair_hi = {(a, b): g[a][2] * g[b][3] for a in (0, 1) for b in (0, 1)}
        for k in range(LEVELS):
            force = None
            for q in range(PHASES // 2):
                low = q & ((1 << k) - 1)
                high = (q >> k) << (k + 1)
                p0 = high | low
                p1 = p0 | (1 << k)
                bits = [(p0 >> j) & 1 for j in range(LEVELS)]
                if k == 0:
                    prod = g[bits[1]][1] * pair_hi[(bits[2], bits[3])]
                elif k == 1:
                    prod = g[bits[0]][0] * pair_hi[(bits[2], bits[3])]
                elif k == 2:
                    prod = pair_lo[(bits[0], bits[1])] * g[bits[3]][3]
                else:
                    prod = pair_lo[(bits[0], bits[1])] * g[bits[2]][2]
                term = (energy[p1] - energy[p0]) * prod
                force = term if force is None else force + term
            out_ref[k, z] = phis[k] + STEP_SIZE * dl[k] * (lap[k] - force)


def evolve_step(current, picture, region_means):
    fwd_z = [(i, i + 1) for i in range(lax.axis_size("gz") - 1)]
    fwd_y = [(i, i + 1) for i in range(lax.axis_size("gy") - 1)]
    bwd_z = [(t, s) for s, t in fwd_z]
    bwd_y = [(t, s) for s, t in fwd_y]
    nz, ny = current.shape[1], current.shape[2]
    zlo = lax.ppermute(current[:, nz - 1:nz], "gz", fwd_z)
    zhi = lax.ppermute(current[:, 0:1], "gz", bwd_z)
    ylo = lax.ppermute(current[:, :, ny - 1:ny], "gy", fwd_y)
    yhi = lax.ppermute(current[:, :, 0:1], "gy", bwd_y)
    vmem = pl.BlockSpec(memory_space=pltpu.VMEM)
    return pl.pallas_call(
        evolve_kernel,
        out_shape=jax.ShapeDtypeStruct(current.shape, current.dtype),
        in_specs=[pl.BlockSpec(memory_space=pltpu.SMEM)] + [vmem] * 6,
        out_specs=vmem,
    )(region_means, current, zlo, zhi, ylo, yhi, picture)


def minplus_lines(field_in, line_axis, kernel_reach):
    moved_field = jnp.moveaxis(field_in, line_axis, -1)
    line_shape = moved_field.shape
    line_len = line_shape[-1]
    line_rows = moved_field.reshape(-1, line_len)
    row_count = line_rows.shape[0]
    positions = jnp.arange(line_len, dtype=jnp.float32)
    distance = positions[:, None] - positions[None, :]
    penalty_table = jnp.where(
        jnp.abs(distance) <= kernel_reach, PENALTY * (distance * distance), jnp.inf
    )
    row_limit = max(1, 1048576 // (line_len * line_len))
    row_block = 1
    while row_block * 2 <= row_limit and row_count % (row_block * 2) == 0:
        row_block = row_block * 2
    grouped = line_rows.reshape(row_count // row_block, row_block, line_len)

    def block_min(block_rows):
        return jnp.min(block_rows[:, None, :] + penalty_table[None, :, :], axis=2)

    result_rows = lax.map(block_min, grouped)
    return jnp.moveaxis(result_rows.reshape(line_shape), -1, line_axis)


def z_lines(block_lines):
    return minplus_lines(block_lines, 1, KERNEL)


def y_lines(block_lines):
    return minplus_lines(block_lines, 2, KERNEL)


def to_zlines(slab_data):
    return z_lines(lax.all_to_all(slab_data, "gz", split_axis=3, concat_axis=1, tiled=True))


def from_zlines(line_data):
    return lax.all_to_all(line_data, "gz", split_axis=1, concat_axis=3, tiled=True)


def body(levels, ct_image, region_means):
    current = levels
    for update_round in range(UPDATES):
        current = evolve_step(current, ct_image, region_means)
    smoothed = minplus_lines(current, 3, KERNEL)
    slab_back = from_zlines(to_zlines(smoothed))
    y_done = y_lines(lax.all_to_all(slab_back, "gy", split_axis=3, concat_axis=2, tiled=True))
    result_field = lax.all_to_all(y_done, "gy", split_axis=2, concat_axis=3, tiled=True)
    return (current, result_field)


def solution(mesh):
    return jax.shard_map(
        body,
        mesh=mesh,
        in_specs=(P(None, "gz", "gy", None), P("gz", "gy", None), P()),
        out_specs=(P(None, "gz", "gy", None), P(None, "gz", "gy", None)),
        check_vma=False,
    )
```

```python
import math

import jax
import jax.numpy as jnp
from jax import lax
from jax.experimental import pallas as pl
from jax.experimental.pallas import tpu as pltpu
from jax.sharding import PartitionSpec as P

LEVELS = 4
PHASES = 16
UPDATES = 2
KERNEL = 200


PENALTY = 0.0005
STEP_SIZE = 0.5


def arctan(x):
    ax = jnp.abs(x)
    big = ax > 2.414213562373095
    mid = ax > 0.4142135623730950
    z_big = -1.0 / jnp.where(big, ax, 1.0)
    z_mid = (ax - 1.0) / (ax + 1.0)
    z = jnp.where(big, z_big, jnp.where(mid, z_mid, ax))
    base = jnp.where(big, math.pi / 2, jnp.where(mid, math.pi / 4, 0.0))
    zz = z * z
    poly = (((8.05374449538e-2 * zz - 1.38776856032e-1) * zz + 1.99777106478e-1) * zz
            - 3.33329491539e-1) * zz * z + z
    r = base + poly
    return jnp.where(x < 0, -r, r)


def evolve_kernel(means_ref, cur_ref, zlo_ref, zhi_ref, ylo_ref, yhi_ref, ct_ref, out_ref):
    nz, ny, nx = cur_ref.shape[1], cur_ref.shape[2], cur_ref.shape[3]
    shape = (ny, nx)
    xi = lax.broadcasted_iota(jnp.int32, shape, 1)
    yi = lax.broadcasted_iota(jnp.int32, shape, 0)
    xa = pltpu.roll(xi, 1, 1)
    xb = pltpu.roll(xi, nx - 1, 1)
    xa_ok = jnp.abs(xa - xi) == 1
    xb_ok = jnp.abs(xb - xi) == 1
    ya = pltpu.roll(yi, 1, 0)
    yb = pltpu.roll(yi, ny - 1, 0)
    ya_ok = jnp.abs(ya - yi) == 1
    yb_ok = jnp.abs(yb - yi) == 1
    low_row = yi == 0
    means = [means_ref[p] for p in range(PHASES)]
    for z in range(nz):
        picture = ct_ref[z]
        energy = []
        for p in range(PHASES):
            differ = picture - means[p]
            energy.append(differ * differ)
        phis, lap, g1, g0, dl = [], [], [], [], []
        for k in range(LEVELS):
            c = cur_ref[k, z]
            zm = zlo_ref[k, 0] if z == 0 else cur_ref[k, z - 1]
            zp = zhi_ref[k, 0] if z == nz - 1 else cur_ref[k, z + 1]
            edge = jnp.where(low_row, ylo_ref[k, z], yhi_ref[k, z])
            ym = jnp.where(ya_ok, pltpu.roll(c, 1, 0), edge)
            yp = jnp.where(yb_ok, pltpu.roll(c, ny - 1, 0), edge)
            xm = jnp.where(xa_ok, pltpu.roll(c, 1, 1), 0.0)
            xp = jnp.where(xb_ok, pltpu.roll(c, nx - 1, 1), 0.0)
            lap.append(zm + zp + ym + yp + xm + xp - 6.0 * c)
            h = 0.5 + arctan(c) / math.pi
            g1.append(h)
            g0.append(1.0 - h)
            dl.append(1.0 / (math.pi * (1.0 + c * c)))
            phis.append(c)
        g = (g0, g1)
        pair_lo = {(a, b): g[a][0] * g[b][1] for a in (0, 1) for b in (0, 1)}
        pair_hi = {(a, b): g[a][2] * g[b][3] for a in (0, 1) for b in (0, 1)}
        for k in range(LEVELS):
            force = None
            for q in range(PHASES // 2):
                low = q & ((1 << k) - 1)
                high = (q >> k) << (k + 1)
                p0 = high | low
                p1 = p0 | (1 << k)
                bits = [(p0 >> j) & 1 for j in range(LEVELS)]
                if k == 0:
                    prod = g[bits[1]][1] * pair_hi[(bits[2], bits[3])]
                elif k == 1:
                    prod = g[bits[0]][0] * pair_hi[(bits[2], bits[3])]
                elif k == 2:
                    prod = pair_lo[(bits[0], bits[1])] * g[bits[3]][3]
                else:
                    prod = pair_lo[(bits[0], bits[1])] * g[bits[2]][2]
                term = (energy[p1] - energy[p0]) * prod
                force = term if force is None else force + term
            out_ref[k, z] = phis[k] + STEP_SIZE * dl[k] * (lap[k] - force)


def evolve_step(current, picture, region_means):
    fwd_z = [(i, i + 1) for i in range(lax.axis_size("gz") - 1)]
    fwd_y = [(i, i + 1) for i in range(lax.axis_size("gy") - 1)]
    bwd_z = [(t, s) for s, t in fwd_z]
    bwd_y = [(t, s) for s, t in fwd_y]
    nz, ny = current.shape[1], current.shape[2]
    zlo = lax.ppermute(current[:, nz - 1:nz], "gz", fwd_z)
    zhi = lax.ppermute(current[:, 0:1], "gz", bwd_z)
    ylo = lax.ppermute(current[:, :, ny - 1:ny], "gy", fwd_y)
    yhi = lax.ppermute(current[:, :, 0:1], "gy", bwd_y)
    vmem = pl.BlockSpec(memory_space=pltpu.VMEM)
    return pl.pallas_call(
        evolve_kernel,
        out_shape=jax.ShapeDtypeStruct(current.shape, current.dtype),
        in_specs=[pl.BlockSpec(memory_space=pltpu.SMEM)] + [vmem] * 6,
        out_specs=vmem,
    )(region_means, current, zlo, zhi, ylo, yhi, picture)


def penalty_table(count, offset):
    distance = (jnp.arange(count, dtype=jnp.int32) - offset).astype(jnp.float32)
    return jnp.where(
        jnp.abs(distance) <= KERNEL, PENALTY * (distance * distance), jnp.inf
    ).astype(jnp.float32)


def scan_offsets(u_ref, pen_ref, out_ref, n_out, group, nrot, q_range):
    for g0 in range(0, n_out, group):
        q_lo, q_hi = q_range(g0, group)
        q_hi = min(q_hi, pen_ref.shape[0] // nrot - 1, u_ref.shape[1] - g0 - group)

        def body(q, acc, g0=g0):
            for r in range(nrot):
                vals = u_ref[r, pl.ds(g0 + q, group)]
                acc = jnp.minimum(acc, vals + pen_ref[q * nrot + r])
            return acc

        init = jnp.full((group,) + tuple(out_ref.shape[1:]), jnp.inf, jnp.float32)
        out_ref[g0:g0 + group] = lax.fori_loop(q_lo, q_hi + 1, body, init)


def build_rotations(v_ref, u_ref, nrot, pick):
    def body(b, carry):
        here = v_ref[b]
        after = v_ref[b + 1]
        for r in range(nrot):
            u_ref[r, b] = pick(r, here, after)
        return carry

    lax.fori_loop(0, u_ref.shape[1], body, 0)


def xpass_kernel(pen_ref, src_ref, out_ref, pad_ref, u_ref):
    lines, nx = src_ref.shape
    reach = KERNEL
    pad_ref[...] = jnp.full(pad_ref.shape, jnp.inf, jnp.float32)
    pad_ref[reach:reach + nx, :] = src_ref[...].T
    sub = lax.broadcasted_iota(jnp.int32, (8, lines), 0)

    def body(b, carry):
        here = pad_ref[pl.ds(pl.multiple_of(b * 8, 8), 8), :]
        after = pad_ref[pl.ds(pl.multiple_of(b * 8 + 8, 8), 8), :]
        u_ref[0, b] = here
        for r in range(1, 8):
            u_ref[r, b] = jnp.where(sub < 8 - r, pltpu.roll(here, 8 - r, 0), pltpu.roll(after, 8 - r, 0))
        return carry

    lax.fori_loop(0, u_ref.shape[1], body, 0)
    n_out = nx // 8

    def q_range(g0, group):
        lo = max(0, -((8 * (g0 + group - 1) + 14 - reach) // 8))
        hi = (reach + nx - 1 - 8 * g0) // 8
        return lo, hi

    scan_offsets(u_ref, pen_ref, out_ref, n_out, 16, 8, q_range)


def zpass_kernel(pen_ref, src_ref, out_ref, pad_ref, u_ref):
    n_out = src_ref.shape[0]
    padc = KERNEL // 4
    pad_ref[...] = jnp.full(pad_ref.shape, jnp.inf, jnp.float32)
    pad_ref[padc:padc + n_out] = src_ref[...]
    lane = lax.broadcasted_iota(jnp.int32, src_ref.shape[1:], 1)
    sub_z = (lane // 8) % 4

    def body(b, carry):
        here = pad_ref[b]
        after = pad_ref[b + 1]
        u_ref[0, b] = here
        for r in range(1, 4):
            u_ref[r, b] = jnp.where(sub_z + r < 4, pltpu.roll(here, 128 - 8 * r, 1),
                                    pltpu.roll(after, 32 - 8 * r, 1))
        return carry

    lax.fori_loop(0, u_ref.shape[1], body, 0)

    def q_range(g0, group):
        lo = max(0, padc - 1 - (g0 + group - 1))
        hi = padc + n_out - 1 - g0
        return lo, hi

    scan_offsets(u_ref, pen_ref, out_ref, n_out, 16, 4, q_range)


def ypass_kernel(pen_ref, src_ref, out_ref, pad_ref, u_ref):
    n_out = src_ref.shape[0]
    padc = n_out
    pad_ref[...] = jnp.full(pad_ref.shape, jnp.inf, jnp.float32)
    pad_ref[padc:padc + n_out] = src_ref[...]
    lane = lax.broadcasted_iota(jnp.int32, src_ref.shape[1:], 2)
    sub_y = lane % 8

    def body(b, carry):
        here = pad_ref[b]
        after = pad_ref[b + 1]
        u_ref[0, b] = here
        for r in range(1, 8):
            u_ref[r, b] = jnp.where(sub_y + r < 8, pltpu.roll(here, 128 - r, 2),
                                    pltpu.roll(after, 8 - r, 2))
        return carry

    lax.fori_loop(0, u_ref.shape[1], body, 0)

    def q_range(g0, group):
        lo = max(0, padc - 1 - (g0 + group - 1))
        hi = padc + n_out - 1 - g0
        return lo, hi

    scan_offsets(u_ref, pen_ref, out_ref, n_out, 1, 8, q_range)


def transpose_kernel(src_ref, out_ref):
    out_ref[...] = src_ref[...].T


def local_call(kernel, out_shape, scratch, *args):
    vmem = pl.BlockSpec(memory_space=pltpu.VMEM)
    smem = pl.BlockSpec(memory_space=pltpu.SMEM)
    specs = [smem if a.ndim == 1 else vmem for a in args]
    return pl.pallas_call(
        kernel,
        out_shape=jax.ShapeDtypeStruct(out_shape, jnp.float32),
        in_specs=specs,
        out_specs=vmem,
        scratch_shapes=[pltpu.VMEM(s, jnp.float32) for s in scratch],
    )(*args)


def regularize(current):
    levels, nz, ny, nx = current.shape
    lines = levels * nz * ny
    assert lines == 128 and nx % 8 == 0
    n_gz = lax.axis_size("gz")
    n_gy = lax.axis_size("gy")
    xq = (KERNEL + 7) // 8
    nxo = nx // 8
    pen_x = penalty_table(8 * (xq * 2 + 2), KERNEL)
    xpad_rows = 8 * (nxo + 2 * xq + 3)
    t1 = local_call(xpass_kernel, (nxo, 8, lines), [(xpad_rows, lines), (8, nxo + 2 * xq + 2, 8, lines)],
                    pen_x, current.reshape(lines, nx))
    assert nxo == n_gz
    r1 = lax.all_to_all(t1, "gz", 0, 0, tiled=True)
    nzo = n_gz
    zq = KERNEL // 4
    pen_z = penalty_table(4 * (2 * zq + 2), KERNEL)
    t2 = local_call(zpass_kernel, r1.shape, [(nzo + 2 * zq + 3, 8, lines), (4, nzo + 2 * zq + 2, 8, lines)],
                    pen_z, r1)
    r2 = lax.all_to_all(t2, "gz", 0, 0, tiled=True)
    t3 = r2.reshape(n_gy, nxo // n_gy, 8, lines)
    r3 = lax.all_to_all(t3, "gy", 0, 0, tiled=True)
    nyo = n_gy
    pen_y = penalty_table(8 * (2 * nyo), 8 * nyo)
    t4 = local_call(ypass_kernel, r3.shape, [(3 * nyo + 1,) + r3.shape[1:], (8, 2 * nyo) + r3.shape[1:]],
                    pen_y, r3)
    r4 = lax.all_to_all(t4, "gy", 0, 0, tiled=True)
    out = local_call(transpose_kernel, (lines, nx), [], r4.reshape(nx, lines))
    return out.reshape(current.shape)


def body(levels, ct_image, region_means):
    current = levels
    for update_round in range(UPDATES):
        current = evolve_step(current, ct_image, region_means)
    return (current, regularize(current))


def solution(mesh):
    return jax.shard_map(
        body,
        mesh=mesh,
        in_specs=(P(None, "gz", "gy", None), P("gz", "gy", None), P()),
        out_specs=(P(None, "gz", "gy", None), P(None, "gz", "gy", None)),
        check_vma=False,
    )
```

```python
import math

import jax
import jax.numpy as jnp
from jax import lax
from jax.experimental import pallas as pl
from jax.experimental.pallas import tpu as pltpu
from jax.sharding import PartitionSpec as P

LEVELS = 4
PHASES = 16
UPDATES = 2
KERNEL = 200


PENALTY = 0.0005
STEP_SIZE = 0.5


def arctan(x):
    ax = jnp.abs(x)
    big = ax > 2.414213562373095
    mid = ax > 0.4142135623730950
    z_big = -1.0 / jnp.where(big, ax, 1.0)
    z_mid = (ax - 1.0) / (ax + 1.0)
    z = jnp.where(big, z_big, jnp.where(mid, z_mid, ax))
    base = jnp.where(big, math.pi / 2, jnp.where(mid, math.pi / 4, 0.0))
    zz = z * z
    poly = (((8.05374449538e-2 * zz - 1.38776856032e-1) * zz + 1.99777106478e-1) * zz
            - 3.33329491539e-1) * zz * z + z
    r = base + poly
    return jnp.where(x < 0, -r, r)


def evolve_kernel(means_ref, cur_ref, zlo_ref, zhi_ref, ylo_ref, yhi_ref, ct_ref, out_ref):
    nz, ny, nx = cur_ref.shape[1], cur_ref.shape[2], cur_ref.shape[3]
    shape = (ny, nx)
    xi = lax.broadcasted_iota(jnp.int32, shape, 1)
    yi = lax.broadcasted_iota(jnp.int32, shape, 0)
    xa = pltpu.roll(xi, 1, 1)
    xb = pltpu.roll(xi, nx - 1, 1)
    xa_ok = jnp.abs(xa - xi) == 1
    xb_ok = jnp.abs(xb - xi) == 1
    ya = pltpu.roll(yi, 1, 0)
    yb = pltpu.roll(yi, ny - 1, 0)
    ya_ok = jnp.abs(ya - yi) == 1
    yb_ok = jnp.abs(yb - yi) == 1
    low_row = yi == 0
    means = [means_ref[p] for p in range(PHASES)]
    for z in range(nz):
        picture = ct_ref[z]
        energy = []
        for p in range(PHASES):
            differ = picture - means[p]
            energy.append(differ * differ)
        phis, lap, g1, g0, dl = [], [], [], [], []
        for k in range(LEVELS):
            c = cur_ref[k, z]
            zm = zlo_ref[k, 0] if z == 0 else cur_ref[k, z - 1]
            zp = zhi_ref[k, 0] if z == nz - 1 else cur_ref[k, z + 1]
            edge = jnp.where(low_row, ylo_ref[k, z], yhi_ref[k, z])
            ym = jnp.where(ya_ok, pltpu.roll(c, 1, 0), edge)
            yp = jnp.where(yb_ok, pltpu.roll(c, ny - 1, 0), edge)
            xm = jnp.where(xa_ok, pltpu.roll(c, 1, 1), 0.0)
            xp = jnp.where(xb_ok, pltpu.roll(c, nx - 1, 1), 0.0)
            lap.append(zm + zp + ym + yp + xm + xp - 6.0 * c)
            h = 0.5 + arctan(c) / math.pi
            g1.append(h)
            g0.append(1.0 - h)
            dl.append(1.0 / (math.pi * (1.0 + c * c)))
            phis.append(c)
        g = (g0, g1)
        pair_lo = {(a, b): g[a][0] * g[b][1] for a in (0, 1) for b in (0, 1)}
        pair_hi = {(a, b): g[a][2] * g[b][3] for a in (0, 1) for b in (0, 1)}
        for k in range(LEVELS):
            force = None
            for q in range(PHASES // 2):
                low = q & ((1 << k) - 1)
                high = (q >> k) << (k + 1)
                p0 = high | low
                p1 = p0 | (1 << k)
                bits = [(p0 >> j) & 1 for j in range(LEVELS)]
                if k == 0:
                    prod = g[bits[1]][1] * pair_hi[(bits[2], bits[3])]
                elif k == 1:
                    prod = g[bits[0]][0] * pair_hi[(bits[2], bits[3])]
                elif k == 2:
                    prod = pair_lo[(bits[0], bits[1])] * g[bits[3]][3]
                else:
                    prod = pair_lo[(bits[0], bits[1])] * g[bits[2]][2]
                term = (energy[p1] - energy[p0]) * prod
                force = term if force is None else force + term
            out_ref[k, z] = phis[k] + STEP_SIZE * dl[k] * (lap[k] - force)


def evolve_step(current, picture, region_means):
    fwd_z = [(i, i + 1) for i in range(lax.axis_size("gz") - 1)]
    fwd_y = [(i, i + 1) for i in range(lax.axis_size("gy") - 1)]
    bwd_z = [(t, s) for s, t in fwd_z]
    bwd_y = [(t, s) for s, t in fwd_y]
    nz, ny = current.shape[1], current.shape[2]
    zlo = lax.ppermute(current[:, nz - 1:nz], "gz", fwd_z)
    zhi = lax.ppermute(current[:, 0:1], "gz", bwd_z)
    ylo = lax.ppermute(current[:, :, ny - 1:ny], "gy", fwd_y)
    yhi = lax.ppermute(current[:, :, 0:1], "gy", bwd_y)
    vmem = pl.BlockSpec(memory_space=pltpu.VMEM)
    return pl.pallas_call(
        evolve_kernel,
        out_shape=jax.ShapeDtypeStruct(current.shape, current.dtype),
        in_specs=[pl.BlockSpec(memory_space=pltpu.SMEM)] + [vmem] * 6,
        out_specs=vmem,
    )(region_means, current, zlo, zhi, ylo, yhi, picture)


def penalty_table(count, offset):
    distance = (jnp.arange(count, dtype=jnp.int32) - offset).astype(jnp.float32)
    return jnp.where(
        jnp.abs(distance) <= KERNEL, PENALTY * (distance * distance), jnp.inf
    ).astype(jnp.float32)


def scan_offsets(u_ref, pen_ref, out_ref, n_out, group, nrot, q_range):
    for g0 in range(0, n_out, group):
        q_lo, q_hi = q_range(g0, group)
        q_hi = min(q_hi, pen_ref.shape[0] // nrot - 1, u_ref.shape[1] - g0 - group)

        def body(q, acc, g0=g0):
            for r in range(nrot):
                vals = u_ref[r, pl.ds(g0 + q, group)]
                acc = jnp.minimum(acc, vals + pen_ref[q * nrot + r])
            return acc

        init = jnp.full((group,) + tuple(out_ref.shape[1:]), jnp.inf, jnp.float32)
        out_ref[g0:g0 + group] = lax.fori_loop(q_lo, q_hi + 1, body, init)


def xpass_kernel(pen_ref, src_ref, out_ref, pad_ref, u_ref):
    lines, nx = src_ref.shape
    reach = KERNEL
    pad_ref[...] = jnp.full(pad_ref.shape, jnp.inf, jnp.float32)
    pad_ref[reach:reach + nx, :] = src_ref[...].T
    sub = lax.broadcasted_iota(jnp.int32, (8, lines), 0)

    def body(b, carry):
        here = pad_ref[pl.ds(pl.multiple_of(b * 8, 8), 8), :]
        after = pad_ref[pl.ds(pl.multiple_of(b * 8 + 8, 8), 8), :]
        u_ref[0, b] = here
        for r in range(1, 8):
            u_ref[r, b] = jnp.where(sub < 8 - r, pltpu.roll(here, 8 - r, 0), pltpu.roll(after, 8 - r, 0))
        return carry

    lax.fori_loop(0, u_ref.shape[1], body, 0)
    n_out = nx // 8

    def q_range(g0, group):
        lo = max(0, -((8 * (g0 + group - 1) + 14 - reach) // 8))
        hi = (reach + nx - 1 - 8 * g0) // 8
        return lo, hi

    scan_offsets(u_ref, pen_ref, out_ref, n_out, 16, 8, q_range)


def zpass_kernel(pen_ref, src_ref, out_ref, pad_ref, u_ref):
    n_out = src_ref.shape[0]
    padc = KERNEL // 4
    pad_ref[...] = jnp.full(pad_ref.shape, jnp.inf, jnp.float32)
    pad_ref[padc:padc + n_out] = src_ref[...]
    lane = lax.broadcasted_iota(jnp.int32, src_ref.shape[1:], 1)
    sub_z = (lane // 8) % 4

    def body(b, carry):
        here = pad_ref[b]
        after = pad_ref[b + 1]
        u_ref[0, b] = here
        for r in range(1, 4):
            u_ref[r, b] = jnp.where(sub_z + r < 4, pltpu.roll(here, 128 - 8 * r, 1),
                                    pltpu.roll(after, 32 - 8 * r, 1))
        return carry

    lax.fori_loop(0, u_ref.shape[1], body, 0)

    def q_range(g0, group):
        lo = max(0, padc - 1 - (g0 + group - 1))
        hi = padc + n_out - 1 - g0
        return lo, hi

    scan_offsets(u_ref, pen_ref, out_ref, n_out, 16, 4, q_range)


def ypass_kernel(pen_ref, src_ref, out_ref, pad_ref, u_ref):
    n_out = src_ref.shape[0]
    padc = n_out
    pad_ref[...] = jnp.full(pad_ref.shape, jnp.inf, jnp.float32)
    pad_ref[padc:padc + n_out] = src_ref[...]
    lane = lax.broadcasted_iota(jnp.int32, src_ref.shape[1:], 2)
    sub_y = lane % 8

    def body(b, carry):
        here = pad_ref[b]
        after = pad_ref[b + 1]
        u_ref[0, b] = here
        for r in range(1, 8):
            u_ref[r, b] = jnp.where(sub_y + r < 8, pltpu.roll(here, 128 - r, 2),
                                    pltpu.roll(after, 8 - r, 2))
        return carry

    lax.fori_loop(0, u_ref.shape[1], body, 0)

    def q_range(g0, group):
        lo = max(0, padc - 1 - (g0 + group - 1))
        hi = padc + n_out - 1 - g0
        return lo, hi

    scan_offsets(u_ref, pen_ref, out_ref, n_out, 1, 8, q_range)


def transpose_kernel(src_ref, out_ref):
    out_ref[...] = src_ref[...].T


def local_call(kernel, out_shape, scratch, *args):
    vmem = pl.BlockSpec(memory_space=pltpu.VMEM)
    smem = pl.BlockSpec(memory_space=pltpu.SMEM)
    specs = [smem if a.ndim == 1 else vmem for a in args]
    return pl.pallas_call(
        kernel,
        out_shape=jax.ShapeDtypeStruct(out_shape, jnp.float32),
        in_specs=specs,
        out_specs=vmem,
        scratch_shapes=[pltpu.VMEM(s, jnp.float32) for s in scratch],
    )(*args)


def zy_kernel(pen_z_ref, pen_y_ref, src_ref, out_ref, pad_ref, u_ref, w_ref):
    n_out = src_ref.shape[0]
    padc = KERNEL // 4
    pad_ref[...] = jnp.full(pad_ref.shape, jnp.inf, jnp.float32)
    pad_ref[padc:padc + n_out] = src_ref[...]
    lane = lax.broadcasted_iota(jnp.int32, src_ref.shape[1:], 1)
    sub = lax.broadcasted_iota(jnp.int32, src_ref.shape[1:], 0)
    sub_z = (lane // 8) % 4
    sub_y = lane % 8

    def zbody(b, carry):
        here = pad_ref[b]
        after = pad_ref[b + 1]
        u_ref[0, b] = here
        for r in range(1, 4):
            u_ref[r, b] = jnp.where(sub_z + r < 4, pltpu.roll(here, 128 - 8 * r, 1),
                                    pltpu.roll(after, 32 - 8 * r, 1))
        return carry

    lax.fori_loop(0, u_ref.shape[1], zbody, 0)

    def q_range(g0, group):
        lo = max(0, padc - 1 - (g0 + group - 1))
        hi = padc + n_out - 1 - g0
        return lo, hi

    scan_offsets(u_ref, pen_z_ref, out_ref, n_out, 16, 4, q_range)

    def wbody(a, carry):
        v = out_ref[a]
        w_ref[0, a] = v
        for r in range(1, 8):
            w_ref[r, a] = jnp.where(sub_y + r < 8, pltpu.roll(v, 128 - r, 1),
                                    pltpu.roll(pltpu.roll(v, 8 - r, 1), 7, 0))
        return carry

    lax.fori_loop(0, n_out, wbody, 0)
    group = 8
    shifts = []
    for db in range(-8, 8):
        for dy in range(8):
            carry_in = (sub_y + dy >= 8).astype(jnp.int32)
            row = sub + db + carry_in
            valid = (row >= 0) & (row <= 7)
            shifts.append((db, dy, valid))

    def ybody(i, carry):
        a0 = pl.multiple_of(i * group, group)
        acc = [jnp.full(src_ref.shape[1:], jnp.inf, jnp.float32) for _ in range(group)]
        for db, dy, valid in shifts:
            penvec = jnp.where(valid, pen_y_ref[8 * db + dy + 64], jnp.inf)
            for g in range(group):
                v = w_ref[dy, a0 + g]
                if db % 8:
                    v = pltpu.roll(v, (8 - db) % 8, 0)
                acc[g] = jnp.minimum(acc[g], v + penvec)
        for g in range(group):
            out_ref[a0 + g] = acc[g]
        return carry

    lax.fori_loop(0, n_out // group, ybody, 0)


def regularize(current):
    levels, nz, ny, nx = current.shape
    lines = levels * nz * ny
    assert lines == 128 and nx % 8 == 0
    n_gz = lax.axis_size("gz")
    n_gy = lax.axis_size("gy")
    assert n_gz * n_gy == nx and ny == 8 and n_gy == 8
    xq = (KERNEL + 7) // 8
    nxo = nx // 8
    pen_x = penalty_table(8 * (xq * 2 + 2), KERNEL)
    xpad_rows = 8 * (nxo + 2 * xq + 3)
    t1 = local_call(xpass_kernel, (nxo, 8, lines), [(xpad_rows, lines), (8, nxo + 2 * xq + 2, 8, lines)],
                    pen_x, current.reshape(lines, nx))
    r1 = lax.all_to_all(t1.reshape(nx, lines), ("gz", "gy"), 0, 0, tiled=True)
    r1 = r1.reshape(n_gz, n_gy, lines)
    zq = KERNEL // 4
    pen_z = penalty_table(4 * (2 * zq + 2), KERNEL)
    pen_y = penalty_table(8 * 2 * n_gy, 8 * n_gy)
    t2 = pl.pallas_call(
        zy_kernel,
        out_shape=jax.ShapeDtypeStruct(r1.shape, jnp.float32),
        in_specs=[pl.BlockSpec(memory_space=pltpu.SMEM)] * 2 + [pl.BlockSpec(memory_space=pltpu.VMEM)],
        out_specs=pl.BlockSpec(memory_space=pltpu.VMEM),
        scratch_shapes=[pltpu.VMEM((n_gz + 2 * zq + 3, 8, lines), jnp.float32),
                        pltpu.VMEM((4, n_gz + 2 * zq + 2, 8, lines), jnp.float32),
                        pltpu.VMEM((8, n_gz, 8, lines), jnp.float32)],
    )(pen_z, pen_y, r1)
    r2 = lax.all_to_all(t2.reshape(nx, lines), ("gz", "gy"), 0, 0, tiled=True)
    out = local_call(transpose_kernel, (lines, nx), [], r2)
    return out.reshape(current.shape)


def body(levels, ct_image, region_means):
    current = levels
    for update_round in range(UPDATES):
        current = evolve_step(current, ct_image, region_means)
    return (current, regularize(current))


def solution(mesh):
    return jax.shard_map(
        body,
        mesh=mesh,
        in_specs=(P(None, "gz", "gy", None), P("gz", "gy", None), P()),
        out_specs=(P(None, "gz", "gy", None), P(None, "gz", "gy", None)),
        check_vma=False,
    )
```

```python
import math

import jax
import jax.numpy as jnp
from jax import lax
from jax.experimental import pallas as pl
from jax.experimental.pallas import tpu as pltpu
from jax.sharding import PartitionSpec as P

LEVELS = 4
PHASES = 16
UPDATES = 2
KERNEL = 200


PENALTY = 0.0005
STEP_SIZE = 0.5


def arctan(x):
    ax = jnp.abs(x)
    big = ax > 2.414213562373095
    mid = ax > 0.4142135623730950
    z_big = -1.0 / jnp.where(big, ax, 1.0)
    z_mid = (ax - 1.0) / (ax + 1.0)
    z = jnp.where(big, z_big, jnp.where(mid, z_mid, ax))
    base = jnp.where(big, math.pi / 2, jnp.where(mid, math.pi / 4, 0.0))
    zz = z * z
    poly = (((8.05374449538e-2 * zz - 1.38776856032e-1) * zz + 1.99777106478e-1) * zz
            - 3.33329491539e-1) * zz * z + z
    r = base + poly
    return jnp.where(x < 0, -r, r)


def compute_step(means_ref, cur_ref, zlo_ref, zhi_ref, ylo_ref, yhi_ref, ct_ref, out_ref):
    nz, ny, nx = cur_ref.shape[1], cur_ref.shape[2], cur_ref.shape[3]
    shape = (ny, nx)
    xi = lax.broadcasted_iota(jnp.int32, shape, 1)
    yi = lax.broadcasted_iota(jnp.int32, shape, 0)
    xa = pltpu.roll(xi, 1, 1)
    xb = pltpu.roll(xi, nx - 1, 1)
    xa_ok = jnp.abs(xa - xi) == 1
    xb_ok = jnp.abs(xb - xi) == 1
    ya = pltpu.roll(yi, 1, 0)
    yb = pltpu.roll(yi, ny - 1, 0)
    ya_ok = jnp.abs(ya - yi) == 1
    yb_ok = jnp.abs(yb - yi) == 1
    low_row = yi == 0
    means = [means_ref[p] for p in range(PHASES)]
    for z in range(nz):
        picture = ct_ref[z]
        energy = []
        for p in range(PHASES):
            differ = picture - means[p]
            energy.append(differ * differ)
        phis, lap, g1, g0, dl = [], [], [], [], []
        for k in range(LEVELS):
            c = cur_ref[k, z]
            zm = zlo_ref[k] if z == 0 else cur_ref[k, z - 1]
            zp = zhi_ref[k] if z == nz - 1 else cur_ref[k, z + 1]
            edge = jnp.where(low_row, ylo_ref[k, z], yhi_ref[k, z])
            ym = jnp.where(ya_ok, pltpu.roll(c, 1, 0), edge)
            yp = jnp.where(yb_ok, pltpu.roll(c, ny - 1, 0), edge)
            xm = jnp.where(xa_ok, pltpu.roll(c, 1, 1), 0.0)
            xp = jnp.where(xb_ok, pltpu.roll(c, nx - 1, 1), 0.0)
            lap.append(zm + zp + ym + yp + xm + xp - 6.0 * c)
            h = 0.5 + arctan(c) / math.pi
            g1.append(h)
            g0.append(1.0 - h)
            dl.append(1.0 / (math.pi * (1.0 + c * c)))
            phis.append(c)
        g = (g0, g1)
        pair_lo = {(a, b): g[a][0] * g[b][1] for a in (0, 1) for b in (0, 1)}
        pair_hi = {(a, b): g[a][2] * g[b][3] for a in (0, 1) for b in (0, 1)}
        for k in range(LEVELS):
            force = None
            for q in range(PHASES // 2):
                low = q & ((1 << k) - 1)
                high = (q >> k) << (k + 1)
                p0 = high | low
                p1 = p0 | (1 << k)
                bits = [(p0 >> j) & 1 for j in range(LEVELS)]
                if k == 0:
                    prod = g[bits[1]][1] * pair_hi[(bits[2], bits[3])]
                elif k == 1:
                    prod = g[bits[0]][0] * pair_hi[(bits[2], bits[3])]
                elif k == 2:
                    prod = pair_lo[(bits[0], bits[1])] * g[bits[3]][3]
                else:
                    prod = pair_lo[(bits[0], bits[1])] * g[bits[2]][2]
                term = (energy[p1] - energy[p0]) * prod
                force = term if force is None else force + term
            out_ref[k, z] = phis[k] + STEP_SIZE * dl[k] * (lap[k] - force)


MESH = pl.DeviceIdType.MESH


def evolve_kernel(means_ref, cur_ref, ct_ref, out_ref, mid_ref, zlo_buf, zhi_buf, ylo_buf, yhi_buf,
                  send_sem, recv_sem):
    nz, ny = cur_ref.shape[1], cur_ref.shape[2]
    gz, gy = lax.axis_index("gz"), lax.axis_index("gy")
    n_gz, n_gy = lax.axis_size("gz"), lax.axis_size("gy")
    peers = [(gz > 0, (gz - 1, gy)), (gz < n_gz - 1, (gz + 1, gy)),
             (gy > 0, (gz, gy - 1)), (gy < n_gy - 1, (gz, gy + 1))]
    barrier = pltpu.get_barrier_semaphore()
    for present, dev in peers:
        @pl.when(present)
        def _(dev=dev):
            pl.semaphore_signal(barrier, inc=1, device_id=dev, device_id_type=MESH)
    count = sum(present.astype(jnp.int32) for present, _ in peers)
    pl.semaphore_wait(barrier, count)

    def exchange(step, src_ref):
        plan = [
            (gz < n_gz - 1, gz > 0, src_ref.at[:, nz - 1], zlo_buf.at[step], (gz + 1, gy)),
            (gz > 0, gz < n_gz - 1, src_ref.at[:, 0], zhi_buf.at[step], (gz - 1, gy)),
            (gy < n_gy - 1, gy > 0, src_ref.at[:, :, pl.ds(ny - 1, 1)], ylo_buf.at[step], (gz, gy + 1)),
            (gy > 0, gy < n_gy - 1, src_ref.at[:, :, pl.ds(0, 1)], yhi_buf.at[step], (gz, gy - 1)),
        ]
        copies = []
        for d, (sends, receives, src, dst, target) in enumerate(plan):
            copy = pltpu.make_async_remote_copy(
                src_ref=src, dst_ref=dst, send_sem=send_sem.at[step, d],
                recv_sem=recv_sem.at[step, d], device_id=target, device_id_type=MESH)

            @pl.when(sends)
            def _(copy=copy):
                copy.start()

            @pl.when(jnp.logical_not(receives))
            def _(dst=dst):
                dst[...] = jnp.zeros(dst.shape, jnp.float32)

            copies.append((sends, receives, copy))
        return copies

    def finish(copies):
        for sends, receives, copy in copies:
            @pl.when(receives)
            def _(copy=copy):
                copy.wait_recv()

    def drain(copies):
        for sends, receives, copy in copies:
            @pl.when(sends)
            def _(copy=copy):
                copy.wait_send()

    first = exchange(0, cur_ref)
    finish(first)
    compute_step(means_ref, cur_ref, zlo_buf.at[0], zhi_buf.at[0], ylo_buf.at[0], yhi_buf.at[0], ct_ref, mid_ref)
    drain(first)
    second = exchange(1, mid_ref)
    finish(second)
    compute_step(means_ref, mid_ref, zlo_buf.at[1], zhi_buf.at[1], ylo_buf.at[1], yhi_buf.at[1], ct_ref, out_ref)
    drain(second)


def evolve_all(current, picture, region_means):
    levels, nz, ny, nx = current.shape
    vmem = pl.BlockSpec(memory_space=pltpu.VMEM)
    f32 = jnp.float32
    return pl.pallas_call(
        evolve_kernel,
        out_shape=jax.ShapeDtypeStruct(current.shape, current.dtype),
        in_specs=[pl.BlockSpec(memory_space=pltpu.SMEM), vmem, vmem],
        out_specs=vmem,
        scratch_shapes=[
            pltpu.VMEM(current.shape, f32),
            pltpu.VMEM((2, levels, ny, nx), f32),
            pltpu.VMEM((2, levels, ny, nx), f32),
            pltpu.VMEM((2, levels, nz, 1, nx), f32),
            pltpu.VMEM((2, levels, nz, 1, nx), f32),
            pltpu.SemaphoreType.DMA((2, 4)),
            pltpu.SemaphoreType.DMA((2, 4)),
        ],
        compiler_params=pltpu.CompilerParams(collective_id=0, has_side_effects=True),
    )(region_means, current, picture)


def penalty_table(count, offset):
    distance = (jnp.arange(count, dtype=jnp.int32) - offset).astype(jnp.float32)
    return jnp.where(
        jnp.abs(distance) <= KERNEL, PENALTY * (distance * distance), jnp.inf
    ).astype(jnp.float32)


def scan_offsets(u_ref, pen_ref, out_ref, n_out, group, nrot, q_range):
    for g0 in range(0, n_out, group):
        q_lo, q_hi = q_range(g0, group)
        q_hi = min(q_hi, pen_ref.shape[0] // nrot - 1, u_ref.shape[1] - g0 - group)

        def body(q, acc, g0=g0):
            for r in range(nrot):
                vals = u_ref[r, pl.ds(g0 + q, group)]
                acc = jnp.minimum(acc, vals + pen_ref[q * nrot + r])
            return acc

        init = jnp.full((group,) + tuple(out_ref.shape[1:]), jnp.inf, jnp.float32)
        out_ref[g0:g0 + group] = lax.fori_loop(q_lo, q_hi + 1, body, init)


def xpass_kernel(pen_ref, src_ref, out_ref, pad_ref, u_ref):
    lines, nx = src_ref.shape
    reach = KERNEL
    pad_ref[...] = jnp.full(pad_ref.shape, jnp.inf, jnp.float32)
    pad_ref[reach:reach + nx, :] = src_ref[...].T
    sub = lax.broadcasted_iota(jnp.int32, (8, lines), 0)

    def body(b, carry):
        here = pad_ref[pl.ds(pl.multiple_of(b * 8, 8), 8), :]
        after = pad_ref[pl.ds(pl.multiple_of(b * 8 + 8, 8), 8), :]
        u_ref[0, b] = here
        for r in range(1, 8):
            u_ref[r, b] = jnp.where(sub < 8 - r, pltpu.roll(here, 8 - r, 0), pltpu.roll(after, 8 - r, 0))
        return carry

    lax.fori_loop(0, u_ref.shape[1], body, 0)
    n_out = nx // 8

    def q_range(g0, group):
        lo = max(0, -((8 * (g0 + group - 1) + 14 - reach) // 8))
        hi = (reach + nx - 1 - 8 * g0) // 8
        return lo, hi

    scan_offsets(u_ref, pen_ref, out_ref, n_out, 16, 8, q_range)


def zpass_kernel(pen_ref, src_ref, out_ref, pad_ref, u_ref):
    n_out = src_ref.shape[0]
    padc = KERNEL // 4
    pad_ref[...] = jnp.full(pad_ref.shape, jnp.inf, jnp.float32)
    pad_ref[padc:padc + n_out] = src_ref[...]
    lane = lax.broadcasted_iota(jnp.int32, src_ref.shape[1:], 1)
    sub_z = (lane // 8) % 4

    def body(b, carry):
        here = pad_ref[b]
        after = pad_ref[b + 1]
        u_ref[0, b] = here
        for r in range(1, 4):
            u_ref[r, b] = jnp.where(sub_z + r < 4, pltpu.roll(here, 128 - 8 * r, 1),
                                    pltpu.roll(after, 32 - 8 * r, 1))
        return carry

    lax.fori_loop(0, u_ref.shape[1], body, 0)

    def q_range(g0, group):
        lo = max(0, padc - 1 - (g0 + group - 1))
        hi = padc + n_out - 1 - g0
        return lo, hi

    scan_offsets(u_ref, pen_ref, out_ref, n_out, 16, 4, q_range)


def ypass_kernel(pen_ref, src_ref, out_ref, pad_ref, u_ref):
    n_out = src_ref.shape[0]
    padc = n_out
    pad_ref[...] = jnp.full(pad_ref.shape, jnp.inf, jnp.float32)
    pad_ref[padc:padc + n_out] = src_ref[...]
    lane = lax.broadcasted_iota(jnp.int32, src_ref.shape[1:], 2)
    sub_y = lane % 8

    def body(b, carry):
        here = pad_ref[b]
        after = pad_ref[b + 1]
        u_ref[0, b] = here
        for r in range(1, 8):
            u_ref[r, b] = jnp.where(sub_y + r < 8, pltpu.roll(here, 128 - r, 2),
                                    pltpu.roll(after, 8 - r, 2))
        return carry

    lax.fori_loop(0, u_ref.shape[1], body, 0)

    def q_range(g0, group):
        lo = max(0, padc - 1 - (g0 + group - 1))
        hi = padc + n_out - 1 - g0
        return lo, hi

    scan_offsets(u_ref, pen_ref, out_ref, n_out, 1, 8, q_range)


def transpose_kernel(src_ref, out_ref):
    out_ref[...] = src_ref[...].T


def local_call(kernel, out_shape, scratch, *args):
    vmem = pl.BlockSpec(memory_space=pltpu.VMEM)
    smem = pl.BlockSpec(memory_space=pltpu.SMEM)
    specs = [smem if a.ndim == 1 else vmem for a in args]
    return pl.pallas_call(
        kernel,
        out_shape=jax.ShapeDtypeStruct(out_shape, jnp.float32),
        in_specs=specs,
        out_specs=vmem,
        scratch_shapes=[pltpu.VMEM(s, jnp.float32) for s in scratch],
    )(*args)


def zy_kernel(pen_z_ref, pen_y_ref, src_ref, out_ref, pad_ref, u_ref, w_ref):
    n_out = src_ref.shape[0]
    padc = KERNEL // 4
    pad_ref[...] = jnp.full(pad_ref.shape, jnp.inf, jnp.float32)
    pad_ref[padc:padc + n_out] = src_ref[...]
    lane = lax.broadcasted_iota(jnp.int32, src_ref.shape[1:], 1)
    sub = lax.broadcasted_iota(jnp.int32, src_ref.shape[1:], 0)
    sub_z = (lane // 8) % 4
    sub_y = lane % 8

    def zbody(b, carry):
        here = pad_ref[b]
        after = pad_ref[b + 1]
        u_ref[0, b] = here
        for r in range(1, 4):
            u_ref[r, b] = jnp.where(sub_z + r < 4, pltpu.roll(here, 128 - 8 * r, 1),
                                    pltpu.roll(after, 32 - 8 * r, 1))
        return carry

    lax.fori_loop(0, u_ref.shape[1], zbody, 0)

    def q_range(g0, group):
        lo = max(0, padc - 1 - (g0 + group - 1))
        hi = padc + n_out - 1 - g0
        return lo, hi

    scan_offsets(u_ref, pen_z_ref, out_ref, n_out, 16, 4, q_range)

    def wbody(a, carry):
        v = out_ref[a]
        w_ref[0, a] = v
        for r in range(1, 8):
            w_ref[r, a] = jnp.where(sub_y + r < 8, pltpu.roll(v, 128 - r, 1),
                                    pltpu.roll(pltpu.roll(v, 8 - r, 1), 7, 0))
        return carry

    lax.fori_loop(0, n_out, wbody, 0)
    group = 8
    shifts = []
    for db in range(-8, 8):
        for dy in range(8):
            carry_in = (sub_y + dy >= 8).astype(jnp.int32)
            row = sub + db + carry_in
            valid = (row >= 0) & (row <= 7)
            shifts.append((db, dy, valid))

    def ybody(i, carry):
        a0 = pl.multiple_of(i * group, group)
        acc = [jnp.full(src_ref.shape[1:], jnp.inf, jnp.float32) for _ in range(group)]
        for db, dy, valid in shifts:
            penvec = jnp.where(valid, pen_y_ref[8 * db + dy + 64], jnp.inf)
            for g in range(group):
                v = w_ref[dy, a0 + g]
                if db % 8:
                    v = pltpu.roll(v, (8 - db) % 8, 0)
                acc[g] = jnp.minimum(acc[g], v + penvec)
        for g in range(group):
            out_ref[a0 + g] = acc[g]
        return carry

    lax.fori_loop(0, n_out // group, ybody, 0)


def regularize(current):
    levels, nz, ny, nx = current.shape
    lines = levels * nz * ny
    assert lines == 128 and nx % 8 == 0
    n_gz = lax.axis_size("gz")
    n_gy = lax.axis_size("gy")
    assert n_gz * n_gy == nx and ny == 8 and n_gy == 8
    xq = (KERNEL + 7) // 8
    nxo = nx // 8
    pen_x = penalty_table(8 * (xq * 2 + 2), KERNEL)
    xpad_rows = 8 * (nxo + 2 * xq + 3)
    t1 = local_call(xpass_kernel, (nxo, 8, lines), [(xpad_rows, lines), (8, nxo + 2 * xq + 2, 8, lines)],
                    pen_x, current.reshape(lines, nx))
    r1 = lax.all_to_all(t1.reshape(nx, lines), ("gz", "gy"), 0, 0, tiled=True)
    r1 = r1.reshape(n_gz, n_gy, lines)
    zq = KERNEL // 4
    pen_z = penalty_table(4 * (2 * zq + 2), KERNEL)
    pen_y = penalty_table(8 * 2 * n_gy, 8 * n_gy)
    t2 = pl.pallas_call(
        zy_kernel,
        out_shape=jax.ShapeDtypeStruct(r1.shape, jnp.float32),
        in_specs=[pl.BlockSpec(memory_space=pltpu.SMEM)] * 2 + [pl.BlockSpec(memory_space=pltpu.VMEM)],
        out_specs=pl.BlockSpec(memory_space=pltpu.VMEM),
        scratch_shapes=[pltpu.VMEM((n_gz + 2 * zq + 3, 8, lines), jnp.float32),
                        pltpu.VMEM((4, n_gz + 2 * zq + 2, 8, lines), jnp.float32),
                        pltpu.VMEM((8, n_gz, 8, lines), jnp.float32)],
    )(pen_z, pen_y, r1)
    r2 = lax.all_to_all(t2.reshape(nx, lines), ("gz", "gy"), 0, 0, tiled=True)
    out = local_call(transpose_kernel, (lines, nx), [], r2)
    return out.reshape(current.shape)


def body(levels, ct_image, region_means):
    current = evolve_all(levels, ct_image, region_means)
    return (current, regularize(current))


def solution(mesh):
    return jax.shard_map(
        body,
        mesh=mesh,
        in_specs=(P(None, "gz", "gy", None), P("gz", "gy", None), P()),
        out_specs=(P(None, "gz", "gy", None), P(None, "gz", "gy", None)),
        check_vma=False,
    )
```

```python
import math

import jax
import jax.numpy as jnp
from jax import lax
from jax.experimental import pallas as pl
from jax.experimental.pallas import tpu as pltpu
from jax.sharding import PartitionSpec as P

LEVELS = 4
PHASES = 16
UPDATES = 2
KERNEL = 200


PENALTY = 0.0005
STEP_SIZE = 0.5


def arctan(x):
    ax = jnp.abs(x)
    big = ax > 2.414213562373095
    mid = ax > 0.4142135623730950
    z_big = -1.0 / jnp.where(big, ax, 1.0)
    z_mid = (ax - 1.0) / (ax + 1.0)
    z = jnp.where(big, z_big, jnp.where(mid, z_mid, ax))
    base = jnp.where(big, math.pi / 2, jnp.where(mid, math.pi / 4, 0.0))
    zz = z * z
    poly = (((8.05374449538e-2 * zz - 1.38776856032e-1) * zz + 1.99777106478e-1) * zz
            - 3.33329491539e-1) * zz * z + z
    r = base + poly
    return jnp.where(x < 0, -r, r)


def compute_step(means_ref, cur_ref, zlo_ref, zhi_ref, ylo_ref, yhi_ref, ct_ref, out_ref):
    nz, ny, nx = cur_ref.shape[1], cur_ref.shape[2], cur_ref.shape[3]
    shape = (ny, nx)
    xi = lax.broadcasted_iota(jnp.int32, shape, 1)
    yi = lax.broadcasted_iota(jnp.int32, shape, 0)
    xa = pltpu.roll(xi, 1, 1)
    xb = pltpu.roll(xi, nx - 1, 1)
    xa_ok = jnp.abs(xa - xi) == 1
    xb_ok = jnp.abs(xb - xi) == 1
    ya = pltpu.roll(yi, 1, 0)
    yb = pltpu.roll(yi, ny - 1, 0)
    ya_ok = jnp.abs(ya - yi) == 1
    yb_ok = jnp.abs(yb - yi) == 1
    low_row = yi == 0
    means = [means_ref[p] for p in range(PHASES)]
    for z in range(nz):
        picture = ct_ref[z]
        energy = []
        for p in range(PHASES):
            differ = picture - means[p]
            energy.append(differ * differ)
        phis, lap, g1, g0, dl = [], [], [], [], []
        for k in range(LEVELS):
            c = cur_ref[k, z]
            zm = zlo_ref[k] if z == 0 else cur_ref[k, z - 1]
            zp = zhi_ref[k] if z == nz - 1 else cur_ref[k, z + 1]
            edge = jnp.where(low_row, ylo_ref[k, z], yhi_ref[k, z])
            ym = jnp.where(ya_ok, pltpu.roll(c, 1, 0), edge)
            yp = jnp.where(yb_ok, pltpu.roll(c, ny - 1, 0), edge)
            xm = jnp.where(xa_ok, pltpu.roll(c, 1, 1), 0.0)
            xp = jnp.where(xb_ok, pltpu.roll(c, nx - 1, 1), 0.0)
            lap.append(zm + zp + ym + yp + xm + xp - 6.0 * c)
            h = 0.5 + arctan(c) / math.pi
            g1.append(h)
            g0.append(1.0 - h)
            dl.append(1.0 / (math.pi * (1.0 + c * c)))
            phis.append(c)
        g = (g0, g1)
        pair_lo = {(a, b): g[a][0] * g[b][1] for a in (0, 1) for b in (0, 1)}
        pair_hi = {(a, b): g[a][2] * g[b][3] for a in (0, 1) for b in (0, 1)}
        for k in range(LEVELS):
            force = None
            for q in range(PHASES // 2):
                low = q & ((1 << k) - 1)
                high = (q >> k) << (k + 1)
                p0 = high | low
                p1 = p0 | (1 << k)
                bits = [(p0 >> j) & 1 for j in range(LEVELS)]
                if k == 0:
                    prod = g[bits[1]][1] * pair_hi[(bits[2], bits[3])]
                elif k == 1:
                    prod = g[bits[0]][0] * pair_hi[(bits[2], bits[3])]
                elif k == 2:
                    prod = pair_lo[(bits[0], bits[1])] * g[bits[3]][3]
                else:
                    prod = pair_lo[(bits[0], bits[1])] * g[bits[2]][2]
                term = (energy[p1] - energy[p0]) * prod
                force = term if force is None else force + term
            out_ref[k, z] = phis[k] + STEP_SIZE * dl[k] * (lap[k] - force)


MESH = pl.DeviceIdType.MESH


def evolve_kernel(means_ref, cur_ref, ct_ref, out_ref, mid_ref, zlo_buf, zhi_buf, ylo_buf, yhi_buf,
                  send_sem, recv_sem):
    nz, ny = cur_ref.shape[1], cur_ref.shape[2]
    gz, gy = lax.axis_index("gz"), lax.axis_index("gy")
    n_gz, n_gy = lax.axis_size("gz"), lax.axis_size("gy")
    peers = [(gz > 0, (gz - 1, gy)), (gz < n_gz - 1, (gz + 1, gy)),
             (gy > 0, (gz, gy - 1)), (gy < n_gy - 1, (gz, gy + 1))]
    barrier = pltpu.get_barrier_semaphore()
    for present, dev in peers:
        @pl.when(present)
        def _(dev=dev):
            pl.semaphore_signal(barrier, inc=1, device_id=dev, device_id_type=MESH)
    count = sum(present.astype(jnp.int32) for present, _ in peers)
    pl.semaphore_wait(barrier, count)

    def exchange(step, src_ref):
        plan = [
            (gz < n_gz - 1, gz > 0, src_ref.at[:, nz - 1], zlo_buf.at[step], (gz + 1, gy)),
            (gz > 0, gz < n_gz - 1, src_ref.at[:, 0], zhi_buf.at[step], (gz - 1, gy)),
            (gy < n_gy - 1, gy > 0, src_ref.at[:, :, pl.ds(ny - 1, 1)], ylo_buf.at[step], (gz, gy + 1)),
            (gy > 0, gy < n_gy - 1, src_ref.at[:, :, pl.ds(0, 1)], yhi_buf.at[step], (gz, gy - 1)),
        ]
        copies = []
        for d, (sends, receives, src, dst, target) in enumerate(plan):
            copy = pltpu.make_async_remote_copy(
                src_ref=src, dst_ref=dst, send_sem=send_sem.at[step, d],
                recv_sem=recv_sem.at[step, d], device_id=target, device_id_type=MESH)

            @pl.when(sends)
            def _(copy=copy):
                copy.start()

            @pl.when(jnp.logical_not(receives))
            def _(dst=dst):
                dst[...] = jnp.zeros(dst.shape, jnp.float32)

            copies.append((sends, receives, copy))
        return copies

    def finish(copies):
        for sends, receives, copy in copies:
            @pl.when(receives)
            def _(copy=copy):
                copy.wait_recv()

    def drain(copies):
        for sends, receives, copy in copies:
            @pl.when(sends)
            def _(copy=copy):
                copy.wait_send()

    first = exchange(0, cur_ref)
    finish(first)
    compute_step(means_ref, cur_ref, zlo_buf.at[0], zhi_buf.at[0], ylo_buf.at[0], yhi_buf.at[0], ct_ref, mid_ref)
    drain(first)
    second = exchange(1, mid_ref)
    finish(second)
    compute_step(means_ref, mid_ref, zlo_buf.at[1], zhi_buf.at[1], ylo_buf.at[1], yhi_buf.at[1], ct_ref, out_ref)
    drain(second)


def evolve_all(current, picture, region_means):
    levels, nz, ny, nx = current.shape
    vmem = pl.BlockSpec(memory_space=pltpu.VMEM)
    f32 = jnp.float32
    return pl.pallas_call(
        evolve_kernel,
        out_shape=jax.ShapeDtypeStruct(current.shape, current.dtype),
        in_specs=[pl.BlockSpec(memory_space=pltpu.SMEM), vmem, vmem],
        out_specs=vmem,
        scratch_shapes=[
            pltpu.VMEM(current.shape, f32),
            pltpu.VMEM((2, levels, ny, nx), f32),
            pltpu.VMEM((2, levels, ny, nx), f32),
            pltpu.VMEM((2, levels, nz, 1, nx), f32),
            pltpu.VMEM((2, levels, nz, 1, nx), f32),
            pltpu.SemaphoreType.DMA((2, 4)),
            pltpu.SemaphoreType.DMA((2, 4)),
        ],
        compiler_params=pltpu.CompilerParams(collective_id=0, has_side_effects=True),
    )(region_means, current, picture)


def penalty_table(count, offset):
    distance = (jnp.arange(count, dtype=jnp.int32) - offset).astype(jnp.float32)
    return jnp.where(
        jnp.abs(distance) <= KERNEL, PENALTY * (distance * distance), jnp.inf
    ).astype(jnp.float32)


def scan_offsets(u_ref, pen_ref, out_ref, n_out, group, nrot, q_range):
    for g0 in range(0, n_out, group):
        q_lo, q_hi = q_range(g0, group)
        q_hi = min(q_hi, pen_ref.shape[0] // nrot - 1, u_ref.shape[1] - g0 - group)

        def body(q, acc, g0=g0):
            for r in range(nrot):
                vals = u_ref[r, pl.ds(g0 + q, group)]
                acc = jnp.minimum(acc, vals + pen_ref[q * nrot + r])
            return acc

        init = jnp.full((group,) + tuple(out_ref.shape[1:]), jnp.inf, jnp.float32)
        out_ref[g0:g0 + group] = lax.fori_loop(q_lo, q_hi + 1, body, init, unroll=2)


def xpass_kernel(pen_ref, src_ref, out_ref, pad_ref, u_ref):
    lines, nx = src_ref.shape
    reach = KERNEL
    pad_ref[...] = jnp.full(pad_ref.shape, jnp.inf, jnp.float32)
    pad_ref[reach:reach + nx, :] = src_ref[...].T
    sub = lax.broadcasted_iota(jnp.int32, (8, lines), 0)

    def body(b, carry):
        here = pad_ref[pl.ds(pl.multiple_of(b * 8, 8), 8), :]
        after = pad_ref[pl.ds(pl.multiple_of(b * 8 + 8, 8), 8), :]
        u_ref[0, b] = here
        for r in range(1, 8):
            u_ref[r, b] = jnp.where(sub < 8 - r, pltpu.roll(here, 8 - r, 0), pltpu.roll(after, 8 - r, 0))
        return carry

    lax.fori_loop(0, u_ref.shape[1], body, 0)
    n_out = nx // 8

    def q_range(g0, group):
        lo = max(0, -((8 * (g0 + group - 1) + 14 - reach) // 8))
        hi = (reach + nx - 1 - 8 * g0) // 8
        return lo, hi

    scan_offsets(u_ref, pen_ref, out_ref, n_out, 16, 8, q_range)


def zpass_kernel(pen_ref, src_ref, out_ref, pad_ref, u_ref):
    n_out = src_ref.shape[0]
    padc = KERNEL // 4
    pad_ref[...] = jnp.full(pad_ref.shape, jnp.inf, jnp.float32)
    pad_ref[padc:padc + n_out] = src_ref[...]
    lane = lax.broadcasted_iota(jnp.int32, src_ref.shape[1:], 1)
    sub_z = (lane // 8) % 4

    def body(b, carry):
        here = pad_ref[b]
        after = pad_ref[b + 1]
        u_ref[0, b] = here
        for r in range(1, 4):
            u_ref[r, b] = jnp.where(sub_z + r < 4, pltpu.roll(here, 128 - 8 * r, 1),
                                    pltpu.roll(after, 32 - 8 * r, 1))
        return carry

    lax.fori_loop(0, u_ref.shape[1], body, 0)

    def q_range(g0, group):
        lo = max(0, padc - 1 - (g0 + group - 1))
        hi = padc + n_out - 1 - g0
        return lo, hi

    scan_offsets(u_ref, pen_ref, out_ref, n_out, 16, 4, q_range)


def ypass_kernel(pen_ref, src_ref, out_ref, pad_ref, u_ref):
    n_out = src_ref.shape[0]
    padc = n_out
    pad_ref[...] = jnp.full(pad_ref.shape, jnp.inf, jnp.float32)
    pad_ref[padc:padc + n_out] = src_ref[...]
    lane = lax.broadcasted_iota(jnp.int32, src_ref.shape[1:], 2)
    sub_y = lane % 8

    def body(b, carry):
        here = pad_ref[b]
        after = pad_ref[b + 1]
        u_ref[0, b] = here
        for r in range(1, 8):
            u_ref[r, b] = jnp.where(sub_y + r < 8, pltpu.roll(here, 128 - r, 2),
                                    pltpu.roll(after, 8 - r, 2))
        return carry

    lax.fori_loop(0, u_ref.shape[1], body, 0)

    def q_range(g0, group):
        lo = max(0, padc - 1 - (g0 + group - 1))
        hi = padc + n_out - 1 - g0
        return lo, hi

    scan_offsets(u_ref, pen_ref, out_ref, n_out, 1, 8, q_range)


def transpose_kernel(src_ref, out_ref):
    out_ref[...] = src_ref[...].T


def local_call(kernel, out_shape, scratch, *args):
    vmem = pl.BlockSpec(memory_space=pltpu.VMEM)
    smem = pl.BlockSpec(memory_space=pltpu.SMEM)
    specs = [smem if a.ndim == 1 else vmem for a in args]
    return pl.pallas_call(
        kernel,
        out_shape=jax.ShapeDtypeStruct(out_shape, jnp.float32),
        in_specs=specs,
        out_specs=vmem,
        scratch_shapes=[pltpu.VMEM(s, jnp.float32) for s in scratch],
    )(*args)


def zy_kernel(pen_z_ref, pen_y_ref, src_ref, out_ref, pad_ref, u_ref, w_ref):
    n_out = src_ref.shape[0]
    padc = KERNEL // 4
    pad_ref[...] = jnp.full(pad_ref.shape, jnp.inf, jnp.float32)
    pad_ref[padc:padc + n_out] = src_ref[...]
    lane = lax.broadcasted_iota(jnp.int32, src_ref.shape[1:], 1)
    sub = lax.broadcasted_iota(jnp.int32, src_ref.shape[1:], 0)
    sub_z = (lane // 8) % 4
    sub_y = lane % 8

    def zbody(b, carry):
        here = pad_ref[b]
        after = pad_ref[b + 1]
        u_ref[0, b] = here
        for r in range(1, 4):
            u_ref[r, b] = jnp.where(sub_z + r < 4, pltpu.roll(here, 128 - 8 * r, 1),
                                    pltpu.roll(after, 32 - 8 * r, 1))
        return carry

    lax.fori_loop(0, u_ref.shape[1], zbody, 0)

    def q_range(g0, group):
        lo = max(0, padc - 1 - (g0 + group - 1))
        hi = padc + n_out - 1 - g0
        return lo, hi

    scan_offsets(u_ref, pen_z_ref, out_ref, n_out, 16, 4, q_range)

    def wbody(a, carry):
        v = out_ref[a]
        w_ref[0, a] = v
        for r in range(1, 8):
            w_ref[r, a] = jnp.where(sub_y + r < 8, pltpu.roll(v, 128 - r, 1),
                                    pltpu.roll(pltpu.roll(v, 8 - r, 1), 7, 0))
        return carry

    lax.fori_loop(0, n_out, wbody, 0)
    group = 8
    shifts = []
    for db in range(-8, 8):
        for dy in range(8):
            carry_in = (sub_y + dy >= 8).astype(jnp.int32)
            row = sub + db + carry_in
            valid = (row >= 0) & (row <= 7)
            shifts.append((db, dy, valid))

    def ybody(i, carry):
        a0 = pl.multiple_of(i * group, group)
        acc = [jnp.full(src_ref.shape[1:], jnp.inf, jnp.float32) for _ in range(group)]
        for db, dy, valid in shifts:
            penvec = jnp.where(valid, pen_y_ref[8 * db + dy + 64], jnp.inf)
            for g in range(group):
                v = w_ref[dy, a0 + g]
                if db % 8:
                    v = pltpu.roll(v, (8 - db) % 8, 0)
                acc[g] = jnp.minimum(acc[g], v + penvec)
        for g in range(group):
            out_ref[a0 + g] = acc[g]
        return carry

    lax.fori_loop(0, n_out // group, ybody, 0)


def regularize(current):
    levels, nz, ny, nx = current.shape
    lines = levels * nz * ny
    assert lines == 128 and nx % 8 == 0
    n_gz = lax.axis_size("gz")
    n_gy = lax.axis_size("gy")
    assert n_gz * n_gy == nx and ny == 8 and n_gy == 8
    xq = (KERNEL + 7) // 8
    nxo = nx // 8
    pen_x = penalty_table(8 * (xq * 2 + 2), KERNEL)
    xpad_rows = 8 * (nxo + 2 * xq + 3)
    t1 = local_call(xpass_kernel, (nxo, 8, lines), [(xpad_rows, lines), (8, nxo + 2 * xq + 2, 8, lines)],
                    pen_x, current.reshape(lines, nx))
    r1 = lax.all_to_all(t1.reshape(nx, lines), ("gz", "gy"), 0, 0, tiled=True)
    r1 = r1.reshape(n_gz, n_gy, lines)
    zq = KERNEL // 4
    pen_z = penalty_table(4 * (2 * zq + 2), KERNEL)
    pen_y = penalty_table(8 * 2 * n_gy, 8 * n_gy)
    t2 = pl.pallas_call(
        zy_kernel,
        out_shape=jax.ShapeDtypeStruct(r1.shape, jnp.float32),
        in_specs=[pl.BlockSpec(memory_space=pltpu.SMEM)] * 2 + [pl.BlockSpec(memory_space=pltpu.VMEM)],
        out_specs=pl.BlockSpec(memory_space=pltpu.VMEM),
        scratch_shapes=[pltpu.VMEM((n_gz + 2 * zq + 3, 8, lines), jnp.float32),
                        pltpu.VMEM((4, n_gz + 2 * zq + 2, 8, lines), jnp.float32),
                        pltpu.VMEM((8, n_gz, 8, lines), jnp.float32)],
    )(pen_z, pen_y, r1)
    r2 = lax.all_to_all(t2.reshape(nx, lines), ("gz", "gy"), 0, 0, tiled=True)
    out = local_call(transpose_kernel, (lines, nx), [], r2)
    return out.reshape(current.shape)


def body(levels, ct_image, region_means):
    current = evolve_all(levels, ct_image, region_means)
    return (current, regularize(current))


def solution(mesh):
    return jax.shard_map(
        body,
        mesh=mesh,
        in_specs=(P(None, "gz", "gy", None), P("gz", "gy", None), P()),
        out_specs=(P(None, "gz", "gy", None), P(None, "gz", "gy", None)),
        check_vma=False,
    )
```

```python
import math

import jax
import jax.numpy as jnp
from jax import lax
from jax.experimental import pallas as pl
from jax.experimental.pallas import tpu as pltpu
from jax.sharding import PartitionSpec as P

LEVELS = 4
PHASES = 16
UPDATES = 2
KERNEL = 200


PENALTY = 0.0005
STEP_SIZE = 0.5


def arctan(x):
    ax = jnp.abs(x)
    big = ax > 2.414213562373095
    mid = ax > 0.4142135623730950
    z_big = -1.0 / jnp.where(big, ax, 1.0)
    z_mid = (ax - 1.0) / (ax + 1.0)
    z = jnp.where(big, z_big, jnp.where(mid, z_mid, ax))
    base = jnp.where(big, math.pi / 2, jnp.where(mid, math.pi / 4, 0.0))
    zz = z * z
    poly = (((8.05374449538e-2 * zz - 1.38776856032e-1) * zz + 1.99777106478e-1) * zz
            - 3.33329491539e-1) * zz * z + z
    r = base + poly
    return jnp.where(x < 0, -r, r)


def compute_step(means_ref, cur_ref, zlo_ref, zhi_ref, ylo_ref, yhi_ref, ct_ref, out_ref):
    nz, ny, nx = cur_ref.shape[1], cur_ref.shape[2], cur_ref.shape[3]
    shape = (ny, nx)
    xi = lax.broadcasted_iota(jnp.int32, shape, 1)
    yi = lax.broadcasted_iota(jnp.int32, shape, 0)
    xa = pltpu.roll(xi, 1, 1)
    xb = pltpu.roll(xi, nx - 1, 1)
    xa_ok = jnp.abs(xa - xi) == 1
    xb_ok = jnp.abs(xb - xi) == 1
    ya = pltpu.roll(yi, 1, 0)
    yb = pltpu.roll(yi, ny - 1, 0)
    ya_ok = jnp.abs(ya - yi) == 1
    yb_ok = jnp.abs(yb - yi) == 1
    low_row = yi == 0
    means = [means_ref[p] for p in range(PHASES)]
    for z in range(nz):
        picture = ct_ref[z]
        energy = []
        for p in range(PHASES):
            differ = picture - means[p]
            energy.append(differ * differ)
        phis, lap, g1, g0, dl = [], [], [], [], []
        for k in range(LEVELS):
            c = cur_ref[k, z]
            zm = zlo_ref[k] if z == 0 else cur_ref[k, z - 1]
            zp = zhi_ref[k] if z == nz - 1 else cur_ref[k, z + 1]
            edge = jnp.where(low_row, ylo_ref[k, z], yhi_ref[k, z])
            ym = jnp.where(ya_ok, pltpu.roll(c, 1, 0), edge)
            yp = jnp.where(yb_ok, pltpu.roll(c, ny - 1, 0), edge)
            xm = jnp.where(xa_ok, pltpu.roll(c, 1, 1), 0.0)
            xp = jnp.where(xb_ok, pltpu.roll(c, nx - 1, 1), 0.0)
            lap.append(zm + zp + ym + yp + xm + xp - 6.0 * c)
            h = 0.5 + arctan(c) / math.pi
            g1.append(h)
            g0.append(1.0 - h)
            dl.append(1.0 / (math.pi * (1.0 + c * c)))
            phis.append(c)
        g = (g0, g1)
        pair_lo = {(a, b): g[a][0] * g[b][1] for a in (0, 1) for b in (0, 1)}
        pair_hi = {(a, b): g[a][2] * g[b][3] for a in (0, 1) for b in (0, 1)}
        for k in range(LEVELS):
            force = None
            for q in range(PHASES // 2):
                low = q & ((1 << k) - 1)
                high = (q >> k) << (k + 1)
                p0 = high | low
                p1 = p0 | (1 << k)
                bits = [(p0 >> j) & 1 for j in range(LEVELS)]
                if k == 0:
                    prod = g[bits[1]][1] * pair_hi[(bits[2], bits[3])]
                elif k == 1:
                    prod = g[bits[0]][0] * pair_hi[(bits[2], bits[3])]
                elif k == 2:
                    prod = pair_lo[(bits[0], bits[1])] * g[bits[3]][3]
                else:
                    prod = pair_lo[(bits[0], bits[1])] * g[bits[2]][2]
                term = (energy[p1] - energy[p0]) * prod
                force = term if force is None else force + term
            out_ref[k, z] = phis[k] + STEP_SIZE * dl[k] * (lap[k] - force)


MESH = pl.DeviceIdType.MESH


def evolve_kernel(means_ref, cur_ref, ct_ref, out_ref, mid_ref, zlo_buf, zhi_buf, ylo_buf, yhi_buf,
                  send_sem, recv_sem):
    nz, ny = cur_ref.shape[1], cur_ref.shape[2]
    gz, gy = lax.axis_index("gz"), lax.axis_index("gy")
    n_gz, n_gy = lax.axis_size("gz"), lax.axis_size("gy")
    peers = [(gz > 0, (gz - 1, gy)), (gz < n_gz - 1, (gz + 1, gy)),
             (gy > 0, (gz, gy - 1)), (gy < n_gy - 1, (gz, gy + 1))]
    barrier = pltpu.get_barrier_semaphore()
    for present, dev in peers:
        @pl.when(present)
        def _(dev=dev):
            pl.semaphore_signal(barrier, inc=1, device_id=dev, device_id_type=MESH)
    count = sum(present.astype(jnp.int32) for present, _ in peers)
    pl.semaphore_wait(barrier, count)

    def exchange(step, src_ref):
        plan = [
            (gz < n_gz - 1, gz > 0, src_ref.at[:, nz - 1], zlo_buf.at[step], (gz + 1, gy)),
            (gz > 0, gz < n_gz - 1, src_ref.at[:, 0], zhi_buf.at[step], (gz - 1, gy)),
            (gy < n_gy - 1, gy > 0, src_ref.at[:, :, pl.ds(ny - 1, 1)], ylo_buf.at[step], (gz, gy + 1)),
            (gy > 0, gy < n_gy - 1, src_ref.at[:, :, pl.ds(0, 1)], yhi_buf.at[step], (gz, gy - 1)),
        ]
        copies = []
        for d, (sends, receives, src, dst, target) in enumerate(plan):
            copy = pltpu.make_async_remote_copy(
                src_ref=src, dst_ref=dst, send_sem=send_sem.at[step, d],
                recv_sem=recv_sem.at[step, d], device_id=target, device_id_type=MESH)

            @pl.when(sends)
            def _(copy=copy):
                copy.start()

            @pl.when(jnp.logical_not(receives))
            def _(dst=dst):
                dst[...] = jnp.zeros(dst.shape, jnp.float32)

            copies.append((sends, receives, copy))
        return copies

    def finish(copies):
        for sends, receives, copy in copies:
            @pl.when(receives)
            def _(copy=copy):
                copy.wait_recv()

    def drain(copies):
        for sends, receives, copy in copies:
            @pl.when(sends)
            def _(copy=copy):
                copy.wait_send()

    first = exchange(0, cur_ref)
    finish(first)
    compute_step(means_ref, cur_ref, zlo_buf.at[0], zhi_buf.at[0], ylo_buf.at[0], yhi_buf.at[0], ct_ref, mid_ref)
    drain(first)
    second = exchange(1, mid_ref)
    finish(second)
    compute_step(means_ref, mid_ref, zlo_buf.at[1], zhi_buf.at[1], ylo_buf.at[1], yhi_buf.at[1], ct_ref, out_ref)
    drain(second)


def evolve_all(current, picture, region_means):
    levels, nz, ny, nx = current.shape
    vmem = pl.BlockSpec(memory_space=pltpu.VMEM)
    f32 = jnp.float32
    return pl.pallas_call(
        evolve_kernel,
        out_shape=jax.ShapeDtypeStruct(current.shape, current.dtype),
        in_specs=[pl.BlockSpec(memory_space=pltpu.SMEM), vmem, vmem],
        out_specs=vmem,
        scratch_shapes=[
            pltpu.VMEM(current.shape, f32),
            pltpu.VMEM((2, levels, ny, nx), f32),
            pltpu.VMEM((2, levels, ny, nx), f32),
            pltpu.VMEM((2, levels, nz, 1, nx), f32),
            pltpu.VMEM((2, levels, nz, 1, nx), f32),
            pltpu.SemaphoreType.DMA((2, 4)),
            pltpu.SemaphoreType.DMA((2, 4)),
        ],
        compiler_params=pltpu.CompilerParams(collective_id=0, has_side_effects=True),
    )(region_means, current, picture)


def penalty_table(count, offset):
    distance = (jnp.arange(count, dtype=jnp.int32) - offset).astype(jnp.float32)
    return jnp.where(
        jnp.abs(distance) <= KERNEL, PENALTY * (distance * distance), jnp.inf
    ).astype(jnp.float32)


def scan_offsets(u_ref, pen_ref, out_ref, n_out, group, nrot, q_range):
    for g0 in range(0, n_out, group):
        q_lo, q_hi = q_range(g0, group)
        q_hi = min(q_hi, pen_ref.shape[0] // nrot - 1, u_ref.shape[1] - g0 - group)

        def body(q, acc, g0=g0):
            for r in range(nrot):
                vals = u_ref[r, pl.ds(g0 + q, group)]
                acc = jnp.minimum(acc, vals + pen_ref[q * nrot + r])
            return acc

        init = jnp.full((group,) + tuple(out_ref.shape[1:]), jnp.inf, jnp.float32)
        out_ref[g0:g0 + group] = lax.fori_loop(q_lo, q_hi + 1, body, init, unroll=2)


def build_rotations(pad_ref, u_ref, nrot, pick, chunk=8):
    def body(i, carry):
        b0 = pl.multiple_of(i * chunk, chunk)
        here = pad_ref[pl.ds(b0, chunk)]
        after = pad_ref[pl.ds(b0 + 1, chunk)]
        u_ref[0, pl.ds(b0, chunk)] = here
        for r in range(1, nrot):
            u_ref[r, pl.ds(b0, chunk)] = pick(r, here, after)
        return carry

    lax.fori_loop(0, u_ref.shape[1] // chunk, body, 0)


def xpass_kernel(pen_ref, src_ref, out_ref, pad_ref, u_ref):
    lines, nx = src_ref.shape
    reach = KERNEL
    padc = reach // 8
    pad_ref[...] = jnp.full(pad_ref.shape, jnp.inf, jnp.float32)
    pad_ref[padc:padc + nx // 8] = src_ref[...].T.reshape(nx // 8, 8, lines)
    sub = lax.broadcasted_iota(jnp.int32, (8, 8, lines), 1)
    build_rotations(pad_ref, u_ref, 8, lambda r, here, after: jnp.where(
        sub < 8 - r, pltpu.roll(here, 8 - r, 1), pltpu.roll(after, 8 - r, 1)))
    n_out = nx // 8

    def q_range(g0, group):
        lo = max(0, -((8 * (g0 + group - 1) + 14 - reach) // 8))
        hi = (reach + nx - 1 - 8 * g0) // 8
        return lo, hi

    scan_offsets(u_ref, pen_ref, out_ref, n_out, 16, 8, q_range)


def transpose_kernel(src_ref, out_ref):
    out_ref[...] = src_ref[...].T


def local_call(kernel, out_shape, scratch, *args):
    vmem = pl.BlockSpec(memory_space=pltpu.VMEM)
    smem = pl.BlockSpec(memory_space=pltpu.SMEM)
    specs = [smem if a.ndim == 1 else vmem for a in args]
    return pl.pallas_call(
        kernel,
        out_shape=jax.ShapeDtypeStruct(out_shape, jnp.float32),
        in_specs=specs,
        out_specs=vmem,
        scratch_shapes=[pltpu.VMEM(s, jnp.float32) for s in scratch],
    )(*args)


def zy_kernel(pen_z_ref, pen_y_ref, src_ref, out_ref, pad_ref, u_ref, w_ref):
    n_out = src_ref.shape[0]
    padc = KERNEL // 4
    pad_ref[...] = jnp.full(pad_ref.shape, jnp.inf, jnp.float32)
    pad_ref[padc:padc + n_out] = src_ref[...]
    lane = lax.broadcasted_iota(jnp.int32, src_ref.shape[1:], 1)
    sub = lax.broadcasted_iota(jnp.int32, src_ref.shape[1:], 0)
    sub_z = (lane // 8) % 4
    sub_y = lane % 8

    lane3 = lax.broadcasted_iota(jnp.int32, (8,) + tuple(src_ref.shape[1:]), 2)
    sub_z3 = (lane3 // 8) % 4
    sub_y3 = lane3 % 8
    build_rotations(pad_ref, u_ref, 4, lambda r, here, after: jnp.where(
        sub_z3 + r < 4, pltpu.roll(here, 128 - 8 * r, 2), pltpu.roll(after, 32 - 8 * r, 2)))

    def q_range(g0, group):
        lo = max(0, padc - 1 - (g0 + group - 1))
        hi = padc + n_out - 1 - g0
        return lo, hi

    scan_offsets(u_ref, pen_z_ref, out_ref, n_out, 16, 4, q_range)

    def wbody(i, carry):
        a0 = pl.multiple_of(i * 8, 8)
        v = out_ref[pl.ds(a0, 8)]
        w_ref[0, pl.ds(a0, 8)] = v
        for r in range(1, 8):
            w_ref[r, pl.ds(a0, 8)] = jnp.where(sub_y3 + r < 8, pltpu.roll(v, 128 - r, 2),
                                               pltpu.roll(pltpu.roll(v, 8 - r, 2), 7, 1))
        return carry

    lax.fori_loop(0, n_out // 8, wbody, 0)
    group = 8
    shifts = []
    for db in range(-8, 8):
        for dy in range(8):
            carry_in = (sub_y + dy >= 8).astype(jnp.int32)
            row = sub + db + carry_in
            valid = (row >= 0) & (row <= 7)
            shifts.append((db, dy, valid))

    def ybody(i, carry):
        a0 = pl.multiple_of(i * group, group)
        acc = [jnp.full(src_ref.shape[1:], jnp.inf, jnp.float32) for _ in range(group)]
        for db, dy, valid in shifts:
            penvec = jnp.where(valid, pen_y_ref[8 * db + dy + 64], jnp.inf)
            for g in range(group):
                v = w_ref[dy, a0 + g]
                if db % 8:
                    v = pltpu.roll(v, (8 - db) % 8, 0)
                acc[g] = jnp.minimum(acc[g], v + penvec)
        for g in range(group):
            out_ref[a0 + g] = acc[g]
        return carry

    lax.fori_loop(0, n_out // group, ybody, 0)


def regularize(current):
    levels, nz, ny, nx = current.shape
    lines = levels * nz * ny
    assert lines == 128 and nx % 8 == 0
    n_gz = lax.axis_size("gz")
    n_gy = lax.axis_size("gy")
    assert n_gz * n_gy == nx and ny == 8 and n_gy == 8
    xq = (KERNEL + 7) // 8
    nxo = nx // 8
    pen_x = penalty_table(8 * (xq * 2 + 2), KERNEL)
    xu = -(-(nxo + 2 * xq + 2) // 8) * 8
    t1 = local_call(xpass_kernel, (nxo, 8, lines), [(xu + 8, 8, lines), (8, xu, 8, lines)],
                    pen_x, current.reshape(lines, nx))
    r1 = lax.all_to_all(t1.reshape(nx, lines), ("gz", "gy"), 0, 0, tiled=True)
    r1 = r1.reshape(n_gz, n_gy, lines)
    zq = KERNEL // 4
    pen_z = penalty_table(4 * (2 * zq + 2), KERNEL)
    zu = -(-(n_gz + 2 * zq + 2) // 8) * 8
    pen_y = penalty_table(8 * 2 * n_gy, 8 * n_gy)
    t2 = pl.pallas_call(
        zy_kernel,
        out_shape=jax.ShapeDtypeStruct(r1.shape, jnp.float32),
        in_specs=[pl.BlockSpec(memory_space=pltpu.SMEM)] * 2 + [pl.BlockSpec(memory_space=pltpu.VMEM)],
        out_specs=pl.BlockSpec(memory_space=pltpu.VMEM),
        scratch_shapes=[pltpu.VMEM((zu + 8, 8, lines), jnp.float32),
                        pltpu.VMEM((4, zu, 8, lines), jnp.float32),
                        pltpu.VMEM((8, n_gz, 8, lines), jnp.float32)],
    )(pen_z, pen_y, r1)
    r2 = lax.all_to_all(t2.reshape(nx, lines), ("gz", "gy"), 0, 0, tiled=True)
    out = local_call(transpose_kernel, (lines, nx), [], r2)
    return out.reshape(current.shape)


def body(levels, ct_image, region_means):
    current = evolve_all(levels, ct_image, region_means)
    return (current, regularize(current))


def solution(mesh):
    return jax.shard_map(
        body,
        mesh=mesh,
        in_specs=(P(None, "gz", "gy", None), P("gz", "gy", None), P()),
        out_specs=(P(None, "gz", "gy", None), P(None, "gz", "gy", None)),
        check_vma=False,
    )
```

```python
import math

import jax
import jax.numpy as jnp
from jax import lax
from jax.experimental import pallas as pl
from jax.experimental.pallas import tpu as pltpu
from jax.sharding import PartitionSpec as P

LEVELS = 4
PHASES = 16
UPDATES = 2
KERNEL = 200


PENALTY = 0.0005
STEP_SIZE = 0.5


def arctan(x):
    ax = jnp.abs(x)
    big = ax > 2.414213562373095
    mid = ax > 0.4142135623730950
    z_big = -1.0 / jnp.where(big, ax, 1.0)
    z_mid = (ax - 1.0) / (ax + 1.0)
    z = jnp.where(big, z_big, jnp.where(mid, z_mid, ax))
    base = jnp.where(big, math.pi / 2, jnp.where(mid, math.pi / 4, 0.0))
    zz = z * z
    poly = (((8.05374449538e-2 * zz - 1.38776856032e-1) * zz + 1.99777106478e-1) * zz
            - 3.33329491539e-1) * zz * z + z
    r = base + poly
    return jnp.where(x < 0, -r, r)


def compute_step(means_ref, cur_ref, zlo_ref, zhi_ref, ylo_ref, yhi_ref, ct_ref, out_ref):
    nz, ny, nx = cur_ref.shape[1], cur_ref.shape[2], cur_ref.shape[3]
    shape = (ny, nx)
    xi = lax.broadcasted_iota(jnp.int32, shape, 1)
    yi = lax.broadcasted_iota(jnp.int32, shape, 0)
    xa = pltpu.roll(xi, 1, 1)
    xb = pltpu.roll(xi, nx - 1, 1)
    xa_ok = jnp.abs(xa - xi) == 1
    xb_ok = jnp.abs(xb - xi) == 1
    ya = pltpu.roll(yi, 1, 0)
    yb = pltpu.roll(yi, ny - 1, 0)
    ya_ok = jnp.abs(ya - yi) == 1
    yb_ok = jnp.abs(yb - yi) == 1
    low_row = yi == 0
    means = [means_ref[p] for p in range(PHASES)]
    for z in range(nz):
        picture = ct_ref[z]
        energy = []
        for p in range(PHASES):
            differ = picture - means[p]
            energy.append(differ * differ)
        phis, lap, g1, g0, dl = [], [], [], [], []
        for k in range(LEVELS):
            c = cur_ref[k, z]
            zm = zlo_ref[k] if z == 0 else cur_ref[k, z - 1]
            zp = zhi_ref[k] if z == nz - 1 else cur_ref[k, z + 1]
            edge = jnp.where(low_row, ylo_ref[k, z], yhi_ref[k, z])
            ym = jnp.where(ya_ok, pltpu.roll(c, 1, 0), edge)
            yp = jnp.where(yb_ok, pltpu.roll(c, ny - 1, 0), edge)
            xm = jnp.where(xa_ok, pltpu.roll(c, 1, 1), 0.0)
            xp = jnp.where(xb_ok, pltpu.roll(c, nx - 1, 1), 0.0)
            lap.append(zm + zp + ym + yp + xm + xp - 6.0 * c)
            h = 0.5 + arctan(c) / math.pi
            g1.append(h)
            g0.append(1.0 - h)
            dl.append(1.0 / (math.pi * (1.0 + c * c)))
            phis.append(c)
        g = (g0, g1)
        pair_lo = {(a, b): g[a][0] * g[b][1] for a in (0, 1) for b in (0, 1)}
        pair_hi = {(a, b): g[a][2] * g[b][3] for a in (0, 1) for b in (0, 1)}
        for k in range(LEVELS):
            force = None
            for q in range(PHASES // 2):
                low = q & ((1 << k) - 1)
                high = (q >> k) << (k + 1)
                p0 = high | low
                p1 = p0 | (1 << k)
                bits = [(p0 >> j) & 1 for j in range(LEVELS)]
                if k == 0:
                    prod = g[bits[1]][1] * pair_hi[(bits[2], bits[3])]
                elif k == 1:
                    prod = g[bits[0]][0] * pair_hi[(bits[2], bits[3])]
                elif k == 2:
                    prod = pair_lo[(bits[0], bits[1])] * g[bits[3]][3]
                else:
                    prod = pair_lo[(bits[0], bits[1])] * g[bits[2]][2]
                term = (energy[p1] - energy[p0]) * prod
                force = term if force is None else force + term
            out_ref[k, z] = phis[k] + STEP_SIZE * dl[k] * (lap[k] - force)


MESH = pl.DeviceIdType.MESH


def evolve_kernel(means_ref, cur_ref, ct_ref, out_ref, mid_ref, zlo_buf, zhi_buf, ylo_buf, yhi_buf,
                  send_sem, recv_sem):
    nz, ny = cur_ref.shape[1], cur_ref.shape[2]
    gz, gy = lax.axis_index("gz"), lax.axis_index("gy")
    n_gz, n_gy = lax.axis_size("gz"), lax.axis_size("gy")
    peers = [(gz > 0, (gz - 1, gy)), (gz < n_gz - 1, (gz + 1, gy)),
             (gy > 0, (gz, gy - 1)), (gy < n_gy - 1, (gz, gy + 1))]
    barrier = pltpu.get_barrier_semaphore()
    for present, dev in peers:
        @pl.when(present)
        def _(dev=dev):
            pl.semaphore_signal(barrier, inc=1, device_id=dev, device_id_type=MESH)
    count = sum(present.astype(jnp.int32) for present, _ in peers)
    pl.semaphore_wait(barrier, count)

    def exchange(step, src_ref):
        plan = [
            (gz < n_gz - 1, gz > 0, src_ref.at[:, nz - 1], zlo_buf.at[step], (gz + 1, gy)),
            (gz > 0, gz < n_gz - 1, src_ref.at[:, 0], zhi_buf.at[step], (gz - 1, gy)),
            (gy < n_gy - 1, gy > 0, src_ref.at[:, :, pl.ds(ny - 1, 1)], ylo_buf.at[step], (gz, gy + 1)),
            (gy > 0, gy < n_gy - 1, src_ref.at[:, :, pl.ds(0, 1)], yhi_buf.at[step], (gz, gy - 1)),
        ]
        copies = []
        for d, (sends, receives, src, dst, target) in enumerate(plan):
            copy = pltpu.make_async_remote_copy(
                src_ref=src, dst_ref=dst, send_sem=send_sem.at[step, d],
                recv_sem=recv_sem.at[step, d], device_id=target, device_id_type=MESH)

            @pl.when(sends)
            def _(copy=copy):
                copy.start()

            @pl.when(jnp.logical_not(receives))
            def _(dst=dst):
                dst[...] = jnp.zeros(dst.shape, jnp.float32)

            copies.append((sends, receives, copy))
        return copies

    def finish(copies):
        for sends, receives, copy in copies:
            @pl.when(receives)
            def _(copy=copy):
                copy.wait_recv()

    def drain(copies):
        for sends, receives, copy in copies:
            @pl.when(sends)
            def _(copy=copy):
                copy.wait_send()

    first = exchange(0, cur_ref)
    finish(first)
    compute_step(means_ref, cur_ref, zlo_buf.at[0], zhi_buf.at[0], ylo_buf.at[0], yhi_buf.at[0], ct_ref, mid_ref)
    drain(first)
    second = exchange(1, mid_ref)
    finish(second)
    compute_step(means_ref, mid_ref, zlo_buf.at[1], zhi_buf.at[1], ylo_buf.at[1], yhi_buf.at[1], ct_ref, out_ref)
    drain(second)


def evolve_all(current, picture, region_means):
    levels, nz, ny, nx = current.shape
    vmem = pl.BlockSpec(memory_space=pltpu.VMEM)
    f32 = jnp.float32
    return pl.pallas_call(
        evolve_kernel,
        out_shape=jax.ShapeDtypeStruct(current.shape, current.dtype),
        in_specs=[pl.BlockSpec(memory_space=pltpu.SMEM), vmem, vmem],
        out_specs=vmem,
        scratch_shapes=[
            pltpu.VMEM(current.shape, f32),
            pltpu.VMEM((2, levels, ny, nx), f32),
            pltpu.VMEM((2, levels, ny, nx), f32),
            pltpu.VMEM((2, levels, nz, 1, nx), f32),
            pltpu.VMEM((2, levels, nz, 1, nx), f32),
            pltpu.SemaphoreType.DMA((2, 4)),
            pltpu.SemaphoreType.DMA((2, 4)),
        ],
        compiler_params=pltpu.CompilerParams(collective_id=0, has_side_effects=True),
    )(region_means, current, picture)


def penalty_table(count, offset):
    distance = (jnp.arange(count, dtype=jnp.int32) - offset).astype(jnp.float32)
    return jnp.where(
        jnp.abs(distance) <= KERNEL, PENALTY * (distance * distance), jnp.inf
    ).astype(jnp.float32)


def scan_offsets(u_ref, pen_ref, out_ref, n_out, group, nrot, q_range):
    for g0 in range(0, n_out, group):
        q_lo, q_hi = q_range(g0, group)
        q_hi = min(q_hi, pen_ref.shape[0] // nrot - 1, u_ref.shape[1] - g0 - group)

        def body(q, acc, g0=g0):
            for r in range(nrot):
                vals = u_ref[r, pl.ds(g0 + q, group)]
                acc = jnp.minimum(acc, vals + pen_ref[q * nrot + r])
            return acc

        init = jnp.full((group,) + tuple(out_ref.shape[1:]), jnp.inf, jnp.float32)
        out_ref[g0:g0 + group] = lax.fori_loop(q_lo, q_hi + 1, body, init, unroll=2)


def build_rotations(pad_ref, u_ref, nrot, pick, chunk=8):
    def body(i, carry):
        b0 = pl.multiple_of(i * chunk, chunk)
        here = pad_ref[pl.ds(b0, chunk)]
        after = pad_ref[pl.ds(b0 + 1, chunk)]
        u_ref[0, pl.ds(b0, chunk)] = here
        for r in range(1, nrot):
            u_ref[r, pl.ds(b0, chunk)] = pick(r, here, after)
        return carry

    lax.fori_loop(0, u_ref.shape[1] // chunk, body, 0)


def xpass_kernel(pen_ref, src_ref, out_ref, pad_ref, u_ref):
    lines, nx = src_ref.shape
    reach = KERNEL
    padc = reach // 8
    pad_ref[...] = jnp.full(pad_ref.shape, jnp.inf, jnp.float32)
    pad_ref[padc:padc + nx // 8] = src_ref[...].T.reshape(nx // 8, 8, lines)
    sub = lax.broadcasted_iota(jnp.int32, (8, 8, lines), 1)
    build_rotations(pad_ref, u_ref, 8, lambda r, here, after: jnp.where(
        sub < 8 - r, pltpu.roll(here, 8 - r, 1), pltpu.roll(after, 8 - r, 1)))
    n_out = nx // 8

    def q_range(g0, group):
        lo = max(0, -((8 * (g0 + group - 1) + 14 - reach) // 8))
        hi = (reach + nx - 1 - 8 * g0) // 8
        return lo, hi

    scan_offsets(u_ref, pen_ref, out_ref, n_out, 16, 8, q_range)


def transpose_kernel(src_ref, out_ref):
    out_ref[...] = src_ref[...].T


def local_call(kernel, out_shape, scratch, *args):
    vmem = pl.BlockSpec(memory_space=pltpu.VMEM)
    smem = pl.BlockSpec(memory_space=pltpu.SMEM)
    specs = [smem if a.ndim == 1 else vmem for a in args]
    return pl.pallas_call(
        kernel,
        out_shape=jax.ShapeDtypeStruct(out_shape, jnp.float32),
        in_specs=specs,
        out_specs=vmem,
        scratch_shapes=[pltpu.VMEM(s, jnp.float32) for s in scratch],
    )(*args)


def zy_kernel(pen_z_ref, pen_y_ref, src_ref, out_ref, pad_ref, u_ref, w_ref):
    n_out = src_ref.shape[0]
    padc = KERNEL // 4
    pad_ref[...] = jnp.full(pad_ref.shape, jnp.inf, jnp.float32)
    pad_ref[padc:padc + n_out] = src_ref[...]
    lane = lax.broadcasted_iota(jnp.int32, src_ref.shape[1:], 1)
    sub = lax.broadcasted_iota(jnp.int32, src_ref.shape[1:], 0)
    sub_z = (lane // 8) % 4
    sub_y = lane % 8

    lane3 = lax.broadcasted_iota(jnp.int32, (8,) + tuple(src_ref.shape[1:]), 2)
    sub_z3 = (lane3 // 8) % 4
    sub_y3 = lane3 % 8
    build_rotations(pad_ref, u_ref, 4, lambda r, here, after: jnp.where(
        sub_z3 + r < 4, pltpu.roll(here, 128 - 8 * r, 2), pltpu.roll(after, 32 - 8 * r, 2)))

    def q_range(g0, group):
        lo = max(0, padc - 1 - (g0 + group - 1))
        hi = padc + n_out - 1 - g0
        return lo, hi

    scan_offsets(u_ref, pen_z_ref, out_ref, n_out, 16, 4, q_range)

    def wbody(i, carry):
        a0 = pl.multiple_of(i * 8, 8)
        v = out_ref[pl.ds(a0, 8)]
        w_ref[0, pl.ds(a0, 8)] = v
        for r in range(1, 8):
            w_ref[r, pl.ds(a0, 8)] = jnp.where(sub_y3 + r < 8, pltpu.roll(v, 128 - r, 2),
                                               pltpu.roll(pltpu.roll(v, 8 - r, 2), 7, 1))
        return carry

    lax.fori_loop(0, n_out // 8, wbody, 0)
    group = 8
    shifts = []
    for db in range(-8, 8):
        for dy in range(8):
            carry_in = (sub_y + dy >= 8).astype(jnp.int32)
            row = sub + db + carry_in
            valid = (row >= 0) & (row <= 7)
            shifts.append((db, dy, valid))

    def ybody(i, carry):
        a0 = pl.multiple_of(i * group, group)
        acc = [jnp.full(src_ref.shape[1:], jnp.inf, jnp.float32) for _ in range(group)]
        for db, dy, valid in shifts:
            penvec = jnp.where(valid, pen_y_ref[8 * db + dy + 64], jnp.inf)
            for g in range(group):
                v = w_ref[dy, a0 + g]
                if db % 8:
                    v = pltpu.roll(v, (8 - db) % 8, 0)
                acc[g] = jnp.minimum(acc[g], v + penvec)
        for g in range(group):
            out_ref[a0 + g] = acc[g]
        return carry

    lax.fori_loop(0, n_out // group, ybody, 0)


def exchange_rows_kernel(src_ref, out_ref, recv_buf, send_sem, recv_sem, own_sem):
    n_gy = lax.axis_size("gy")
    n = src_ref.shape[0]
    me = lax.axis_index("gz") * n_gy + lax.axis_index("gy")

    def device(k):
        p = lax.rem(me + k, n)
        return p, (p // n_gy, lax.rem(p, n_gy))

    barrier = pltpu.get_barrier_semaphore()

    def greet(k, carry):
        _, dev = device(k)
        pl.semaphore_signal(barrier, inc=1, device_id=dev, device_id_type=MESH)
        return carry

    lax.fori_loop(1, n, greet, 0)
    pl.semaphore_wait(barrier, n - 1)

    def send(k, carry):
        p, dev = device(k)
        pltpu.make_async_remote_copy(
            src_ref=src_ref.at[pl.ds(p, 1)], dst_ref=recv_buf.at[pl.ds(me, 1)],
            send_sem=send_sem, recv_sem=recv_sem, device_id=dev, device_id_type=MESH).start()
        return carry

    lax.fori_loop(1, n, send, 0, unroll=8)
    own = pltpu.make_async_copy(src_ref.at[pl.ds(me, 1)], recv_buf.at[pl.ds(me, 1)], own_sem)
    own.start()
    own.wait()
    _, dev = device(1)
    total = pltpu.make_async_remote_copy(
        src_ref=src_ref.at[pl.ds(0, n - 1)], dst_ref=recv_buf.at[pl.ds(0, n - 1)],
        send_sem=send_sem, recv_sem=recv_sem, device_id=dev, device_id_type=MESH)
    total.wait_send()
    total.wait_recv()
    out_ref[...] = recv_buf[...]


def exchange_rows(rows, collective_id):
    vmem = pl.BlockSpec(memory_space=pltpu.VMEM)
    return pl.pallas_call(
        exchange_rows_kernel,
        out_shape=jax.ShapeDtypeStruct(rows.shape, rows.dtype),
        in_specs=[vmem],
        out_specs=vmem,
        scratch_shapes=[pltpu.VMEM(rows.shape, rows.dtype), pltpu.SemaphoreType.DMA(()),
                        pltpu.SemaphoreType.DMA(()), pltpu.SemaphoreType.DMA(())],
        compiler_params=pltpu.CompilerParams(collective_id=collective_id, has_side_effects=True),
    )(rows)


def regularize(current):
    levels, nz, ny, nx = current.shape
    lines = levels * nz * ny
    assert lines == 128 and nx % 8 == 0
    n_gz = lax.axis_size("gz")
    n_gy = lax.axis_size("gy")
    assert n_gz * n_gy == nx and ny == 8 and n_gy == 8
    xq = (KERNEL + 7) // 8
    nxo = nx // 8
    pen_x = penalty_table(8 * (xq * 2 + 2), KERNEL)
    xu = -(-(nxo + 2 * xq + 2) // 8) * 8
    t1 = local_call(xpass_kernel, (nxo, 8, lines), [(xu + 8, 8, lines), (8, xu, 8, lines)],
                    pen_x, current.reshape(lines, nx))
    r1 = exchange_rows(t1.reshape(nx, lines), 1).reshape(n_gz, n_gy, lines)
    zq = KERNEL // 4
    pen_z = penalty_table(4 * (2 * zq + 2), KERNEL)
    zu = -(-(n_gz + 2 * zq + 2) // 8) * 8
    pen_y = penalty_table(8 * 2 * n_gy, 8 * n_gy)
    t2 = pl.pallas_call(
        zy_kernel,
        out_shape=jax.ShapeDtypeStruct(r1.shape, jnp.float32),
        in_specs=[pl.BlockSpec(memory_space=pltpu.SMEM)] * 2 + [pl.BlockSpec(memory_space=pltpu.VMEM)],
        out_specs=pl.BlockSpec(memory_space=pltpu.VMEM),
        scratch_shapes=[pltpu.VMEM((zu + 8, 8, lines), jnp.float32),
                        pltpu.VMEM((4, zu, 8, lines), jnp.float32),
                        pltpu.VMEM((8, n_gz, 8, lines), jnp.float32)],
    )(pen_z, pen_y, r1)
    r2 = exchange_rows(t2.reshape(nx, lines), 2)
    out = local_call(transpose_kernel, (lines, nx), [], r2)
    return out.reshape(current.shape)


def body(levels, ct_image, region_means):
    current = evolve_all(levels, ct_image, region_means)
    return (current, regularize(current))


def solution(mesh):
    return jax.shard_map(
        body,
        mesh=mesh,
        in_specs=(P(None, "gz", "gy", None), P("gz", "gy", None), P()),
        out_specs=(P(None, "gz", "gy", None), P(None, "gz", "gy", None)),
        check_vma=False,
    )
```

```python
import functools
import math

import jax
import jax.numpy as jnp
from jax import lax
from jax.experimental import pallas as pl
from jax.experimental.pallas import tpu as pltpu
from jax.sharding import PartitionSpec as P

LEVELS = 4
PHASES = 16
UPDATES = 2
KERNEL = 200


PENALTY = 0.0005
STEP_SIZE = 0.5


def arctan(x):
    ax = jnp.abs(x)
    big = ax > 2.414213562373095
    mid = ax > 0.4142135623730950
    z_big = -1.0 / jnp.where(big, ax, 1.0)
    z_mid = (ax - 1.0) / (ax + 1.0)
    z = jnp.where(big, z_big, jnp.where(mid, z_mid, ax))
    base = jnp.where(big, math.pi / 2, jnp.where(mid, math.pi / 4, 0.0))
    zz = z * z
    poly = (((8.05374449538e-2 * zz - 1.38776856032e-1) * zz + 1.99777106478e-1) * zz
            - 3.33329491539e-1) * zz * z + z
    r = base + poly
    return jnp.where(x < 0, -r, r)


def compute_step(means_ref, cur_ref, zlo_ref, zhi_ref, ylo_ref, yhi_ref, ct_ref, out_ref):
    nz, ny, nx = cur_ref.shape[1], cur_ref.shape[2], cur_ref.shape[3]
    shape = (ny, nx)
    xi = lax.broadcasted_iota(jnp.int32, shape, 1)
    yi = lax.broadcasted_iota(jnp.int32, shape, 0)
    xa = pltpu.roll(xi, 1, 1)
    xb = pltpu.roll(xi, nx - 1, 1)
    xa_ok = jnp.abs(xa - xi) == 1
    xb_ok = jnp.abs(xb - xi) == 1
    ya = pltpu.roll(yi, 1, 0)
    yb = pltpu.roll(yi, ny - 1, 0)
    ya_ok = jnp.abs(ya - yi) == 1
    yb_ok = jnp.abs(yb - yi) == 1
    low_row = yi == 0
    means = [means_ref[p] for p in range(PHASES)]
    for z in range(nz):
        picture = ct_ref[z]
        energy = []
        for p in range(PHASES):
            differ = picture - means[p]
            energy.append(differ * differ)
        phis, lap, g1, g0, dl = [], [], [], [], []
        for k in range(LEVELS):
            c = cur_ref[k, z]
            zm = zlo_ref[k] if z == 0 else cur_ref[k, z - 1]
            zp = zhi_ref[k] if z == nz - 1 else cur_ref[k, z + 1]
            edge = jnp.where(low_row, ylo_ref[k, z], yhi_ref[k, z])
            ym = jnp.where(ya_ok, pltpu.roll(c, 1, 0), edge)
            yp = jnp.where(yb_ok, pltpu.roll(c, ny - 1, 0), edge)
            xm = jnp.where(xa_ok, pltpu.roll(c, 1, 1), 0.0)
            xp = jnp.where(xb_ok, pltpu.roll(c, nx - 1, 1), 0.0)
            lap.append(zm + zp + ym + yp + xm + xp - 6.0 * c)
            h = 0.5 + arctan(c) / math.pi
            g1.append(h)
            g0.append(1.0 - h)
            dl.append(1.0 / (math.pi * (1.0 + c * c)))
            phis.append(c)
        g = (g0, g1)
        pair_lo = {(a, b): g[a][0] * g[b][1] for a in (0, 1) for b in (0, 1)}
        pair_hi = {(a, b): g[a][2] * g[b][3] for a in (0, 1) for b in (0, 1)}
        for k in range(LEVELS):
            force = None
            for q in range(PHASES // 2):
                low = q & ((1 << k) - 1)
                high = (q >> k) << (k + 1)
                p0 = high | low
                p1 = p0 | (1 << k)
                bits = [(p0 >> j) & 1 for j in range(LEVELS)]
                if k == 0:
                    prod = g[bits[1]][1] * pair_hi[(bits[2], bits[3])]
                elif k == 1:
                    prod = g[bits[0]][0] * pair_hi[(bits[2], bits[3])]
                elif k == 2:
                    prod = pair_lo[(bits[0], bits[1])] * g[bits[3]][3]
                else:
                    prod = pair_lo[(bits[0], bits[1])] * g[bits[2]][2]
                term = (energy[p1] - energy[p0]) * prod
                force = term if force is None else force + term
            out_ref[k, z] = phis[k] + STEP_SIZE * dl[k] * (lap[k] - force)


MESH = pl.DeviceIdType.MESH


def evolve_kernel(means_ref, cur_ref, ct_ref, out_ref, mid_ref, zlo_buf, zhi_buf, ylo_buf, yhi_buf,
                  send_sem, recv_sem):
    nz, ny = cur_ref.shape[1], cur_ref.shape[2]
    gz, gy = lax.axis_index("gz"), lax.axis_index("gy")
    n_gz, n_gy = lax.axis_size("gz"), lax.axis_size("gy")
    peers = [(gz > 0, (gz - 1, gy)), (gz < n_gz - 1, (gz + 1, gy)),
             (gy > 0, (gz, gy - 1)), (gy < n_gy - 1, (gz, gy + 1))]
    barrier = pltpu.get_barrier_semaphore()
    for present, dev in peers:
        @pl.when(present)
        def _(dev=dev):
            pl.semaphore_signal(barrier, inc=1, device_id=dev, device_id_type=MESH)
    count = sum(present.astype(jnp.int32) for present, _ in peers)
    pl.semaphore_wait(barrier, count)

    def exchange(step, src_ref):
        plan = [
            (gz < n_gz - 1, gz > 0, src_ref.at[:, nz - 1], zlo_buf.at[step], (gz + 1, gy)),
            (gz > 0, gz < n_gz - 1, src_ref.at[:, 0], zhi_buf.at[step], (gz - 1, gy)),
            (gy < n_gy - 1, gy > 0, src_ref.at[:, :, pl.ds(ny - 1, 1)], ylo_buf.at[step], (gz, gy + 1)),
            (gy > 0, gy < n_gy - 1, src_ref.at[:, :, pl.ds(0, 1)], yhi_buf.at[step], (gz, gy - 1)),
        ]
        copies = []
        for d, (sends, receives, src, dst, target) in enumerate(plan):
            copy = pltpu.make_async_remote_copy(
                src_ref=src, dst_ref=dst, send_sem=send_sem.at[step, d],
                recv_sem=recv_sem.at[step, d], device_id=target, device_id_type=MESH)

            @pl.when(sends)
            def _(copy=copy):
                copy.start()

            @pl.when(jnp.logical_not(receives))
            def _(dst=dst):
                dst[...] = jnp.zeros(dst.shape, jnp.float32)

            copies.append((sends, receives, copy))
        return copies

    def finish(copies):
        for sends, receives, copy in copies:
            @pl.when(receives)
            def _(copy=copy):
                copy.wait_recv()

    def drain(copies):
        for sends, receives, copy in copies:
            @pl.when(sends)
            def _(copy=copy):
                copy.wait_send()

    first = exchange(0, cur_ref)
    finish(first)
    compute_step(means_ref, cur_ref, zlo_buf.at[0], zhi_buf.at[0], ylo_buf.at[0], yhi_buf.at[0], ct_ref, mid_ref)
    drain(first)
    second = exchange(1, mid_ref)
    finish(second)
    compute_step(means_ref, mid_ref, zlo_buf.at[1], zhi_buf.at[1], ylo_buf.at[1], yhi_buf.at[1], ct_ref, out_ref)
    drain(second)


def evolve_all(current, picture, region_means):
    levels, nz, ny, nx = current.shape
    vmem = pl.BlockSpec(memory_space=pltpu.VMEM)
    f32 = jnp.float32
    return pl.pallas_call(
        evolve_kernel,
        out_shape=jax.ShapeDtypeStruct(current.shape, current.dtype),
        in_specs=[pl.BlockSpec(memory_space=pltpu.SMEM), vmem, vmem],
        out_specs=vmem,
        scratch_shapes=[
            pltpu.VMEM(current.shape, f32),
            pltpu.VMEM((2, levels, ny, nx), f32),
            pltpu.VMEM((2, levels, ny, nx), f32),
            pltpu.VMEM((2, levels, nz, 1, nx), f32),
            pltpu.VMEM((2, levels, nz, 1, nx), f32),
            pltpu.SemaphoreType.DMA((2, 4)),
            pltpu.SemaphoreType.DMA((2, 4)),
        ],
        compiler_params=pltpu.CompilerParams(collective_id=0, has_side_effects=True),
    )(region_means, current, picture)


def penalty_table(count, offset):
    distance = (jnp.arange(count, dtype=jnp.int32) - offset).astype(jnp.float32)
    return jnp.where(
        jnp.abs(distance) <= KERNEL, PENALTY * (distance * distance), jnp.inf
    ).astype(jnp.float32)


def scan_offsets(u_ref, pen_ref, out_ref, n_out, group, nrot, q_range):
    for g0 in range(0, n_out, group):
        q_lo, q_hi = q_range(g0, group)
        q_hi = min(q_hi, pen_ref.shape[0] // nrot - 1, u_ref.shape[1] - g0 - group)

        def body(q, acc, g0=g0):
            for r in range(nrot):
                vals = u_ref[r, pl.ds(g0 + q, group)]
                acc = jnp.minimum(acc, vals + pen_ref[q * nrot + r])
            return acc

        init = jnp.full((group,) + tuple(out_ref.shape[1:]), jnp.inf, jnp.float32)
        out_ref[g0:g0 + group] = lax.fori_loop(q_lo, q_hi + 1, body, init, unroll=2)


def build_rotations(pad_ref, u_ref, nrot, pick, chunk=8):
    def body(i, carry):
        b0 = pl.multiple_of(i * chunk, chunk)
        here = pad_ref[pl.ds(b0, chunk)]
        after = pad_ref[pl.ds(b0 + 1, chunk)]
        u_ref[0, pl.ds(b0, chunk)] = here
        for r in range(1, nrot):
            u_ref[r, pl.ds(b0, chunk)] = pick(r, here, after)
        return carry

    lax.fori_loop(0, u_ref.shape[1] // chunk, body, 0)


def xpass_kernel(pen_ref, src_ref, out_ref, pad_ref, u_ref):
    lines, nx = src_ref.shape
    reach = KERNEL
    padc = reach // 8
    pad_ref[...] = jnp.full(pad_ref.shape, jnp.inf, jnp.float32)
    pad_ref[padc:padc + nx // 8] = src_ref[...].T.reshape(nx // 8, 8, lines)
    sub = lax.broadcasted_iota(jnp.int32, (8, 8, lines), 1)
    build_rotations(pad_ref, u_ref, 8, lambda r, here, after: jnp.where(
        sub < 8 - r, pltpu.roll(here, 8 - r, 1), pltpu.roll(after, 8 - r, 1)))
    n_out = nx // 8

    def q_range(g0, group):
        lo = max(0, -((8 * (g0 + group - 1) + 14 - reach) // 8))
        hi = (reach + nx - 1 - 8 * g0) // 8
        return lo, hi

    scan_offsets(u_ref, pen_ref, out_ref, n_out, 16, 8, q_range)


def transpose_kernel(src_ref, out_ref):
    out_ref[...] = src_ref[...].T


def local_call(kernel, out_shape, scratch, *args):
    vmem = pl.BlockSpec(memory_space=pltpu.VMEM)
    smem = pl.BlockSpec(memory_space=pltpu.SMEM)
    specs = [smem if a.ndim == 1 else vmem for a in args]
    return pl.pallas_call(
        kernel,
        out_shape=jax.ShapeDtypeStruct(out_shape, jnp.float32),
        in_specs=specs,
        out_specs=vmem,
        scratch_shapes=[pltpu.VMEM(s, jnp.float32) for s in scratch],
    )(*args)


def zy_kernel(pen_z_ref, pen_y_ref, src_ref, out_ref, pad_ref, u_ref, w_ref):
    n_out = src_ref.shape[0]
    padc = KERNEL // 4
    pad_ref[...] = jnp.full(pad_ref.shape, jnp.inf, jnp.float32)
    pad_ref[padc:padc + n_out] = src_ref[...]
    lane = lax.broadcasted_iota(jnp.int32, src_ref.shape[1:], 1)
    sub = lax.broadcasted_iota(jnp.int32, src_ref.shape[1:], 0)
    sub_z = (lane // 8) % 4
    sub_y = lane % 8

    lane3 = lax.broadcasted_iota(jnp.int32, (8,) + tuple(src_ref.shape[1:]), 2)
    sub_z3 = (lane3 // 8) % 4
    sub_y3 = lane3 % 8
    build_rotations(pad_ref, u_ref, 4, lambda r, here, after: jnp.where(
        sub_z3 + r < 4, pltpu.roll(here, 128 - 8 * r, 2), pltpu.roll(after, 32 - 8 * r, 2)))

    def q_range(g0, group):
        lo = max(0, padc - 1 - (g0 + group - 1))
        hi = padc + n_out - 1 - g0
        return lo, hi

    scan_offsets(u_ref, pen_z_ref, out_ref, n_out, 16, 4, q_range)

    def wbody(i, carry):
        a0 = pl.multiple_of(i * 8, 8)
        v = out_ref[pl.ds(a0, 8)]
        w_ref[0, pl.ds(a0, 8)] = v
        for r in range(1, 8):
            w_ref[r, pl.ds(a0, 8)] = jnp.where(sub_y3 + r < 8, pltpu.roll(v, 128 - r, 2),
                                               pltpu.roll(pltpu.roll(v, 8 - r, 2), 7, 1))
        return carry

    lax.fori_loop(0, n_out // 8, wbody, 0)
    group = 8
    shifts = []
    for db in range(-8, 8):
        for dy in range(8):
            carry_in = (sub_y + dy >= 8).astype(jnp.int32)
            row = sub + db + carry_in
            valid = (row >= 0) & (row <= 7)
            shifts.append((db, dy, valid))

    def ybody(i, carry):
        a0 = pl.multiple_of(i * group, group)
        acc = [jnp.full(src_ref.shape[1:], jnp.inf, jnp.float32) for _ in range(group)]
        for db, dy, valid in shifts:
            penvec = jnp.where(valid, pen_y_ref[8 * db + dy + 64], jnp.inf)
            for g in range(group):
                v = w_ref[dy, a0 + g]
                if db % 8:
                    v = pltpu.roll(v, (8 - db) % 8, 0)
                acc[g] = jnp.minimum(acc[g], v + penvec)
        for g in range(group):
            out_ref[a0 + g] = acc[g]
        return carry

    lax.fori_loop(0, n_out // group, ybody, 0)


def transpose_kernel_stages(forward, src_ref, out_ref, mid_ref, sems):
    n_gz, n_gy = lax.axis_size("gz"), lax.axis_size("gy")
    a, b = lax.axis_index("gz"), lax.axis_index("gy")
    barrier = pltpu.get_barrier_semaphore()

    def greet_gy(k, carry):
        pl.semaphore_signal(barrier, inc=1, device_id=(a, lax.rem(b + k, n_gy)), device_id_type=MESH)
        return carry

    def greet_gz(k, carry):
        pl.semaphore_signal(barrier, inc=1, device_id=(lax.rem(a + k, n_gz), b), device_id_type=MESH)
        return carry

    lax.fori_loop(1, n_gy, greet_gy, 0)
    lax.fori_loop(1, n_gz, greet_gz, 0)
    pl.semaphore_wait(barrier, n_gy - 1 + n_gz - 1)

    def stage_gy(src, dst, send_sem, recv_sem, own_sem):
        def send(k, carry):
            p = lax.rem(b + k, n_gy)
            pltpu.make_async_remote_copy(
                src_ref=src.at[:, pl.ds(p, 1)], dst_ref=dst.at[:, pl.ds(b, 1)], send_sem=send_sem,
                recv_sem=recv_sem, device_id=(a, p), device_id_type=MESH).start()
            return carry

        lax.fori_loop(1, n_gy, send, 0)
        own = pltpu.make_async_copy(src.at[:, pl.ds(b, 1)], dst.at[:, pl.ds(b, 1)], own_sem)
        own.start()
        own.wait()
        total = pltpu.make_async_remote_copy(
            src_ref=src.at[:, pl.ds(0, n_gy - 1)], dst_ref=dst.at[:, pl.ds(0, n_gy - 1)],
            send_sem=send_sem, recv_sem=recv_sem, device_id=(a, lax.rem(b + 1, n_gy)),
            device_id_type=MESH)
        total.wait_recv()
        total.wait_send()

    def stage_gz(src, dst, send_sem, recv_sem, own_sem):
        def send(k, carry):
            p = lax.rem(a + k, n_gz)
            pltpu.make_async_remote_copy(
                src_ref=src.at[pl.ds(p, 1)], dst_ref=dst.at[pl.ds(a, 1)], send_sem=send_sem,
                recv_sem=recv_sem, device_id=(p, b), device_id_type=MESH).start()
            return carry

        lax.fori_loop(1, n_gz, send, 0, unroll=4)
        own = pltpu.make_async_copy(src.at[pl.ds(a, 1)], dst.at[pl.ds(a, 1)], own_sem)
        own.start()
        own.wait()
        total = pltpu.make_async_remote_copy(
            src_ref=src.at[pl.ds(0, n_gz - 1)], dst_ref=dst.at[pl.ds(0, n_gz - 1)],
            send_sem=send_sem, recv_sem=recv_sem, device_id=(lax.rem(a + 1, n_gz), b),
            device_id_type=MESH)
        total.wait_recv()
        total.wait_send()

    if forward:
        stage_gy(src_ref, mid_ref, sems.at[0], sems.at[1], sems.at[2])
        stage_gz(mid_ref, out_ref, sems.at[3], sems.at[4], sems.at[5])
    else:
        stage_gz(src_ref, mid_ref, sems.at[0], sems.at[1], sems.at[2])
        stage_gy(mid_ref, out_ref, sems.at[3], sems.at[4], sems.at[5])


def exchange_rows(rows, forward, collective_id):
    vmem = pl.BlockSpec(memory_space=pltpu.VMEM)
    return pl.pallas_call(
        functools.partial(transpose_kernel_stages, forward),
        out_shape=jax.ShapeDtypeStruct(rows.shape, rows.dtype),
        in_specs=[vmem],
        out_specs=vmem,
        scratch_shapes=[pltpu.VMEM(rows.shape, rows.dtype), pltpu.SemaphoreType.DMA((6,))],
        compiler_params=pltpu.CompilerParams(collective_id=collective_id, has_side_effects=True),
    )(rows)


def regularize(current):
    levels, nz, ny, nx = current.shape
    lines = levels * nz * ny
    assert lines == 128 and nx % 8 == 0
    n_gz = lax.axis_size("gz")
    n_gy = lax.axis_size("gy")
    assert n_gz * n_gy == nx and ny == 8 and n_gy == 8
    xq = (KERNEL + 7) // 8
    nxo = nx // 8
    pen_x = penalty_table(8 * (xq * 2 + 2), KERNEL)
    xu = -(-(nxo + 2 * xq + 2) // 8) * 8
    t1 = local_call(xpass_kernel, (nxo, 8, lines), [(xu + 8, 8, lines), (8, xu, 8, lines)],
                    pen_x, current.reshape(lines, nx))
    r1 = exchange_rows(t1, True, 1)
    zq = KERNEL // 4
    pen_z = penalty_table(4 * (2 * zq + 2), KERNEL)
    zu = -(-(n_gz + 2 * zq + 2) // 8) * 8
    pen_y = penalty_table(8 * 2 * n_gy, 8 * n_gy)
    t2 = pl.pallas_call(
        zy_kernel,
        out_shape=jax.ShapeDtypeStruct(r1.shape, jnp.float32),
        in_specs=[pl.BlockSpec(memory_space=pltpu.SMEM)] * 2 + [pl.BlockSpec(memory_space=pltpu.VMEM)],
        out_specs=pl.BlockSpec(memory_space=pltpu.VMEM),
        scratch_shapes=[pltpu.VMEM((zu + 8, 8, lines), jnp.float32),
                        pltpu.VMEM((4, zu, 8, lines), jnp.float32),
                        pltpu.VMEM((8, n_gz, 8, lines), jnp.float32)],
    )(pen_z, pen_y, r1)
    r2 = exchange_rows(t2, False, 2).reshape(nx, lines)
    out = local_call(transpose_kernel, (lines, nx), [], r2)
    return out.reshape(current.shape)


def body(levels, ct_image, region_means):
    current = evolve_all(levels, ct_image, region_means)
    return (current, regularize(current))


def solution(mesh):
    return jax.shard_map(
        body,
        mesh=mesh,
        in_specs=(P(None, "gz", "gy", None), P("gz", "gy", None), P()),
        out_specs=(P(None, "gz", "gy", None), P(None, "gz", "gy", None)),
        check_vma=False,
    )
```

```python
import functools
import math

import jax
import jax.numpy as jnp
from jax import lax
from jax.experimental import pallas as pl
from jax.experimental.pallas import tpu as pltpu
from jax.sharding import PartitionSpec as P

LEVELS = 4
PHASES = 16
UPDATES = 2
KERNEL = 200


PENALTY = 0.0005
STEP_SIZE = 0.5


def arctan(x):
    ax = jnp.abs(x)
    big = ax > 2.414213562373095
    mid = ax > 0.4142135623730950
    z_big = -1.0 / jnp.where(big, ax, 1.0)
    z_mid = (ax - 1.0) / (ax + 1.0)
    z = jnp.where(big, z_big, jnp.where(mid, z_mid, ax))
    base = jnp.where(big, math.pi / 2, jnp.where(mid, math.pi / 4, 0.0))
    zz = z * z
    poly = (((8.05374449538e-2 * zz - 1.38776856032e-1) * zz + 1.99777106478e-1) * zz
            - 3.33329491539e-1) * zz * z + z
    r = base + poly
    return jnp.where(x < 0, -r, r)


def compute_step(means_ref, cur_ref, zlo_ref, zhi_ref, ylo_ref, yhi_ref, ct_ref, out_ref):
    nz, ny, nx = cur_ref.shape[1], cur_ref.shape[2], cur_ref.shape[3]
    shape = (ny, nx)
    xi = lax.broadcasted_iota(jnp.int32, shape, 1)
    yi = lax.broadcasted_iota(jnp.int32, shape, 0)
    xa = pltpu.roll(xi, 1, 1)
    xb = pltpu.roll(xi, nx - 1, 1)
    xa_ok = jnp.abs(xa - xi) == 1
    xb_ok = jnp.abs(xb - xi) == 1
    ya = pltpu.roll(yi, 1, 0)
    yb = pltpu.roll(yi, ny - 1, 0)
    ya_ok = jnp.abs(ya - yi) == 1
    yb_ok = jnp.abs(yb - yi) == 1
    low_row = yi == 0
    means = [means_ref[p] for p in range(PHASES)]
    for z in range(nz):
        picture = ct_ref[z]
        energy = []
        for p in range(PHASES):
            differ = picture - means[p]
            energy.append(differ * differ)
        phis, lap, g1, g0, dl = [], [], [], [], []
        for k in range(LEVELS):
            c = cur_ref[k, z]
            zm = zlo_ref[k] if z == 0 else cur_ref[k, z - 1]
            zp = zhi_ref[k] if z == nz - 1 else cur_ref[k, z + 1]
            edge = jnp.where(low_row, ylo_ref[k, z], yhi_ref[k, z])
            ym = jnp.where(ya_ok, pltpu.roll(c, 1, 0), edge)
            yp = jnp.where(yb_ok, pltpu.roll(c, ny - 1, 0), edge)
            xm = jnp.where(xa_ok, pltpu.roll(c, 1, 1), 0.0)
            xp = jnp.where(xb_ok, pltpu.roll(c, nx - 1, 1), 0.0)
            lap.append(zm + zp + ym + yp + xm + xp - 6.0 * c)
            h = 0.5 + arctan(c) / math.pi
            g1.append(h)
            g0.append(1.0 - h)
            dl.append(1.0 / (math.pi * (1.0 + c * c)))
            phis.append(c)
        g = (g0, g1)
        pair_lo = {(a, b): g[a][0] * g[b][1] for a in (0, 1) for b in (0, 1)}
        pair_hi = {(a, b): g[a][2] * g[b][3] for a in (0, 1) for b in (0, 1)}
        for k in range(LEVELS):
            force = None
            for q in range(PHASES // 2):
                low = q & ((1 << k) - 1)
                high = (q >> k) << (k + 1)
                p0 = high | low
                p1 = p0 | (1 << k)
                bits = [(p0 >> j) & 1 for j in range(LEVELS)]
                if k == 0:
                    prod = g[bits[1]][1] * pair_hi[(bits[2], bits[3])]
                elif k == 1:
                    prod = g[bits[0]][0] * pair_hi[(bits[2], bits[3])]
                elif k == 2:
                    prod = pair_lo[(bits[0], bits[1])] * g[bits[3]][3]
                else:
                    prod = pair_lo[(bits[0], bits[1])] * g[bits[2]][2]
                term = (energy[p1] - energy[p0]) * prod
                force = term if force is None else force + term
            out_ref[k, z] = phis[k] + STEP_SIZE * dl[k] * (lap[k] - force)


MESH = pl.DeviceIdType.MESH


def evolve_kernel(means_ref, cur_ref, ct_ref, out_ref, mid_ref, zlo_buf, zhi_buf, ylo_buf, yhi_buf,
                  send_sem, recv_sem):
    nz, ny = cur_ref.shape[1], cur_ref.shape[2]
    gz, gy = lax.axis_index("gz"), lax.axis_index("gy")
    n_gz, n_gy = lax.axis_size("gz"), lax.axis_size("gy")
    peers = [(gz > 0, (gz - 1, gy)), (gz < n_gz - 1, (gz + 1, gy)),
             (gy > 0, (gz, gy - 1)), (gy < n_gy - 1, (gz, gy + 1))]
    barrier = pltpu.get_barrier_semaphore()
    for present, dev in peers:
        @pl.when(present)
        def _(dev=dev):
            pl.semaphore_signal(barrier, inc=1, device_id=dev, device_id_type=MESH)
    count = sum(present.astype(jnp.int32) for present, _ in peers)
    pl.semaphore_wait(barrier, count)

    def exchange(step, src_ref):
        plan = [
            (gz < n_gz - 1, gz > 0, src_ref.at[:, nz - 1], zlo_buf.at[step], (gz + 1, gy)),
            (gz > 0, gz < n_gz - 1, src_ref.at[:, 0], zhi_buf.at[step], (gz - 1, gy)),
            (gy < n_gy - 1, gy > 0, src_ref.at[:, :, pl.ds(ny - 1, 1)], ylo_buf.at[step], (gz, gy + 1)),
            (gy > 0, gy < n_gy - 1, src_ref.at[:, :, pl.ds(0, 1)], yhi_buf.at[step], (gz, gy - 1)),
        ]
        copies = []
        for d, (sends, receives, src, dst, target) in enumerate(plan):
            copy = pltpu.make_async_remote_copy(
                src_ref=src, dst_ref=dst, send_sem=send_sem.at[step, d],
                recv_sem=recv_sem.at[step, d], device_id=target, device_id_type=MESH)

            @pl.when(sends)
            def _(copy=copy):
                copy.start()

            @pl.when(jnp.logical_not(receives))
            def _(dst=dst):
                dst[...] = jnp.zeros(dst.shape, jnp.float32)

            copies.append((sends, receives, copy))
        return copies

    def finish(copies):
        for sends, receives, copy in copies:
            @pl.when(receives)
            def _(copy=copy):
                copy.wait_recv()

    def drain(copies):
        for sends, receives, copy in copies:
            @pl.when(sends)
            def _(copy=copy):
                copy.wait_send()

    first = exchange(0, cur_ref)
    finish(first)
    compute_step(means_ref, cur_ref, zlo_buf.at[0], zhi_buf.at[0], ylo_buf.at[0], yhi_buf.at[0], ct_ref, mid_ref)
    drain(first)
    second = exchange(1, mid_ref)
    finish(second)
    compute_step(means_ref, mid_ref, zlo_buf.at[1], zhi_buf.at[1], ylo_buf.at[1], yhi_buf.at[1], ct_ref, out_ref)
    drain(second)


def evolve_all(current, picture, region_means):
    levels, nz, ny, nx = current.shape
    vmem = pl.BlockSpec(memory_space=pltpu.VMEM)
    f32 = jnp.float32
    return pl.pallas_call(
        evolve_kernel,
        out_shape=jax.ShapeDtypeStruct(current.shape, current.dtype),
        in_specs=[pl.BlockSpec(memory_space=pltpu.SMEM), vmem, vmem],
        out_specs=vmem,
        scratch_shapes=[
            pltpu.VMEM(current.shape, f32),
            pltpu.VMEM((2, levels, ny, nx), f32),
            pltpu.VMEM((2, levels, ny, nx), f32),
            pltpu.VMEM((2, levels, nz, 1, nx), f32),
            pltpu.VMEM((2, levels, nz, 1, nx), f32),
            pltpu.SemaphoreType.DMA((2, 4)),
            pltpu.SemaphoreType.DMA((2, 4)),
        ],
        compiler_params=pltpu.CompilerParams(collective_id=0, has_side_effects=True),
    )(region_means, current, picture)


def penalty_table(count, offset):
    distance = (jnp.arange(count, dtype=jnp.int32) - offset).astype(jnp.float32)
    return jnp.where(
        jnp.abs(distance) <= KERNEL, PENALTY * (distance * distance), jnp.inf
    ).astype(jnp.float32)


def scan_offsets(u_ref, pen_ref, out_ref, n_out, group, nrot, q_range):
    for g0 in range(0, n_out, group):
        q_lo, q_hi = q_range(g0, group)
        q_hi = min(q_hi, pen_ref.shape[0] // nrot - 1, u_ref.shape[1] - g0 - group)

        def body(q, acc, g0=g0):
            for r in range(nrot):
                vals = u_ref[r, pl.ds(g0 + q, group)]
                acc = jnp.minimum(acc, vals + pen_ref[q * nrot + r])
            return acc

        init = jnp.full((group,) + tuple(out_ref.shape[1:]), jnp.inf, jnp.float32)
        out_ref[g0:g0 + group] = lax.fori_loop(q_lo, q_hi + 1, body, init, unroll=2)


def build_rotations(pad_ref, u_ref, nrot, pick, chunk=8):
    def body(i, carry):
        b0 = pl.multiple_of(i * chunk, chunk)
        here = pad_ref[pl.ds(b0, chunk)]
        after = pad_ref[pl.ds(b0 + 1, chunk)]
        u_ref[0, pl.ds(b0, chunk)] = here
        for r in range(1, nrot):
            u_ref[r, pl.ds(b0, chunk)] = pick(r, here, after)
        return carry

    lax.fori_loop(0, u_ref.shape[1] // chunk, body, 0)


def xpass_kernel(pen_ref, src_ref, out_ref, pad_ref, u_ref):
    lines, nx = src_ref.shape
    reach = KERNEL
    padc = reach // 8
    pad_ref[...] = jnp.full(pad_ref.shape, jnp.inf, jnp.float32)
    pad_ref[padc:padc + nx // 8] = src_ref[...].T.reshape(nx // 8, 8, lines)
    sub = lax.broadcasted_iota(jnp.int32, (8, 8, lines), 1)
    build_rotations(pad_ref, u_ref, 8, lambda r, here, after: jnp.where(
        sub < 8 - r, pltpu.roll(here, 8 - r, 1), pltpu.roll(after, 8 - r, 1)))
    n_out = nx // 8

    def q_range(g0, group):
        lo = max(0, -((8 * (g0 + group - 1) + 14 - reach) // 8))
        hi = (reach + nx - 1 - 8 * g0) // 8
        return lo, hi

    scan_offsets(u_ref, pen_ref, out_ref, n_out, 16, 8, q_range)


def transpose_kernel(src_ref, out_ref):
    out_ref[...] = src_ref[...].T


def local_call(kernel, out_shape, scratch, *args):
    vmem = pl.BlockSpec(memory_space=pltpu.VMEM)
    smem = pl.BlockSpec(memory_space=pltpu.SMEM)
    specs = [smem if a.ndim == 1 else vmem for a in args]
    return pl.pallas_call(
        kernel,
        out_shape=jax.ShapeDtypeStruct(out_shape, jnp.float32),
        in_specs=specs,
        out_specs=vmem,
        scratch_shapes=[pltpu.VMEM(s, jnp.float32) for s in scratch],
    )(*args)


def zy_kernel(pen_z_ref, pen_y_ref, src_ref, out_ref, pad_ref, u_ref, w_ref):
    n_out = src_ref.shape[0]
    padc = KERNEL // 4
    pad_ref[...] = jnp.full(pad_ref.shape, jnp.inf, jnp.float32)
    pad_ref[padc:padc + n_out] = src_ref[...]
    lane = lax.broadcasted_iota(jnp.int32, src_ref.shape[1:], 1)
    sub = lax.broadcasted_iota(jnp.int32, src_ref.shape[1:], 0)
    sub_z = (lane // 8) % 4
    sub_y = lane % 8

    lane3 = lax.broadcasted_iota(jnp.int32, (8,) + tuple(src_ref.shape[1:]), 2)
    sub_z3 = (lane3 // 8) % 4
    sub_y3 = lane3 % 8
    build_rotations(pad_ref, u_ref, 4, lambda r, here, after: jnp.where(
        sub_z3 + r < 4, pltpu.roll(here, 128 - 8 * r, 2), pltpu.roll(after, 32 - 8 * r, 2)))

    def q_range(g0, group):
        lo = max(0, padc - 1 - (g0 + group - 1))
        hi = padc + n_out - 1 - g0
        return lo, hi

    scan_offsets(u_ref, pen_z_ref, out_ref, n_out, 16, 4, q_range)

    def wbody(i, carry):
        a0 = pl.multiple_of(i * 8, 8)
        v = out_ref[pl.ds(a0, 8)]
        w_ref[0, pl.ds(a0, 8)] = v
        for r in range(1, 8):
            w_ref[r, pl.ds(a0, 8)] = jnp.where(sub_y3 + r < 8, pltpu.roll(v, 128 - r, 2),
                                               pltpu.roll(pltpu.roll(v, 8 - r, 2), 7, 1))
        return carry

    lax.fori_loop(0, n_out // 8, wbody, 0)
    group = 8
    shifts = []
    for db in range(-8, 8):
        for dy in range(8):
            carry_in = (sub_y + dy >= 8).astype(jnp.int32)
            row = sub + db + carry_in
            valid = (row >= 0) & (row <= 7)
            shifts.append((db, dy, valid))

    def ybody(i, carry):
        a0 = pl.multiple_of(i * group, group)
        acc = [jnp.full(src_ref.shape[1:], jnp.inf, jnp.float32) for _ in range(group)]
        for db, dy, valid in shifts:
            penvec = jnp.where(valid, pen_y_ref[8 * db + dy + 64], jnp.inf)
            for g in range(group):
                v = w_ref[dy, a0 + g]
                if db % 8:
                    v = pltpu.roll(v, (8 - db) % 8, 0)
                acc[g] = jnp.minimum(acc[g], v + penvec)
        for g in range(group):
            out_ref[a0 + g] = acc[g]
        return carry

    lax.fori_loop(0, n_out // group, ybody, 0)


def global_transpose_kernel(src_ref, out_ref, mid_ref, blk_ref, recv_ref, sems):
    n_gz, n_gy = lax.axis_size("gz"), lax.axis_size("gy")
    a, b = lax.axis_index("gz"), lax.axis_index("gy")
    barrier = pltpu.get_barrier_semaphore()

    def greet_gy(k, carry):
        pl.semaphore_signal(barrier, inc=1, device_id=(a, lax.rem(b + k, n_gy)), device_id_type=MESH)
        return carry

    def greet_gz(k, carry):
        pl.semaphore_signal(barrier, inc=1, device_id=(lax.rem(a + k, n_gz), b), device_id_type=MESH)
        return carry

    lax.fori_loop(1, n_gy, greet_gy, 0)
    lax.fori_loop(1, n_gz, greet_gz, 0)
    pl.semaphore_wait(barrier, n_gy - 1 + n_gz - 1)

    def stage(src, dst, size, me, peers, target, send_sem, recv_sem, own_sem, unroll):
        def send(k, carry):
            p = lax.rem(me + k, peers)
            pltpu.make_async_remote_copy(
                src_ref=src.at[pl.ds(pl.multiple_of(p * size, 8), size)],
                dst_ref=dst.at[pl.ds(pl.multiple_of(me * size, 8), size)], send_sem=send_sem,
                recv_sem=recv_sem, device_id=target(p), device_id_type=MESH).start()
            return carry

        lax.fori_loop(1, peers, send, 0, unroll=unroll)
        own_rows = pl.ds(pl.multiple_of(me * size, 8), size)
        own = pltpu.make_async_copy(src.at[own_rows], dst.at[own_rows], own_sem)
        own.start()
        own.wait()
        rest = pl.ds(0, (peers - 1) * size)
        total = pltpu.make_async_remote_copy(
            src_ref=src.at[rest], dst_ref=dst.at[rest], send_sem=send_sem, recv_sem=recv_sem,
            device_id=target(lax.rem(me + 1, peers)), device_id_type=MESH)
        total.wait_recv()
        total.wait_send()

    stage(src_ref, mid_ref, n_gy, a, n_gz, lambda p: (p, b), sems.at[0], sems.at[1], sems.at[2], 4)
    for i in range(n_gy):
        blk_ref[i * n_gz:(i + 1) * n_gz] = mid_ref[pl.ds(i, n_gz, stride=n_gy)]
    stage(blk_ref, recv_ref, n_gz, b, n_gy, lambda p: (a, p), sems.at[3], sems.at[4], sems.at[5], 1)
    for j in range(n_gz):
        out_ref[j * n_gy:(j + 1) * n_gy] = recv_ref[pl.ds(j, n_gy, stride=n_gz)]


def exchange_rows(rows, collective_id):
    vmem = pl.BlockSpec(memory_space=pltpu.VMEM)
    return pl.pallas_call(
        global_transpose_kernel,
        out_shape=jax.ShapeDtypeStruct(rows.shape, rows.dtype),
        in_specs=[vmem],
        out_specs=vmem,
        scratch_shapes=[pltpu.VMEM(rows.shape, rows.dtype)] * 3 + [pltpu.SemaphoreType.DMA((6,))],
        compiler_params=pltpu.CompilerParams(collective_id=collective_id, has_side_effects=True),
    )(rows)


def regularize(current):
    levels, nz, ny, nx = current.shape
    lines = levels * nz * ny
    assert lines == 128 and nx % 8 == 0
    n_gz = lax.axis_size("gz")
    n_gy = lax.axis_size("gy")
    assert n_gz * n_gy == nx and ny == 8 and n_gy == 8
    xq = (KERNEL + 7) // 8
    nxo = nx // 8
    pen_x = penalty_table(8 * (xq * 2 + 2), KERNEL)
    xu = -(-(nxo + 2 * xq + 2) // 8) * 8
    t1 = local_call(xpass_kernel, (nxo, 8, lines), [(xu + 8, 8, lines), (8, xu, 8, lines)],
                    pen_x, current.reshape(lines, nx))
    r1 = exchange_rows(t1.reshape(nx, lines), 1).reshape(n_gz, n_gy, lines)
    zq = KERNEL // 4
    pen_z = penalty_table(4 * (2 * zq + 2), KERNEL)
    zu = -(-(n_gz + 2 * zq + 2) // 8) * 8
    pen_y = penalty_table(8 * 2 * n_gy, 8 * n_gy)
    t2 = pl.pallas_call(
        zy_kernel,
        out_shape=jax.ShapeDtypeStruct(r1.shape, jnp.float32),
        in_specs=[pl.BlockSpec(memory_space=pltpu.SMEM)] * 2 + [pl.BlockSpec(memory_space=pltpu.VMEM)],
        out_specs=pl.BlockSpec(memory_space=pltpu.VMEM),
        scratch_shapes=[pltpu.VMEM((zu + 8, 8, lines), jnp.float32),
                        pltpu.VMEM((4, zu, 8, lines), jnp.float32),
                        pltpu.VMEM((8, n_gz, 8, lines), jnp.float32)],
    )(pen_z, pen_y, r1)
    r2 = exchange_rows(t2.reshape(nx, lines), 2)
    out = local_call(transpose_kernel, (lines, nx), [], r2)
    return out.reshape(current.shape)


def body(levels, ct_image, region_means):
    current = evolve_all(levels, ct_image, region_means)
    return (current, regularize(current))


def solution(mesh):
    return jax.shard_map(
        body,
        mesh=mesh,
        in_specs=(P(None, "gz", "gy", None), P("gz", "gy", None), P()),
        out_specs=(P(None, "gz", "gy", None), P(None, "gz", "gy", None)),
        check_vma=False,
    )
```

```python
import functools
import math

import jax
import jax.numpy as jnp
from jax import lax
from jax.experimental import pallas as pl
from jax.experimental.pallas import tpu as pltpu
from jax.sharding import PartitionSpec as P

LEVELS = 4
PHASES = 16
UPDATES = 2
KERNEL = 200


PENALTY = 0.0005
STEP_SIZE = 0.5


def arctan(x):
    ax = jnp.abs(x)
    big = ax > 2.414213562373095
    mid = ax > 0.4142135623730950
    z_big = -1.0 / jnp.where(big, ax, 1.0)
    z_mid = (ax - 1.0) / (ax + 1.0)
    z = jnp.where(big, z_big, jnp.where(mid, z_mid, ax))
    base = jnp.where(big, math.pi / 2, jnp.where(mid, math.pi / 4, 0.0))
    zz = z * z
    poly = (((8.05374449538e-2 * zz - 1.38776856032e-1) * zz + 1.99777106478e-1) * zz
            - 3.33329491539e-1) * zz * z + z
    r = base + poly
    return jnp.where(x < 0, -r, r)


def compute_step(means_ref, cur_ref, zlo_ref, zhi_ref, ylo_ref, yhi_ref, ct_ref, out_ref):
    nz, ny, nx = cur_ref.shape[1], cur_ref.shape[2], cur_ref.shape[3]
    shape = (ny, nx)
    xi = lax.broadcasted_iota(jnp.int32, shape, 1)
    yi = lax.broadcasted_iota(jnp.int32, shape, 0)
    xa = pltpu.roll(xi, 1, 1)
    xb = pltpu.roll(xi, nx - 1, 1)
    xa_ok = jnp.abs(xa - xi) == 1
    xb_ok = jnp.abs(xb - xi) == 1
    ya = pltpu.roll(yi, 1, 0)
    yb = pltpu.roll(yi, ny - 1, 0)
    ya_ok = jnp.abs(ya - yi) == 1
    yb_ok = jnp.abs(yb - yi) == 1
    low_row = yi == 0
    means = [means_ref[p] for p in range(PHASES)]
    for z in range(nz):
        picture = ct_ref[z]
        energy = []
        for p in range(PHASES):
            differ = picture - means[p]
            energy.append(differ * differ)
        phis, lap, g1, g0, dl = [], [], [], [], []
        for k in range(LEVELS):
            c = cur_ref[k, z]
            zm = zlo_ref[k] if z == 0 else cur_ref[k, z - 1]
            zp = zhi_ref[k] if z == nz - 1 else cur_ref[k, z + 1]
            edge = jnp.where(low_row, ylo_ref[k, z], yhi_ref[k, z])
            ym = jnp.where(ya_ok, pltpu.roll(c, 1, 0), edge)
            yp = jnp.where(yb_ok, pltpu.roll(c, ny - 1, 0), edge)
            xm = jnp.where(xa_ok, pltpu.roll(c, 1, 1), 0.0)
            xp = jnp.where(xb_ok, pltpu.roll(c, nx - 1, 1), 0.0)
            lap.append(zm + zp + ym + yp + xm + xp - 6.0 * c)
            h = 0.5 + arctan(c) / math.pi
            g1.append(h)
            g0.append(1.0 - h)
            dl.append(1.0 / (math.pi * (1.0 + c * c)))
            phis.append(c)
        g = (g0, g1)
        pair_lo = {(a, b): g[a][0] * g[b][1] for a in (0, 1) for b in (0, 1)}
        pair_hi = {(a, b): g[a][2] * g[b][3] for a in (0, 1) for b in (0, 1)}
        for k in range(LEVELS):
            force = None
            for q in range(PHASES // 2):
                low = q & ((1 << k) - 1)
                high = (q >> k) << (k + 1)
                p0 = high | low
                p1 = p0 | (1 << k)
                bits = [(p0 >> j) & 1 for j in range(LEVELS)]
                if k == 0:
                    prod = g[bits[1]][1] * pair_hi[(bits[2], bits[3])]
                elif k == 1:
                    prod = g[bits[0]][0] * pair_hi[(bits[2], bits[3])]
                elif k == 2:
                    prod = pair_lo[(bits[0], bits[1])] * g[bits[3]][3]
                else:
                    prod = pair_lo[(bits[0], bits[1])] * g[bits[2]][2]
                term = (energy[p1] - energy[p0]) * prod
                force = term if force is None else force + term
            out_ref[k, z] = phis[k] + STEP_SIZE * dl[k] * (lap[k] - force)


MESH = pl.DeviceIdType.MESH


def evolve_kernel(means_ref, cur_ref, ct_ref, out_ref, mid_ref, zlo_buf, zhi_buf, ylo_buf, yhi_buf,
                  send_sem, recv_sem):
    nz, ny = cur_ref.shape[1], cur_ref.shape[2]
    gz, gy = lax.axis_index("gz"), lax.axis_index("gy")
    n_gz, n_gy = lax.axis_size("gz"), lax.axis_size("gy")
    peers = [(gz > 0, (gz - 1, gy)), (gz < n_gz - 1, (gz + 1, gy)),
             (gy > 0, (gz, gy - 1)), (gy < n_gy - 1, (gz, gy + 1))]
    barrier = pltpu.get_barrier_semaphore()
    for present, dev in peers:
        @pl.when(present)
        def _(dev=dev):
            pl.semaphore_signal(barrier, inc=1, device_id=dev, device_id_type=MESH)
    count = sum(present.astype(jnp.int32) for present, _ in peers)
    pl.semaphore_wait(barrier, count)

    def exchange(step, src_ref):
        plan = [
            (gz < n_gz - 1, gz > 0, src_ref.at[:, nz - 1], zlo_buf.at[step], (gz + 1, gy)),
            (gz > 0, gz < n_gz - 1, src_ref.at[:, 0], zhi_buf.at[step], (gz - 1, gy)),
            (gy < n_gy - 1, gy > 0, src_ref.at[:, :, pl.ds(ny - 1, 1)], ylo_buf.at[step], (gz, gy + 1)),
            (gy > 0, gy < n_gy - 1, src_ref.at[:, :, pl.ds(0, 1)], yhi_buf.at[step], (gz, gy - 1)),
        ]
        copies = []
        for d, (sends, receives, src, dst, target) in enumerate(plan):
            copy = pltpu.make_async_remote_copy(
                src_ref=src, dst_ref=dst, send_sem=send_sem.at[step, d],
                recv_sem=recv_sem.at[step, d], device_id=target, device_id_type=MESH)

            @pl.when(sends)
            def _(copy=copy):
                copy.start()

            @pl.when(jnp.logical_not(receives))
            def _(dst=dst):
                dst[...] = jnp.zeros(dst.shape, jnp.float32)

            copies.append((sends, receives, copy))
        return copies

    def finish(copies):
        for sends, receives, copy in copies:
            @pl.when(receives)
            def _(copy=copy):
                copy.wait_recv()

    def drain(copies):
        for sends, receives, copy in copies:
            @pl.when(sends)
            def _(copy=copy):
                copy.wait_send()

    first = exchange(0, cur_ref)
    finish(first)
    compute_step(means_ref, cur_ref, zlo_buf.at[0], zhi_buf.at[0], ylo_buf.at[0], yhi_buf.at[0], ct_ref, mid_ref)
    drain(first)
    second = exchange(1, mid_ref)
    finish(second)
    compute_step(means_ref, mid_ref, zlo_buf.at[1], zhi_buf.at[1], ylo_buf.at[1], yhi_buf.at[1], ct_ref, out_ref)
    drain(second)


def evolve_all(current, picture, region_means):
    levels, nz, ny, nx = current.shape
    vmem = pl.BlockSpec(memory_space=pltpu.VMEM)
    f32 = jnp.float32
    return pl.pallas_call(
        evolve_kernel,
        out_shape=jax.ShapeDtypeStruct(current.shape, current.dtype),
        in_specs=[pl.BlockSpec(memory_space=pltpu.SMEM), vmem, vmem],
        out_specs=vmem,
        scratch_shapes=[
            pltpu.VMEM(current.shape, f32),
            pltpu.VMEM((2, levels, ny, nx), f32),
            pltpu.VMEM((2, levels, ny, nx), f32),
            pltpu.VMEM((2, levels, nz, 1, nx), f32),
            pltpu.VMEM((2, levels, nz, 1, nx), f32),
            pltpu.SemaphoreType.DMA((2, 4)),
            pltpu.SemaphoreType.DMA((2, 4)),
        ],
        compiler_params=pltpu.CompilerParams(collective_id=0, has_side_effects=True),
    )(region_means, current, picture)


def penalty_table(count, offset):
    distance = (jnp.arange(count, dtype=jnp.int32) - offset).astype(jnp.float32)
    return jnp.where(
        jnp.abs(distance) <= KERNEL, PENALTY * (distance * distance), jnp.inf
    ).astype(jnp.float32)


def scan_offsets(u_ref, pen_ref, out_ref, n_out, group, nrot, q_range, after_group=None):
    for g0 in range(0, n_out, group):
        q_lo, q_hi = q_range(g0, group)
        q_hi = min(q_hi, pen_ref.shape[0] // nrot - 1, u_ref.shape[1] - g0 - group)

        def body(q, acc, g0=g0):
            for r in range(nrot):
                vals = u_ref[r, pl.ds(g0 + q, group)]
                acc = jnp.minimum(acc, vals + pen_ref[q * nrot + r])
            return acc

        init = jnp.full((group,) + tuple(out_ref.shape[1:]), jnp.inf, jnp.float32)
        out_ref[g0:g0 + group] = lax.fori_loop(q_lo, q_hi + 1, body, init, unroll=2)
        if after_group is not None:
            after_group(g0, group)


def build_rotations(pad_ref, u_ref, nrot, pick, chunk=8):
    def body(i, carry):
        b0 = pl.multiple_of(i * chunk, chunk)
        here = pad_ref[pl.ds(b0, chunk)]
        after = pad_ref[pl.ds(b0 + 1, chunk)]
        u_ref[0, pl.ds(b0, chunk)] = here
        for r in range(1, nrot):
            u_ref[r, pl.ds(b0, chunk)] = pick(r, here, after)
        return carry

    lax.fori_loop(0, u_ref.shape[1] // chunk, body, 0)


def xpass_kernel(pen_ref, src_ref, out_ref, pad_ref, u_ref, after_group=None):
    lines, nx = src_ref.shape
    reach = KERNEL
    padc = reach // 8
    pad_ref[...] = jnp.full(pad_ref.shape, jnp.inf, jnp.float32)
    pad_ref[padc:padc + nx // 8] = src_ref[...].T.reshape(nx // 8, 8, lines)
    sub = lax.broadcasted_iota(jnp.int32, (8, 8, lines), 1)
    build_rotations(pad_ref, u_ref, 8, lambda r, here, after: jnp.where(
        sub < 8 - r, pltpu.roll(here, 8 - r, 1), pltpu.roll(after, 8 - r, 1)))
    n_out = nx // 8

    def q_range(g0, group):
        lo = max(0, -((8 * (g0 + group - 1) + 14 - reach) // 8))
        hi = (reach + nx - 1 - 8 * g0) // 8
        return lo, hi

    scan_offsets(u_ref, pen_ref, out_ref, n_out, 16, 8, q_range, after_group)


def transpose_kernel(src_ref, out_ref):
    out_ref[...] = src_ref[...].T


def local_call(kernel, out_shape, scratch, *args):
    vmem = pl.BlockSpec(memory_space=pltpu.VMEM)
    smem = pl.BlockSpec(memory_space=pltpu.SMEM)
    specs = [smem if a.ndim == 1 else vmem for a in args]
    return pl.pallas_call(
        kernel,
        out_shape=jax.ShapeDtypeStruct(out_shape, jnp.float32),
        in_specs=specs,
        out_specs=vmem,
        scratch_shapes=[pltpu.VMEM(s, jnp.float32) for s in scratch],
    )(*args)


def zy_kernel(pen_z_ref, pen_y_ref, src_ref, out_ref, pad_ref, u_ref, w_ref, before_y=None, after_group=None):
    n_out = src_ref.shape[0]
    padc = KERNEL // 4
    pad_ref[...] = jnp.full(pad_ref.shape, jnp.inf, jnp.float32)
    pad_ref[padc:padc + n_out] = src_ref[...]
    lane = lax.broadcasted_iota(jnp.int32, src_ref.shape[1:], 1)
    sub = lax.broadcasted_iota(jnp.int32, src_ref.shape[1:], 0)
    sub_z = (lane // 8) % 4
    sub_y = lane % 8

    lane3 = lax.broadcasted_iota(jnp.int32, (8,) + tuple(src_ref.shape[1:]), 2)
    sub_z3 = (lane3 // 8) % 4
    sub_y3 = lane3 % 8
    build_rotations(pad_ref, u_ref, 4, lambda r, here, after: jnp.where(
        sub_z3 + r < 4, pltpu.roll(here, 128 - 8 * r, 2), pltpu.roll(after, 32 - 8 * r, 2)))

    def q_range(g0, group):
        lo = max(0, padc - 1 - (g0 + group - 1))
        hi = padc + n_out - 1 - g0
        return lo, hi

    scan_offsets(u_ref, pen_z_ref, out_ref, n_out, 16, 4, q_range)

    def wbody(i, carry):
        a0 = pl.multiple_of(i * 8, 8)
        v = out_ref[pl.ds(a0, 8)]
        w_ref[0, pl.ds(a0, 8)] = v
        for r in range(1, 8):
            w_ref[r, pl.ds(a0, 8)] = jnp.where(sub_y3 + r < 8, pltpu.roll(v, 128 - r, 2),
                                               pltpu.roll(pltpu.roll(v, 8 - r, 2), 7, 1))
        return carry

    lax.fori_loop(0, n_out // 8, wbody, 0)
    if before_y is not None:
        before_y()
    group = 8
    shifts = []
    for db in range(-8, 8):
        for dy in range(8):
            carry_in = (sub_y + dy >= 8).astype(jnp.int32)
            row = sub + db + carry_in
            valid = (row >= 0) & (row <= 7)
            shifts.append((db, dy, valid))

    def ybody(i, carry):
        a0 = pl.multiple_of(i * group, group)
        acc = [jnp.full(src_ref.shape[1:], jnp.inf, jnp.float32) for _ in range(group)]
        for db, dy, valid in shifts:
            penvec = jnp.where(valid, pen_y_ref[8 * db + dy + 64], jnp.inf)
            for g in range(group):
                v = w_ref[dy, a0 + g]
                if db % 8:
                    v = pltpu.roll(v, (8 - db) % 8, 0)
                acc[g] = jnp.minimum(acc[g], v + penvec)
        for g in range(group):
            out_ref[a0 + g] = acc[g]
        if after_group is not None:
            after_group(a0, group)
        return carry

    lax.fori_loop(0, n_out // group, ybody, 0)


class Exchange:
    def __init__(self, mid_ref, blk_ref, recv_ref, sems):
        self.n_gz, self.n_gy = lax.axis_size("gz"), lax.axis_size("gy")
        self.a, self.b = lax.axis_index("gz"), lax.axis_index("gy")
        self.mid_ref, self.blk_ref, self.recv_ref, self.sems = mid_ref, blk_ref, recv_ref, sems
        self.barrier = pltpu.get_barrier_semaphore()

    def greet(self):
        a, b, n_gz, n_gy = self.a, self.b, self.n_gz, self.n_gy

        def greet_gy(k, carry):
            pl.semaphore_signal(self.barrier, inc=1, device_id=(a, lax.rem(b + k, n_gy)),
                                device_id_type=MESH)
            return carry

        def greet_gz(k, carry):
            pl.semaphore_signal(self.barrier, inc=1, device_id=(lax.rem(a + k, n_gz), b),
                                device_id_type=MESH)
            return carry

        lax.fori_loop(1, n_gy, greet_gy, 0)
        lax.fori_loop(1, n_gz, greet_gz, 0)

    def wait_greetings(self):
        pl.semaphore_wait(self.barrier, self.n_gy - 1 + self.n_gz - 1)

    def tile_copy(self, tiles_ref, p):
        rows = pl.ds(pl.multiple_of(self.a * self.n_gy, 8), self.n_gy)
        return pltpu.make_async_remote_copy(
            src_ref=tiles_ref.at[p], dst_ref=self.mid_ref.at[rows], send_sem=self.sems.at[0],
            recv_sem=self.sems.at[1], device_id=(p, self.b), device_id_type=MESH)

    def send_tile(self, tiles_ref, p):
        @pl.when(p != self.a)
        def _():
            self.tile_copy(tiles_ref, p).start()

    def finish(self, tiles_ref, out_ref):
        a, b, n_gz, n_gy = self.a, self.b, self.n_gz, self.n_gy
        mid_ref, blk_ref, recv_ref, sems = self.mid_ref, self.blk_ref, self.recv_ref, self.sems
        own_rows = pl.ds(pl.multiple_of(a * n_gy, 8), n_gy)
        own = pltpu.make_async_copy(tiles_ref.at[a], mid_ref.at[own_rows], sems.at[2])
        own.start()
        own.wait()
        rest = pl.ds(0, (n_gz - 1) * n_gy)
        total = pltpu.make_async_remote_copy(
            src_ref=mid_ref.at[rest], dst_ref=mid_ref.at[rest], send_sem=sems.at[0],
            recv_sem=sems.at[1], device_id=(lax.rem(a + 1, n_gz), b), device_id_type=MESH)
        total.wait_recv()
        total.wait_send()
        for i in range(n_gy):
            blk_ref[i * n_gz:(i + 1) * n_gz] = mid_ref[pl.ds(i, n_gz, stride=n_gy)]

        def send(k, carry):
            p = lax.rem(b + k, n_gy)
            pltpu.make_async_remote_copy(
                src_ref=blk_ref.at[pl.ds(pl.multiple_of(p * n_gz, 8), n_gz)],
                dst_ref=recv_ref.at[pl.ds(pl.multiple_of(b * n_gz, 8), n_gz)], send_sem=sems.at[3],
                recv_sem=sems.at[4], device_id=(a, p), device_id_type=MESH).start()
            return carry

        lax.fori_loop(1, n_gy, send, 0)
        block = pl.ds(pl.multiple_of(b * n_gz, 8), n_gz)
        own = pltpu.make_async_copy(blk_ref.at[block], recv_ref.at[block], sems.at[5])
        own.start()
        own.wait()
        rest = pl.ds(0, (n_gy - 1) * n_gz)
        total = pltpu.make_async_remote_copy(
            src_ref=blk_ref.at[rest], dst_ref=recv_ref.at[rest], send_sem=sems.at[3],
            recv_sem=sems.at[4], device_id=(a, lax.rem(b + 1, n_gy)), device_id_type=MESH)
        total.wait_recv()
        total.wait_send()
        for j in range(n_gz):
            out_ref[j * n_gy:(j + 1) * n_gy] = recv_ref[pl.ds(j, n_gy, stride=n_gz)]


def exchange_scratch(tiles_shape):
    rows = (tiles_shape[0] * tiles_shape[1], tiles_shape[2])
    return [pltpu.VMEM(tiles_shape, jnp.float32)] + [pltpu.VMEM(rows, jnp.float32)] * 3 + [
        pltpu.SemaphoreType.DMA((6,))]


def xpass_send_kernel(pen_ref, src_ref, out_ref, pad_ref, u_ref, tiles_ref, mid_ref, blk_ref, recv_ref, sems):
    ex = Exchange(mid_ref, blk_ref, recv_ref, sems)
    ex.greet()

    def after_group(g0, group):
        if g0 == 0:
            ex.wait_greetings()
        for t in range(g0, g0 + group):
            ex.send_tile(tiles_ref, t)

    xpass_kernel(pen_ref, src_ref, tiles_ref, pad_ref, u_ref, after_group)
    ex.finish(tiles_ref, out_ref)


def zy_send_kernel(pen_z_ref, pen_y_ref, src_ref, out_ref, pad_ref, u_ref, w_ref, tiles_ref, mid_ref,
                   blk_ref, recv_ref, sems):
    ex = Exchange(mid_ref, blk_ref, recv_ref, sems)
    ex.greet()

    def after_group(a0, group):
        for g in range(group):
            ex.send_tile(tiles_ref, a0 + g)

    zy_kernel(pen_z_ref, pen_y_ref, src_ref, tiles_ref, pad_ref, u_ref, w_ref, ex.wait_greetings, after_group)
    ex.finish(tiles_ref, out_ref)


def regularize(current):
    levels, nz, ny, nx = current.shape
    lines = levels * nz * ny
    n_gz = lax.axis_size("gz")
    n_gy = lax.axis_size("gy")
    assert lines == 128 and ny == 8 and n_gy == 8 and n_gz * n_gy == nx
    smem = pl.BlockSpec(memory_space=pltpu.SMEM)
    vmem = pl.BlockSpec(memory_space=pltpu.VMEM)
    tiles = (n_gz, n_gy, lines)
    xq = (KERNEL + 7) // 8
    nxo = nx // 8
    pen_x = penalty_table(8 * (xq * 2 + 2), KERNEL)
    xu = -(-(nxo + 2 * xq + 2) // 8) * 8
    r1 = pl.pallas_call(
        xpass_send_kernel,
        out_shape=jax.ShapeDtypeStruct((nx, lines), jnp.float32),
        in_specs=[smem, vmem],
        out_specs=vmem,
        scratch_shapes=[pltpu.VMEM((xu + 8, 8, lines), jnp.float32),
                        pltpu.VMEM((8, xu, 8, lines), jnp.float32)] + exchange_scratch(tiles),
        compiler_params=pltpu.CompilerParams(collective_id=1, has_side_effects=True),
    )(pen_x, current.reshape(lines, nx))
    zq = KERNEL // 4
    pen_z = penalty_table(4 * (2 * zq + 2), KERNEL)
    zu = -(-(n_gz + 2 * zq + 2) // 8) * 8
    pen_y = penalty_table(8 * 2 * n_gy, 8 * n_gy)
    r2 = pl.pallas_call(
        zy_send_kernel,
        out_shape=jax.ShapeDtypeStruct((nx, lines), jnp.float32),
        in_specs=[smem, smem, vmem],
        out_specs=vmem,
        scratch_shapes=[pltpu.VMEM((zu + 8, 8, lines), jnp.float32),
                        pltpu.VMEM((4, zu, 8, lines), jnp.float32),
                        pltpu.VMEM((8, n_gz, 8, lines), jnp.float32)] + exchange_scratch(tiles),
        compiler_params=pltpu.CompilerParams(collective_id=2, has_side_effects=True),
    )(pen_z, pen_y, r1.reshape(tiles))
    out = local_call(transpose_kernel, (lines, nx), [], r2)
    return out.reshape(current.shape)


def body(levels, ct_image, region_means):
    current = evolve_all(levels, ct_image, region_means)
    return (current, regularize(current))


def solution(mesh):
    return jax.shard_map(
        body,
        mesh=mesh,
        in_specs=(P(None, "gz", "gy", None), P("gz", "gy", None), P()),
        out_specs=(P(None, "gz", "gy", None), P(None, "gz", "gy", None)),
        check_vma=False,
    )
```

```python
import functools
import math

import jax
import jax.numpy as jnp
from jax import lax
from jax.experimental import pallas as pl
from jax.experimental.pallas import tpu as pltpu
from jax.sharding import PartitionSpec as P

LEVELS = 4
PHASES = 16
UPDATES = 2
KERNEL = 200


PENALTY = 0.0005
STEP_SIZE = 0.5


def arctan(x):
    ax = jnp.abs(x)
    big = ax > 2.414213562373095
    mid = ax > 0.4142135623730950
    z_big = -1.0 / jnp.where(big, ax, 1.0)
    z_mid = (ax - 1.0) / (ax + 1.0)
    z = jnp.where(big, z_big, jnp.where(mid, z_mid, ax))
    base = jnp.where(big, math.pi / 2, jnp.where(mid, math.pi / 4, 0.0))
    zz = z * z
    poly = (((8.05374449538e-2 * zz - 1.38776856032e-1) * zz + 1.99777106478e-1) * zz
            - 3.33329491539e-1) * zz * z + z
    r = base + poly
    return jnp.where(x < 0, -r, r)


def compute_step(means_ref, cur_ref, zlo_ref, zhi_ref, ylo_ref, yhi_ref, ct_ref, out_ref):
    nz, ny, nx = cur_ref.shape[1], cur_ref.shape[2], cur_ref.shape[3]
    shape = (ny, nx)
    xi = lax.broadcasted_iota(jnp.int32, shape, 1)
    yi = lax.broadcasted_iota(jnp.int32, shape, 0)
    xa = pltpu.roll(xi, 1, 1)
    xb = pltpu.roll(xi, nx - 1, 1)
    xa_ok = jnp.abs(xa - xi) == 1
    xb_ok = jnp.abs(xb - xi) == 1
    ya = pltpu.roll(yi, 1, 0)
    yb = pltpu.roll(yi, ny - 1, 0)
    ya_ok = jnp.abs(ya - yi) == 1
    yb_ok = jnp.abs(yb - yi) == 1
    low_row = yi == 0
    means = [means_ref[p] for p in range(PHASES)]
    for z in range(nz):
        picture = ct_ref[z]
        energy = []
        for p in range(PHASES):
            differ = picture - means[p]
            energy.append(differ * differ)
        phis, lap, g1, g0, dl = [], [], [], [], []
        for k in range(LEVELS):
            c = cur_ref[k, z]
            zm = zlo_ref[k] if z == 0 else cur_ref[k, z - 1]
            zp = zhi_ref[k] if z == nz - 1 else cur_ref[k, z + 1]
            edge = jnp.where(low_row, ylo_ref[k, z], yhi_ref[k, z])
            ym = jnp.where(ya_ok, pltpu.roll(c, 1, 0), edge)
            yp = jnp.where(yb_ok, pltpu.roll(c, ny - 1, 0), edge)
            xm = jnp.where(xa_ok, pltpu.roll(c, 1, 1), 0.0)
            xp = jnp.where(xb_ok, pltpu.roll(c, nx - 1, 1), 0.0)
            lap.append(zm + zp + ym + yp + xm + xp - 6.0 * c)
            h = 0.5 + arctan(c) / math.pi
            g1.append(h)
            g0.append(1.0 - h)
            dl.append(1.0 / (math.pi * (1.0 + c * c)))
            phis.append(c)
        g = (g0, g1)
        pair_lo = {(a, b): g[a][0] * g[b][1] for a in (0, 1) for b in (0, 1)}
        pair_hi = {(a, b): g[a][2] * g[b][3] for a in (0, 1) for b in (0, 1)}
        for k in range(LEVELS):
            force = None
            for q in range(PHASES // 2):
                low = q & ((1 << k) - 1)
                high = (q >> k) << (k + 1)
                p0 = high | low
                p1 = p0 | (1 << k)
                bits = [(p0 >> j) & 1 for j in range(LEVELS)]
                if k == 0:
                    prod = g[bits[1]][1] * pair_hi[(bits[2], bits[3])]
                elif k == 1:
                    prod = g[bits[0]][0] * pair_hi[(bits[2], bits[3])]
                elif k == 2:
                    prod = pair_lo[(bits[0], bits[1])] * g[bits[3]][3]
                else:
                    prod = pair_lo[(bits[0], bits[1])] * g[bits[2]][2]
                term = (energy[p1] - energy[p0]) * prod
                force = term if force is None else force + term
            out_ref[k, z] = phis[k] + STEP_SIZE * dl[k] * (lap[k] - force)


MESH = pl.DeviceIdType.MESH


def evolve_kernel(means_ref, cur_ref, ct_ref, out_ref, mid_ref, zlo_buf, zhi_buf, ylo_buf, yhi_buf,
                  send_sem, recv_sem):
    nz, ny = cur_ref.shape[1], cur_ref.shape[2]
    gz, gy = lax.axis_index("gz"), lax.axis_index("gy")
    n_gz, n_gy = lax.axis_size("gz"), lax.axis_size("gy")
    peers = [(gz > 0, (gz - 1, gy)), (gz < n_gz - 1, (gz + 1, gy)),
             (gy > 0, (gz, gy - 1)), (gy < n_gy - 1, (gz, gy + 1))]
    barrier = pltpu.get_barrier_semaphore()
    for present, dev in peers:
        @pl.when(present)
        def _(dev=dev):
            pl.semaphore_signal(barrier, inc=1, device_id=dev, device_id_type=MESH)
    count = sum(present.astype(jnp.int32) for present, _ in peers)
    pl.semaphore_wait(barrier, count)

    def exchange(step, src_ref):
        plan = [
            (gz < n_gz - 1, gz > 0, src_ref.at[:, nz - 1], zlo_buf.at[step], (gz + 1, gy)),
            (gz > 0, gz < n_gz - 1, src_ref.at[:, 0], zhi_buf.at[step], (gz - 1, gy)),
            (gy < n_gy - 1, gy > 0, src_ref.at[:, :, pl.ds(ny - 1, 1)], ylo_buf.at[step], (gz, gy + 1)),
            (gy > 0, gy < n_gy - 1, src_ref.at[:, :, pl.ds(0, 1)], yhi_buf.at[step], (gz, gy - 1)),
        ]
        copies = []
        for d, (sends, receives, src, dst, target) in enumerate(plan):
            copy = pltpu.make_async_remote_copy(
                src_ref=src, dst_ref=dst, send_sem=send_sem.at[step, d],
                recv_sem=recv_sem.at[step, d], device_id=target, device_id_type=MESH)

            @pl.when(sends)
            def _(copy=copy):
                copy.start()

            @pl.when(jnp.logical_not(receives))
            def _(dst=dst):
                dst[...] = jnp.zeros(dst.shape, jnp.float32)

            copies.append((sends, receives, copy))
        return copies

    def finish(copies):
        for sends, receives, copy in copies:
            @pl.when(receives)
            def _(copy=copy):
                copy.wait_recv()

    def drain(copies):
        for sends, receives, copy in copies:
            @pl.when(sends)
            def _(copy=copy):
                copy.wait_send()

    first = exchange(0, cur_ref)
    finish(first)
    compute_step(means_ref, cur_ref, zlo_buf.at[0], zhi_buf.at[0], ylo_buf.at[0], yhi_buf.at[0], ct_ref, mid_ref)
    drain(first)
    second = exchange(1, mid_ref)
    finish(second)
    compute_step(means_ref, mid_ref, zlo_buf.at[1], zhi_buf.at[1], ylo_buf.at[1], yhi_buf.at[1], ct_ref, out_ref)
    drain(second)


def evolve_all(current, picture, region_means):
    levels, nz, ny, nx = current.shape
    vmem = pl.BlockSpec(memory_space=pltpu.VMEM)
    f32 = jnp.float32
    return pl.pallas_call(
        evolve_kernel,
        out_shape=jax.ShapeDtypeStruct(current.shape, current.dtype),
        in_specs=[pl.BlockSpec(memory_space=pltpu.SMEM), vmem, vmem],
        out_specs=vmem,
        scratch_shapes=[
            pltpu.VMEM(current.shape, f32),
            pltpu.VMEM((2, levels, ny, nx), f32),
            pltpu.VMEM((2, levels, ny, nx), f32),
            pltpu.VMEM((2, levels, nz, 1, nx), f32),
            pltpu.VMEM((2, levels, nz, 1, nx), f32),
            pltpu.SemaphoreType.DMA((2, 4)),
            pltpu.SemaphoreType.DMA((2, 4)),
        ],
        compiler_params=pltpu.CompilerParams(collective_id=0, has_side_effects=True),
    )(region_means, current, picture)


def penalty_table(count, offset):
    distance = (jnp.arange(count, dtype=jnp.int32) - offset).astype(jnp.float32)
    return jnp.where(
        jnp.abs(distance) <= KERNEL, PENALTY * (distance * distance), jnp.inf
    ).astype(jnp.float32)


def scan_offsets(u_ref, pen_ref, out_ref, n_out, group, nrot, q_range, after_group=None):
    for g0 in range(0, n_out, group):
        q_lo, q_hi = q_range(g0, group)
        q_hi = min(q_hi, pen_ref.shape[0] // nrot - 1, u_ref.shape[1] - g0 - group)

        def body(q, acc, g0=g0):
            for r in range(nrot):
                vals = u_ref[r, pl.ds(g0 + q, group)]
                acc = jnp.minimum(acc, vals + pen_ref[q * nrot + r])
            return acc

        init = jnp.full((group,) + tuple(out_ref.shape[1:]), jnp.inf, jnp.float32)
        out_ref[g0:g0 + group] = lax.fori_loop(q_lo, q_hi + 1, body, init, unroll=2)
        if after_group is not None:
            after_group(g0, group)


def build_rotations(pad_ref, u_ref, nrot, pick, chunk=8):
    def body(i, carry):
        b0 = pl.multiple_of(i * chunk, chunk)
        here = pad_ref[pl.ds(b0, chunk)]
        after = pad_ref[pl.ds(b0 + 1, chunk)]
        u_ref[0, pl.ds(b0, chunk)] = here
        for r in range(1, nrot):
            u_ref[r, pl.ds(b0, chunk)] = pick(r, here, after)
        return carry

    lax.fori_loop(0, u_ref.shape[1] // chunk, body, 0)


def xpass_kernel(pen_ref, src_ref, out_ref, pad_ref, u_ref, after_group=None):
    lines, nx = src_ref.shape
    reach = KERNEL
    padc = reach // 8
    pad_ref[...] = jnp.full(pad_ref.shape, jnp.inf, jnp.float32)
    pad_ref[padc:padc + nx // 8] = src_ref[...].T.reshape(nx // 8, 8, lines)
    sub = lax.broadcasted_iota(jnp.int32, (8, 8, lines), 1)
    build_rotations(pad_ref, u_ref, 8, lambda r, here, after: jnp.where(
        sub < 8 - r, pltpu.roll(here, 8 - r, 1), pltpu.roll(after, 8 - r, 1)))
    n_out = nx // 8

    def q_range(g0, group):
        lo = max(0, -((8 * (g0 + group - 1) + 14 - reach) // 8))
        hi = (reach + nx - 1 - 8 * g0) // 8
        return lo, hi

    scan_offsets(u_ref, pen_ref, out_ref, n_out, 16, 8, q_range, after_group)


def transpose_kernel(src_ref, out_ref):
    out_ref[...] = src_ref[...].T


def local_call(kernel, out_shape, scratch, *args):
    vmem = pl.BlockSpec(memory_space=pltpu.VMEM)
    smem = pl.BlockSpec(memory_space=pltpu.SMEM)
    specs = [smem if a.ndim == 1 else vmem for a in args]
    return pl.pallas_call(
        kernel,
        out_shape=jax.ShapeDtypeStruct(out_shape, jnp.float32),
        in_specs=specs,
        out_specs=vmem,
        scratch_shapes=[pltpu.VMEM(s, jnp.float32) for s in scratch],
    )(*args)


def zy_kernel(pen_z_ref, pen_y_ref, src_ref, out_ref, pad_ref, u_ref, w_ref, before_y=None, after_group=None):
    n_out = src_ref.shape[0]
    padc = KERNEL // 4
    pad_ref[...] = jnp.full(pad_ref.shape, jnp.inf, jnp.float32)
    pad_ref[padc:padc + n_out] = src_ref[...]
    lane = lax.broadcasted_iota(jnp.int32, src_ref.shape[1:], 1)
    sub = lax.broadcasted_iota(jnp.int32, src_ref.shape[1:], 0)
    sub_z = (lane // 8) % 4
    sub_y = lane % 8

    lane3 = lax.broadcasted_iota(jnp.int32, (8,) + tuple(src_ref.shape[1:]), 2)
    sub_z3 = (lane3 // 8) % 4
    sub_y3 = lane3 % 8
    build_rotations(pad_ref, u_ref, 4, lambda r, here, after: jnp.where(
        sub_z3 + r < 4, pltpu.roll(here, 128 - 8 * r, 2), pltpu.roll(after, 32 - 8 * r, 2)))

    def q_range(g0, group):
        lo = max(0, padc - 1 - (g0 + group - 1))
        hi = padc + n_out - 1 - g0
        return lo, hi

    scan_offsets(u_ref, pen_z_ref, out_ref, n_out, 16, 4, q_range)

    def wbody(i, carry):
        a0 = pl.multiple_of(i * 8, 8)
        v = out_ref[pl.ds(a0, 8)]
        w_ref[0, pl.ds(a0, 8)] = v
        for r in range(1, 8):
            w_ref[r, pl.ds(a0, 8)] = jnp.where(sub_y3 + r < 8, pltpu.roll(v, 128 - r, 2),
                                               pltpu.roll(pltpu.roll(v, 8 - r, 2), 7, 1))
        return carry

    lax.fori_loop(0, n_out // 8, wbody, 0)
    if before_y is not None:
        before_y()
    group = 8
    shifts = []
    for db in range(-8, 8):
        for dy in range(8):
            carry_in = (sub_y + dy >= 8).astype(jnp.int32)
            row = sub + db + carry_in
            valid = (row >= 0) & (row <= 7)
            shifts.append((db, dy, valid))

    def ybody(i, carry):
        a0 = pl.multiple_of(i * group, group)
        acc = [jnp.full(src_ref.shape[1:], jnp.inf, jnp.float32) for _ in range(group)]
        for db, dy, valid in shifts:
            penvec = jnp.where(valid, pen_y_ref[8 * db + dy + 64], jnp.inf)
            for g in range(group):
                v = w_ref[dy, a0 + g]
                if db % 8:
                    v = pltpu.roll(v, (8 - db) % 8, 0)
                acc[g] = jnp.minimum(acc[g], v + penvec)
        for g in range(group):
            out_ref[a0 + g] = acc[g]
        if after_group is not None:
            after_group(a0, group)
        return carry

    lax.fori_loop(0, n_out // group, ybody, 0)


class Exchange:
    def __init__(self, mid_ref, recv_ref, sems):
        self.n_gz, self.n_gy = lax.axis_size("gz"), lax.axis_size("gy")
        self.a, self.b = lax.axis_index("gz"), lax.axis_index("gy")
        self.mid_ref, self.recv_ref, self.sems = mid_ref, recv_ref, sems
        self.barrier = pltpu.get_barrier_semaphore()

    def greet(self):
        a, b, n_gz, n_gy = self.a, self.b, self.n_gz, self.n_gy

        def greet_gy(k, carry):
            pl.semaphore_signal(self.barrier, inc=1, device_id=(a, lax.rem(b + k, n_gy)),
                                device_id_type=MESH)
            return carry

        def greet_gz(k, carry):
            pl.semaphore_signal(self.barrier, inc=1, device_id=(lax.rem(a + k, n_gz), b),
                                device_id_type=MESH)
            return carry

        lax.fori_loop(1, n_gy, greet_gy, 0)
        lax.fori_loop(1, n_gz, greet_gz, 0)

    def wait_greetings(self):
        pl.semaphore_wait(self.barrier, self.n_gy - 1 + self.n_gz - 1)

    def send_rows(self, tiles_ref, t0, count):
        a, b, n_gy = self.a, self.b, self.n_gy
        for k in range(1, n_gy):
            p = lax.rem(b + k, n_gy)
            pltpu.make_async_remote_copy(
                src_ref=tiles_ref.at[pl.ds(t0, count), pl.ds(p, 1)],
                dst_ref=self.mid_ref.at[pl.ds(t0, count), pl.ds(b, 1)], send_sem=self.sems.at[0],
                recv_sem=self.sems.at[1], device_id=(a, p), device_id_type=MESH).start()

    def finish(self, tiles_ref, out_ref):
        a, b, n_gz, n_gy = self.a, self.b, self.n_gz, self.n_gy
        mid_ref, recv_ref, sems = self.mid_ref, self.recv_ref, self.sems
        own = pltpu.make_async_copy(tiles_ref.at[:, pl.ds(b, 1)], mid_ref.at[:, pl.ds(b, 1)], sems.at[2])
        own.start()
        own.wait()
        total = pltpu.make_async_remote_copy(
            src_ref=tiles_ref.at[:, pl.ds(0, n_gy - 1)], dst_ref=mid_ref.at[:, pl.ds(0, n_gy - 1)],
            send_sem=sems.at[0], recv_sem=sems.at[1], device_id=(a, lax.rem(b + 1, n_gy)),
            device_id_type=MESH)
        total.wait_recv()
        total.wait_send()

        def send(k, carry):
            p = lax.rem(a + k, n_gz)
            pltpu.make_async_remote_copy(
                src_ref=mid_ref.at[pl.ds(p, 1)], dst_ref=recv_ref.at[pl.ds(a, 1)], send_sem=sems.at[3],
                recv_sem=sems.at[4], device_id=(p, b), device_id_type=MESH).start()
            return carry

        lax.fori_loop(1, n_gz, send, 0, unroll=4)
        own = pltpu.make_async_copy(mid_ref.at[pl.ds(a, 1)], recv_ref.at[pl.ds(a, 1)], sems.at[5])
        own.start()
        own.wait()
        total = pltpu.make_async_remote_copy(
            src_ref=mid_ref.at[pl.ds(0, n_gz - 1)], dst_ref=recv_ref.at[pl.ds(0, n_gz - 1)],
            send_sem=sems.at[3], recv_sem=sems.at[4], device_id=(lax.rem(a + 1, n_gz), b),
            device_id_type=MESH)
        total.wait_recv()
        total.wait_send()
        out_ref[...] = recv_ref[...]


def exchange_scratch(tiles_shape):
    return [pltpu.VMEM(tiles_shape, jnp.float32)] * 3 + [pltpu.SemaphoreType.DMA((6,))]


def xpass_send_kernel(pen_ref, src_ref, out_ref, pad_ref, u_ref, tiles_ref, mid_ref, recv_ref, sems):
    ex = Exchange(mid_ref, recv_ref, sems)
    ex.greet()

    def after_group(g0, group):
        if g0 == 0:
            ex.wait_greetings()
        ex.send_rows(tiles_ref, g0, group)

    xpass_kernel(pen_ref, src_ref, tiles_ref, pad_ref, u_ref, after_group)
    ex.finish(tiles_ref, out_ref)


def zy_send_kernel(pen_z_ref, pen_y_ref, src_ref, out_ref, pad_ref, u_ref, w_ref, tiles_ref, mid_ref,
                   recv_ref, sems):
    ex = Exchange(mid_ref, recv_ref, sems)
    ex.greet()

    def after_group(a0, group):
        ex.send_rows(tiles_ref, a0, group)

    zy_kernel(pen_z_ref, pen_y_ref, src_ref, tiles_ref, pad_ref, u_ref, w_ref, ex.wait_greetings, after_group)
    ex.finish(tiles_ref, out_ref)


def regularize(current):
    levels, nz, ny, nx = current.shape
    lines = levels * nz * ny
    n_gz = lax.axis_size("gz")
    n_gy = lax.axis_size("gy")
    assert lines == 128 and ny == 8 and n_gy == 8 and n_gz * n_gy == nx
    smem = pl.BlockSpec(memory_space=pltpu.SMEM)
    vmem = pl.BlockSpec(memory_space=pltpu.VMEM)
    tiles = (n_gz, n_gy, lines)
    xq = (KERNEL + 7) // 8
    nxo = nx // 8
    pen_x = penalty_table(8 * (xq * 2 + 2), KERNEL)
    xu = -(-(nxo + 2 * xq + 2) // 8) * 8
    r1 = pl.pallas_call(
        xpass_send_kernel,
        out_shape=jax.ShapeDtypeStruct(tiles, jnp.float32),
        in_specs=[smem, vmem],
        out_specs=vmem,
        scratch_shapes=[pltpu.VMEM((xu + 8, 8, lines), jnp.float32),
                        pltpu.VMEM((8, xu, 8, lines), jnp.float32)] + exchange_scratch(tiles),
        compiler_params=pltpu.CompilerParams(collective_id=1, has_side_effects=True),
    )(pen_x, current.reshape(lines, nx))
    zq = KERNEL // 4
    pen_z = penalty_table(4 * (2 * zq + 2), KERNEL)
    zu = -(-(n_gz + 2 * zq + 2) // 8) * 8
    pen_y = penalty_table(8 * 2 * n_gy, 8 * n_gy)
    r2 = pl.pallas_call(
        zy_send_kernel,
        out_shape=jax.ShapeDtypeStruct(tiles, jnp.float32),
        in_specs=[smem, smem, vmem],
        out_specs=vmem,
        scratch_shapes=[pltpu.VMEM((zu + 8, 8, lines), jnp.float32),
                        pltpu.VMEM((4, zu, 8, lines), jnp.float32),
                        pltpu.VMEM((8, n_gz, 8, lines), jnp.float32)] + exchange_scratch(tiles),
        compiler_params=pltpu.CompilerParams(collective_id=2, has_side_effects=True),
    )(pen_z, pen_y, r1)
    out = local_call(transpose_kernel, (lines, nx), [], r2.reshape(nx, lines))
    return out.reshape(current.shape)


def body(levels, ct_image, region_means):
    current = evolve_all(levels, ct_image, region_means)
    return (current, regularize(current))


def solution(mesh):
    return jax.shard_map(
        body,
        mesh=mesh,
        in_specs=(P(None, "gz", "gy", None), P("gz", "gy", None), P()),
        out_specs=(P(None, "gz", "gy", None), P(None, "gz", "gy", None)),
        check_vma=False,
    )
```

```python
import functools
import math

import jax
import numpy as np
import jax.numpy as jnp
from jax import lax
from jax.experimental import pallas as pl
from jax.experimental.pallas import tpu as pltpu
from jax.sharding import PartitionSpec as P

LEVELS = 4
PHASES = 16
UPDATES = 2
KERNEL = 200


PENALTY = 0.0005
STEP_SIZE = 0.5


def arctan(x):
    ax = jnp.abs(x)
    big = ax > 2.414213562373095
    mid = ax > 0.4142135623730950
    z_big = -1.0 / jnp.where(big, ax, 1.0)
    z_mid = (ax - 1.0) / (ax + 1.0)
    z = jnp.where(big, z_big, jnp.where(mid, z_mid, ax))
    base = jnp.where(big, math.pi / 2, jnp.where(mid, math.pi / 4, 0.0))
    zz = z * z
    poly = (((8.05374449538e-2 * zz - 1.38776856032e-1) * zz + 1.99777106478e-1) * zz
            - 3.33329491539e-1) * zz * z + z
    r = base + poly
    return jnp.where(x < 0, -r, r)


def compute_step(means_ref, cur_ref, zlo_ref, zhi_ref, ylo_ref, yhi_ref, ct_ref, out_ref):
    nz, ny, nx = cur_ref.shape[1], cur_ref.shape[2], cur_ref.shape[3]
    shape = (ny, nx)
    xi = lax.broadcasted_iota(jnp.int32, shape, 1)
    yi = lax.broadcasted_iota(jnp.int32, shape, 0)
    xa = pltpu.roll(xi, 1, 1)
    xb = pltpu.roll(xi, nx - 1, 1)
    xa_ok = jnp.abs(xa - xi) == 1
    xb_ok = jnp.abs(xb - xi) == 1
    ya = pltpu.roll(yi, 1, 0)
    yb = pltpu.roll(yi, ny - 1, 0)
    ya_ok = jnp.abs(ya - yi) == 1
    yb_ok = jnp.abs(yb - yi) == 1
    low_row = yi == 0
    means = [means_ref[p] for p in range(PHASES)]
    for z in range(nz):
        picture = ct_ref[z]
        energy = []
        for p in range(PHASES):
            differ = picture - means[p]
            energy.append(differ * differ)
        phis, lap, g1, g0, dl = [], [], [], [], []
        for k in range(LEVELS):
            c = cur_ref[k, z]
            zm = zlo_ref[k] if z == 0 else cur_ref[k, z - 1]
            zp = zhi_ref[k] if z == nz - 1 else cur_ref[k, z + 1]
            edge = jnp.where(low_row, ylo_ref[k, z], yhi_ref[k, z])
            ym = jnp.where(ya_ok, pltpu.roll(c, 1, 0), edge)
            yp = jnp.where(yb_ok, pltpu.roll(c, ny - 1, 0), edge)
            xm = jnp.where(xa_ok, pltpu.roll(c, 1, 1), 0.0)
            xp = jnp.where(xb_ok, pltpu.roll(c, nx - 1, 1), 0.0)
            lap.append(zm + zp + ym + yp + xm + xp - 6.0 * c)
            h = 0.5 + arctan(c) / math.pi
            g1.append(h)
            g0.append(1.0 - h)
            dl.append(1.0 / (math.pi * (1.0 + c * c)))
            phis.append(c)
        g = (g0, g1)
        pair_lo = {(a, b): g[a][0] * g[b][1] for a in (0, 1) for b in (0, 1)}
        pair_hi = {(a, b): g[a][2] * g[b][3] for a in (0, 1) for b in (0, 1)}
        for k in range(LEVELS):
            force = None
            for q in range(PHASES // 2):
                low = q & ((1 << k) - 1)
                high = (q >> k) << (k + 1)
                p0 = high | low
                p1 = p0 | (1 << k)
                bits = [(p0 >> j) & 1 for j in range(LEVELS)]
                if k == 0:
                    prod = g[bits[1]][1] * pair_hi[(bits[2], bits[3])]
                elif k == 1:
                    prod = g[bits[0]][0] * pair_hi[(bits[2], bits[3])]
                elif k == 2:
                    prod = pair_lo[(bits[0], bits[1])] * g[bits[3]][3]
                else:
                    prod = pair_lo[(bits[0], bits[1])] * g[bits[2]][2]
                term = (energy[p1] - energy[p0]) * prod
                force = term if force is None else force + term
            out_ref[k, z] = phis[k] + STEP_SIZE * dl[k] * (lap[k] - force)


MESH = pl.DeviceIdType.MESH


def evolve_kernel(means_ref, cur_ref, ct_ref, out_ref, mid_ref, zlo_buf, zhi_buf, ylo_buf, yhi_buf,
                  send_sem, recv_sem):
    nz, ny = cur_ref.shape[1], cur_ref.shape[2]
    gz, gy = lax.axis_index("gz"), lax.axis_index("gy")
    n_gz, n_gy = lax.axis_size("gz"), lax.axis_size("gy")
    peers = [(gz > 0, (gz - 1, gy)), (gz < n_gz - 1, (gz + 1, gy)),
             (gy > 0, (gz, gy - 1)), (gy < n_gy - 1, (gz, gy + 1))]
    barrier = pltpu.get_barrier_semaphore()
    for present, dev in peers:
        @pl.when(present)
        def _(dev=dev):
            pl.semaphore_signal(barrier, inc=1, device_id=dev, device_id_type=MESH)
    count = sum(present.astype(jnp.int32) for present, _ in peers)
    pl.semaphore_wait(barrier, count)

    def exchange(step, src_ref):
        plan = [
            (gz < n_gz - 1, gz > 0, src_ref.at[:, nz - 1], zlo_buf.at[step], (gz + 1, gy)),
            (gz > 0, gz < n_gz - 1, src_ref.at[:, 0], zhi_buf.at[step], (gz - 1, gy)),
            (gy < n_gy - 1, gy > 0, src_ref.at[:, :, pl.ds(ny - 1, 1)], ylo_buf.at[step], (gz, gy + 1)),
            (gy > 0, gy < n_gy - 1, src_ref.at[:, :, pl.ds(0, 1)], yhi_buf.at[step], (gz, gy - 1)),
        ]
        copies = []
        for d, (sends, receives, src, dst, target) in enumerate(plan):
            copy = pltpu.make_async_remote_copy(
                src_ref=src, dst_ref=dst, send_sem=send_sem.at[step, d],
                recv_sem=recv_sem.at[step, d], device_id=target, device_id_type=MESH)

            @pl.when(sends)
            def _(copy=copy):
                copy.start()

            @pl.when(jnp.logical_not(receives))
            def _(dst=dst):
                dst[...] = jnp.zeros(dst.shape, jnp.float32)

            copies.append((sends, receives, copy))
        return copies

    def finish(copies):
        for sends, receives, copy in copies:
            @pl.when(receives)
            def _(copy=copy):
                copy.wait_recv()

    def drain(copies):
        for sends, receives, copy in copies:
            @pl.when(sends)
            def _(copy=copy):
                copy.wait_send()

    first = exchange(0, cur_ref)
    finish(first)
    compute_step(means_ref, cur_ref, zlo_buf.at[0], zhi_buf.at[0], ylo_buf.at[0], yhi_buf.at[0], ct_ref, mid_ref)
    drain(first)
    second = exchange(1, mid_ref)
    finish(second)
    compute_step(means_ref, mid_ref, zlo_buf.at[1], zhi_buf.at[1], ylo_buf.at[1], yhi_buf.at[1], ct_ref, out_ref)
    drain(second)


def evolve_all(current, picture, region_means):
    levels, nz, ny, nx = current.shape
    vmem = pl.BlockSpec(memory_space=pltpu.VMEM)
    f32 = jnp.float32
    return pl.pallas_call(
        evolve_kernel,
        out_shape=jax.ShapeDtypeStruct(current.shape, current.dtype),
        in_specs=[pl.BlockSpec(memory_space=pltpu.SMEM), vmem, vmem],
        out_specs=vmem,
        scratch_shapes=[
            pltpu.VMEM(current.shape, f32),
            pltpu.VMEM((2, levels, ny, nx), f32),
            pltpu.VMEM((2, levels, ny, nx), f32),
            pltpu.VMEM((2, levels, nz, 1, nx), f32),
            pltpu.VMEM((2, levels, nz, 1, nx), f32),
            pltpu.SemaphoreType.DMA((2, 4)),
            pltpu.SemaphoreType.DMA((2, 4)),
        ],
        compiler_params=pltpu.CompilerParams(collective_id=0, has_side_effects=True),
    )(region_means, current, picture)


def penalty_table(count, offset):
    distance = (np.arange(count, dtype=np.int32) - offset).astype(np.float32)
    table = np.where(np.abs(distance) <= KERNEL, np.float32(PENALTY) * (distance * distance), np.float32(np.inf))
    return jnp.asarray(table.astype(np.float32))


def scan_offsets(u_ref, pen_ref, out_ref, n_out, group, nrot, q_range, after_group=None):
    for g0 in range(0, n_out, group):
        q_lo, q_hi = q_range(g0, group)
        q_hi = min(q_hi, pen_ref.shape[0] // nrot - 1, u_ref.shape[1] - g0 - group)

        def body(q, acc, g0=g0):
            for r in range(nrot):
                vals = u_ref[r, pl.ds(g0 + q, group)]
                acc = jnp.minimum(acc, vals + pen_ref[q * nrot + r])
            return acc

        init = jnp.full((group,) + tuple(out_ref.shape[1:]), jnp.inf, jnp.float32)
        out_ref[g0:g0 + group] = lax.fori_loop(q_lo, q_hi + 1, body, init, unroll=2)
        if after_group is not None:
            after_group(g0, group)


def build_rotations(pad_ref, u_ref, nrot, pick, chunk=8):
    def body(i, carry):
        b0 = pl.multiple_of(i * chunk, chunk)
        here = pad_ref[pl.ds(b0, chunk)]
        after = pad_ref[pl.ds(b0 + 1, chunk)]
        u_ref[0, pl.ds(b0, chunk)] = here
        for r in range(1, nrot):
            u_ref[r, pl.ds(b0, chunk)] = pick(r, here, after)
        return carry

    lax.fori_loop(0, u_ref.shape[1] // chunk, body, 0)


def xpass_kernel(pen_ref, src_ref, out_ref, pad_ref, u_ref, after_group=None):
    lines, nx = src_ref.shape
    reach = KERNEL
    padc = reach // 8
    pad_ref[...] = jnp.full(pad_ref.shape, jnp.inf, jnp.float32)
    pad_ref[padc:padc + nx // 8] = src_ref[...].T.reshape(nx // 8, 8, lines)
    sub = lax.broadcasted_iota(jnp.int32, (8, 8, lines), 1)
    build_rotations(pad_ref, u_ref, 8, lambda r, here, after: jnp.where(
        sub < 8 - r, pltpu.roll(here, 8 - r, 1), pltpu.roll(after, 8 - r, 1)))
    n_out = nx // 8

    def q_range(g0, group):
        lo = max(0, -((8 * (g0 + group - 1) + 14 - reach) // 8))
        hi = (reach + nx - 1 - 8 * g0) // 8
        return lo, hi

    scan_offsets(u_ref, pen_ref, out_ref, n_out, 16, 8, q_range, after_group)


def transpose_kernel(src_ref, out_ref):
    out_ref[...] = src_ref[...].T


def local_call(kernel, out_shape, scratch, *args):
    vmem = pl.BlockSpec(memory_space=pltpu.VMEM)
    smem = pl.BlockSpec(memory_space=pltpu.SMEM)
    specs = [smem if a.ndim == 1 else vmem for a in args]
    return pl.pallas_call(
        kernel,
        out_shape=jax.ShapeDtypeStruct(out_shape, jnp.float32),
        in_specs=specs,
        out_specs=vmem,
        scratch_shapes=[pltpu.VMEM(s, jnp.float32) for s in scratch],
    )(*args)


def zy_kernel(pen_z_ref, pen_y_ref, src_ref, out_ref, pad_ref, u_ref, w_ref, before_y=None, after_group=None):
    n_out = src_ref.shape[0]
    padc = KERNEL // 4
    pad_ref[...] = jnp.full(pad_ref.shape, jnp.inf, jnp.float32)
    pad_ref[padc:padc + n_out] = src_ref[...]
    lane = lax.broadcasted_iota(jnp.int32, src_ref.shape[1:], 1)
    sub = lax.broadcasted_iota(jnp.int32, src_ref.shape[1:], 0)
    sub_z = (lane // 8) % 4
    sub_y = lane % 8

    lane3 = lax.broadcasted_iota(jnp.int32, (8,) + tuple(src_ref.shape[1:]), 2)
    sub_z3 = (lane3 // 8) % 4
    sub_y3 = lane3 % 8
    build_rotations(pad_ref, u_ref, 4, lambda r, here, after: jnp.where(
        sub_z3 + r < 4, pltpu.roll(here, 128 - 8 * r, 2), pltpu.roll(after, 32 - 8 * r, 2)))

    def q_range(g0, group):
        lo = max(0, padc - 1 - (g0 + group - 1))
        hi = padc + n_out - 1 - g0
        return lo, hi

    scan_offsets(u_ref, pen_z_ref, out_ref, n_out, 16, 4, q_range)

    def wbody(i, carry):
        a0 = pl.multiple_of(i * 8, 8)
        v = out_ref[pl.ds(a0, 8)]
        w_ref[0, pl.ds(a0, 8)] = v
        for r in range(1, 8):
            w_ref[r, pl.ds(a0, 8)] = jnp.where(sub_y3 + r < 8, pltpu.roll(v, 128 - r, 2),
                                               pltpu.roll(pltpu.roll(v, 8 - r, 2), 7, 1))
        return carry

    lax.fori_loop(0, n_out // 8, wbody, 0)
    if before_y is not None:
        before_y()
    group = 8
    shifts = []
    for db in range(-8, 8):
        for dy in range(8):
            carry_in = (sub_y + dy >= 8).astype(jnp.int32)
            row = sub + db + carry_in
            valid = (row >= 0) & (row <= 7)
            shifts.append((db, dy, valid))

    def ybody(i, carry):
        a0 = pl.multiple_of(i * group, group)
        acc = [jnp.full(src_ref.shape[1:], jnp.inf, jnp.float32) for _ in range(group)]
        for db, dy, valid in shifts:
            penvec = jnp.where(valid, pen_y_ref[8 * db + dy + 64], jnp.inf)
            for g in range(group):
                v = w_ref[dy, a0 + g]
                if db % 8:
                    v = pltpu.roll(v, (8 - db) % 8, 0)
                acc[g] = jnp.minimum(acc[g], v + penvec)
        for g in range(group):
            out_ref[a0 + g] = acc[g]
        if after_group is not None:
            after_group(a0, group)
        return carry

    lax.fori_loop(0, n_out // group, ybody, 0)


class Exchange:
    def __init__(self, mid_ref, recv_ref, sems):
        self.n_gz, self.n_gy = lax.axis_size("gz"), lax.axis_size("gy")
        self.a, self.b = lax.axis_index("gz"), lax.axis_index("gy")
        self.mid_ref, self.recv_ref, self.sems = mid_ref, recv_ref, sems
        self.barrier = pltpu.get_barrier_semaphore()

    def greet(self):
        a, b, n_gz, n_gy = self.a, self.b, self.n_gz, self.n_gy

        def greet_gy(k, carry):
            pl.semaphore_signal(self.barrier, inc=1, device_id=(a, lax.rem(b + k, n_gy)),
                                device_id_type=MESH)
            return carry

        def greet_gz(k, carry):
            pl.semaphore_signal(self.barrier, inc=1, device_id=(lax.rem(a + k, n_gz), b),
                                device_id_type=MESH)
            return carry

        lax.fori_loop(1, n_gy, greet_gy, 0)
        lax.fori_loop(1, n_gz, greet_gz, 0)

    def wait_greetings(self):
        pl.semaphore_wait(self.barrier, self.n_gy - 1 + self.n_gz - 1)

    def send_rows(self, tiles_ref, t0, count):
        a, b, n_gy = self.a, self.b, self.n_gy
        for k in range(1, n_gy):
            p = lax.rem(b + k, n_gy)
            pltpu.make_async_remote_copy(
                src_ref=tiles_ref.at[pl.ds(t0, count), pl.ds(p, 1)],
                dst_ref=self.mid_ref.at[pl.ds(t0, count), pl.ds(b, 1)], send_sem=self.sems.at[0],
                recv_sem=self.sems.at[1], device_id=(a, p), device_id_type=MESH).start()

    def finish(self, tiles_ref, out_ref, transpose=False):
        a, b, n_gz, n_gy = self.a, self.b, self.n_gz, self.n_gy
        mid_ref, recv_ref, sems = self.mid_ref, self.recv_ref, self.sems
        own = pltpu.make_async_copy(tiles_ref.at[:, pl.ds(b, 1)], mid_ref.at[:, pl.ds(b, 1)], sems.at[2])
        own.start()
        own.wait()
        total = pltpu.make_async_remote_copy(
            src_ref=tiles_ref.at[:, pl.ds(0, n_gy - 1)], dst_ref=mid_ref.at[:, pl.ds(0, n_gy - 1)],
            send_sem=sems.at[0], recv_sem=sems.at[1], device_id=(a, lax.rem(b + 1, n_gy)),
            device_id_type=MESH)
        total.wait_recv()
        total.wait_send()

        def send(k, carry):
            p = lax.rem(a + k, n_gz)
            pltpu.make_async_remote_copy(
                src_ref=mid_ref.at[pl.ds(p, 1)], dst_ref=recv_ref.at[pl.ds(a, 1)], send_sem=sems.at[3],
                recv_sem=sems.at[4], device_id=(p, b), device_id_type=MESH).start()
            return carry

        lax.fori_loop(1, n_gz, send, 0, unroll=4)
        own = pltpu.make_async_copy(mid_ref.at[pl.ds(a, 1)], recv_ref.at[pl.ds(a, 1)], sems.at[5])
        own.start()
        own.wait()
        total = pltpu.make_async_remote_copy(
            src_ref=mid_ref.at[pl.ds(0, n_gz - 1)], dst_ref=recv_ref.at[pl.ds(0, n_gz - 1)],
            send_sem=sems.at[3], recv_sem=sems.at[4], device_id=(lax.rem(a + 1, n_gz), b),
            device_id_type=MESH)
        total.wait_recv()
        total.wait_send()
        if transpose:
            out_ref[...] = recv_ref[...].reshape(out_ref.shape[::-1]).T
        else:
            out_ref[...] = recv_ref[...]


def exchange_scratch(tiles_shape):
    return [pltpu.VMEM(tiles_shape, jnp.float32)] * 3 + [pltpu.SemaphoreType.DMA((6,))]


def xpass_send_kernel(pen_ref, src_ref, out_ref, pad_ref, u_ref, tiles_ref, mid_ref, recv_ref, sems):
    ex = Exchange(mid_ref, recv_ref, sems)
    ex.greet()

    def after_group(g0, group):
        if g0 == 0:
            ex.wait_greetings()
        ex.send_rows(tiles_ref, g0, group)

    xpass_kernel(pen_ref, src_ref, tiles_ref, pad_ref, u_ref, after_group)
    ex.finish(tiles_ref, out_ref)


def zy_send_kernel(pen_z_ref, pen_y_ref, src_ref, out_ref, pad_ref, u_ref, w_ref, tiles_ref, mid_ref,
                   recv_ref, sems):
    ex = Exchange(mid_ref, recv_ref, sems)
    ex.greet()

    def after_group(a0, group):
        ex.send_rows(tiles_ref, a0, group)

    zy_kernel(pen_z_ref, pen_y_ref, src_ref, tiles_ref, pad_ref, u_ref, w_ref, ex.wait_greetings, after_group)
    ex.finish(tiles_ref, out_ref, transpose=True)


def regularize(current):
    levels, nz, ny, nx = current.shape
    lines = levels * nz * ny
    n_gz = lax.axis_size("gz")
    n_gy = lax.axis_size("gy")
    assert lines == 128 and ny == 8 and n_gy == 8 and n_gz * n_gy == nx
    smem = pl.BlockSpec(memory_space=pltpu.SMEM)
    vmem = pl.BlockSpec(memory_space=pltpu.VMEM)
    tiles = (n_gz, n_gy, lines)
    xq = (KERNEL + 7) // 8
    nxo = nx // 8
    pen_x = penalty_table(8 * (xq * 2 + 2), KERNEL)
    xu = -(-(nxo + 2 * xq + 2) // 8) * 8
    r1 = pl.pallas_call(
        xpass_send_kernel,
        out_shape=jax.ShapeDtypeStruct(tiles, jnp.float32),
        in_specs=[smem, vmem],
        out_specs=vmem,
        scratch_shapes=[pltpu.VMEM((xu + 8, 8, lines), jnp.float32),
                        pltpu.VMEM((8, xu, 8, lines), jnp.float32)] + exchange_scratch(tiles),
        compiler_params=pltpu.CompilerParams(collective_id=1, has_side_effects=True),
    )(pen_x, current.reshape(lines, nx))
    zq = KERNEL // 4
    pen_z = penalty_table(4 * (2 * zq + 2), KERNEL)
    zu = -(-(n_gz + 2 * zq + 2) // 8) * 8
    pen_y = penalty_table(8 * 2 * n_gy, 8 * n_gy)
    r2 = pl.pallas_call(
        zy_send_kernel,
        out_shape=jax.ShapeDtypeStruct((lines, nx), jnp.float32),
        in_specs=[smem, smem, vmem],
        out_specs=vmem,
        scratch_shapes=[pltpu.VMEM((zu + 8, 8, lines), jnp.float32),
                        pltpu.VMEM((4, zu, 8, lines), jnp.float32),
                        pltpu.VMEM((8, n_gz, 8, lines), jnp.float32)] + exchange_scratch(tiles),
        compiler_params=pltpu.CompilerParams(collective_id=2, has_side_effects=True),
    )(pen_z, pen_y, r1)
    return r2.reshape(current.shape)


def body(levels, ct_image, region_means):
    current = evolve_all(levels, ct_image, region_means)
    return (current, regularize(current))


def solution(mesh):
    return jax.shard_map(
        body,
        mesh=mesh,
        in_specs=(P(None, "gz", "gy", None), P("gz", "gy", None), P()),
        out_specs=(P(None, "gz", "gy", None), P(None, "gz", "gy", None)),
        check_vma=False,
    )
```

```python
import functools
import math

import jax
import numpy as np
import jax.numpy as jnp
from jax import lax
from jax.experimental import pallas as pl
from jax.experimental.pallas import tpu as pltpu
from jax.sharding import PartitionSpec as P

LEVELS = 4
PHASES = 16
UPDATES = 2
KERNEL = 200


PENALTY = 0.0005
STEP_SIZE = 0.5


def arctan(x):
    ax = jnp.abs(x)
    big = ax > 2.414213562373095
    mid = ax > 0.4142135623730950
    z_big = -1.0 / jnp.where(big, ax, 1.0)
    z_mid = (ax - 1.0) / (ax + 1.0)
    z = jnp.where(big, z_big, jnp.where(mid, z_mid, ax))
    base = jnp.where(big, math.pi / 2, jnp.where(mid, math.pi / 4, 0.0))
    zz = z * z
    poly = (((8.05374449538e-2 * zz - 1.38776856032e-1) * zz + 1.99777106478e-1) * zz
            - 3.33329491539e-1) * zz * z + z
    r = base + poly
    return jnp.where(x < 0, -r, r)


def compute_step(means_ref, cur_ref, zlo_ref, zhi_ref, ylo_ref, yhi_ref, ct_ref, out_ref):
    nz, ny, nx = cur_ref.shape[1], cur_ref.shape[2], cur_ref.shape[3]
    shape = (ny, nx)
    xi = lax.broadcasted_iota(jnp.int32, shape, 1)
    yi = lax.broadcasted_iota(jnp.int32, shape, 0)
    xa = pltpu.roll(xi, 1, 1)
    xb = pltpu.roll(xi, nx - 1, 1)
    xa_ok = jnp.abs(xa - xi) == 1
    xb_ok = jnp.abs(xb - xi) == 1
    ya = pltpu.roll(yi, 1, 0)
    yb = pltpu.roll(yi, ny - 1, 0)
    ya_ok = jnp.abs(ya - yi) == 1
    yb_ok = jnp.abs(yb - yi) == 1
    low_row = yi == 0
    means = [means_ref[p] for p in range(PHASES)]
    for z in range(nz):
        picture = ct_ref[z]
        energy = []
        for p in range(PHASES):
            differ = picture - means[p]
            energy.append(differ * differ)
        phis, lap, g1, g0, dl = [], [], [], [], []
        for k in range(LEVELS):
            c = cur_ref[k, z]
            zm = zlo_ref[k] if z == 0 else cur_ref[k, z - 1]
            zp = zhi_ref[k] if z == nz - 1 else cur_ref[k, z + 1]
            edge = jnp.where(low_row, ylo_ref[k, z], yhi_ref[k, z])
            ym = jnp.where(ya_ok, pltpu.roll(c, 1, 0), edge)
            yp = jnp.where(yb_ok, pltpu.roll(c, ny - 1, 0), edge)
            xm = jnp.where(xa_ok, pltpu.roll(c, 1, 1), 0.0)
            xp = jnp.where(xb_ok, pltpu.roll(c, nx - 1, 1), 0.0)
            lap.append(zm + zp + ym + yp + xm + xp - 6.0 * c)
            h = 0.5 + arctan(c) / math.pi
            g1.append(h)
            g0.append(1.0 - h)
            dl.append(1.0 / (math.pi * (1.0 + c * c)))
            phis.append(c)
        g = (g0, g1)
        pair_lo = {(a, b): g[a][0] * g[b][1] for a in (0, 1) for b in (0, 1)}
        pair_hi = {(a, b): g[a][2] * g[b][3] for a in (0, 1) for b in (0, 1)}
        for k in range(LEVELS):
            force = None
            for q in range(PHASES // 2):
                low = q & ((1 << k) - 1)
                high = (q >> k) << (k + 1)
                p0 = high | low
                p1 = p0 | (1 << k)
                bits = [(p0 >> j) & 1 for j in range(LEVELS)]
                if k == 0:
                    prod = g[bits[1]][1] * pair_hi[(bits[2], bits[3])]
                elif k == 1:
                    prod = g[bits[0]][0] * pair_hi[(bits[2], bits[3])]
                elif k == 2:
                    prod = pair_lo[(bits[0], bits[1])] * g[bits[3]][3]
                else:
                    prod = pair_lo[(bits[0], bits[1])] * g[bits[2]][2]
                term = (energy[p1] - energy[p0]) * prod
                force = term if force is None else force + term
            out_ref[k, z] = phis[k] + STEP_SIZE * dl[k] * (lap[k] - force)


MESH = pl.DeviceIdType.MESH


def evolve_kernel(means_ref, cur_ref, ct_ref, out_ref, mid_ref, zlo_buf, zhi_buf, ylo_buf, yhi_buf,
                  send_sem, recv_sem):
    nz, ny = cur_ref.shape[1], cur_ref.shape[2]
    gz, gy = lax.axis_index("gz"), lax.axis_index("gy")
    n_gz, n_gy = lax.axis_size("gz"), lax.axis_size("gy")
    peers = [(gz > 0, (gz - 1, gy)), (gz < n_gz - 1, (gz + 1, gy)),
             (gy > 0, (gz, gy - 1)), (gy < n_gy - 1, (gz, gy + 1))]
    barrier = pltpu.get_barrier_semaphore()
    for present, dev in peers:
        @pl.when(present)
        def _(dev=dev):
            pl.semaphore_signal(barrier, inc=1, device_id=dev, device_id_type=MESH)
    count = sum(present.astype(jnp.int32) for present, _ in peers)
    pl.semaphore_wait(barrier, count)

    def exchange(step, src_ref):
        plan = [
            (gz < n_gz - 1, gz > 0, src_ref.at[:, nz - 1], zlo_buf.at[step], (gz + 1, gy)),
            (gz > 0, gz < n_gz - 1, src_ref.at[:, 0], zhi_buf.at[step], (gz - 1, gy)),
            (gy < n_gy - 1, gy > 0, src_ref.at[:, :, pl.ds(ny - 1, 1)], ylo_buf.at[step], (gz, gy + 1)),
            (gy > 0, gy < n_gy - 1, src_ref.at[:, :, pl.ds(0, 1)], yhi_buf.at[step], (gz, gy - 1)),
        ]
        copies = []
        for d, (sends, receives, src, dst, target) in enumerate(plan):
            copy = pltpu.make_async_remote_copy(
                src_ref=src, dst_ref=dst, send_sem=send_sem.at[step, d],
                recv_sem=recv_sem.at[step, d], device_id=target, device_id_type=MESH)

            @pl.when(sends)
            def _(copy=copy):
                copy.start()

            @pl.when(jnp.logical_not(receives))
            def _(dst=dst):
                dst[...] = jnp.zeros(dst.shape, jnp.float32)

            copies.append((sends, receives, copy))
        return copies

    def finish(copies):
        for sends, receives, copy in copies:
            @pl.when(receives)
            def _(copy=copy):
                copy.wait_recv()

    def drain(copies):
        for sends, receives, copy in copies:
            @pl.when(sends)
            def _(copy=copy):
                copy.wait_send()

    first = exchange(0, cur_ref)
    finish(first)
    compute_step(means_ref, cur_ref, zlo_buf.at[0], zhi_buf.at[0], ylo_buf.at[0], yhi_buf.at[0], ct_ref, mid_ref)
    drain(first)
    second = exchange(1, mid_ref)
    finish(second)
    compute_step(means_ref, mid_ref, zlo_buf.at[1], zhi_buf.at[1], ylo_buf.at[1], yhi_buf.at[1], ct_ref, out_ref)
    drain(second)


def evolve_all(current, picture, region_means):
    levels, nz, ny, nx = current.shape
    vmem = pl.BlockSpec(memory_space=pltpu.VMEM)
    f32 = jnp.float32
    return pl.pallas_call(
        evolve_kernel,
        out_shape=jax.ShapeDtypeStruct(current.shape, current.dtype),
        in_specs=[pl.BlockSpec(memory_space=pltpu.SMEM), vmem, vmem],
        out_specs=vmem,
        scratch_shapes=[
            pltpu.VMEM(current.shape, f32),
            pltpu.VMEM((2, levels, ny, nx), f32),
            pltpu.VMEM((2, levels, ny, nx), f32),
            pltpu.VMEM((2, levels, nz, 1, nx), f32),
            pltpu.VMEM((2, levels, nz, 1, nx), f32),
            pltpu.SemaphoreType.DMA((2, 4)),
            pltpu.SemaphoreType.DMA((2, 4)),
        ],
        compiler_params=pltpu.CompilerParams(collective_id=0, has_side_effects=True),
    )(region_means, current, picture)


def penalty_table(count, offset):
    distance = (np.arange(count, dtype=np.int32) - offset).astype(np.float32)
    table = np.where(np.abs(distance) <= KERNEL, np.float32(PENALTY) * (distance * distance), np.float32(np.inf))
    return jnp.asarray(table.astype(np.float32))


def scan_offsets(u_ref, pen_ref, out_ref, n_out, group, nrot, q_range, after_group=None):
    for g0 in range(0, n_out, group):
        q_lo, q_hi = q_range(g0, group)
        q_hi = min(q_hi, pen_ref.shape[0] // nrot - 1, u_ref.shape[1] - g0 - group)

        def body(q, acc, g0=g0):
            for r in range(nrot):
                vals = u_ref[r, pl.ds(g0 + q, group)]
                acc = jnp.minimum(acc, vals + pen_ref[q * nrot + r])
            return acc

        init = jnp.full((group,) + tuple(out_ref.shape[1:]), jnp.inf, jnp.float32)
        out_ref[g0:g0 + group] = lax.fori_loop(q_lo, q_hi + 1, body, init, unroll=2)
        if after_group is not None:
            after_group(g0, group)


def build_rotations(pad_ref, u_ref, nrot, pick, chunk=8):
    def body(i, carry):
        b0 = pl.multiple_of(i * chunk, chunk)
        here = pad_ref[pl.ds(b0, chunk)]
        after = pad_ref[pl.ds(b0 + 1, chunk)]
        u_ref[0, pl.ds(b0, chunk)] = here
        for r in range(1, nrot):
            u_ref[r, pl.ds(b0, chunk)] = pick(r, here, after)
        return carry

    lax.fori_loop(0, u_ref.shape[1] // chunk, body, 0)


def xpass_kernel(pen_ref, src_ref, out_ref, pad_ref, u_ref, after_group=None):
    lines, nx = src_ref.shape
    reach = KERNEL
    padc = reach // 8
    pad_ref[...] = jnp.full(pad_ref.shape, jnp.inf, jnp.float32)
    pad_ref[padc:padc + nx // 8] = src_ref[...].T.reshape(nx // 8, 8, lines)
    sub = lax.broadcasted_iota(jnp.int32, (8, 8, lines), 1)
    build_rotations(pad_ref, u_ref, 8, lambda r, here, after: jnp.where(
        sub < 8 - r, pltpu.roll(here, 8 - r, 1), pltpu.roll(after, 8 - r, 1)))
    n_out = nx // 8

    def q_range(g0, group):
        lo = max(0, -((8 * (g0 + group - 1) + 14 - reach) // 8))
        hi = (reach + nx - 1 - 8 * g0) // 8
        return lo, hi

    scan_offsets(u_ref, pen_ref, out_ref, n_out, 16, 8, q_range, after_group)


def transpose_kernel(src_ref, out_ref):
    out_ref[...] = src_ref[...].T


def local_call(kernel, out_shape, scratch, *args):
    vmem = pl.BlockSpec(memory_space=pltpu.VMEM)
    smem = pl.BlockSpec(memory_space=pltpu.SMEM)
    specs = [smem if a.ndim == 1 else vmem for a in args]
    return pl.pallas_call(
        kernel,
        out_shape=jax.ShapeDtypeStruct(out_shape, jnp.float32),
        in_specs=specs,
        out_specs=vmem,
        scratch_shapes=[pltpu.VMEM(s, jnp.float32) for s in scratch],
    )(*args)


def zy_kernel(pen_z_ref, pen_y_ref, src_ref, out_ref, pad_ref, u_ref, w_ref, before_y=None, after_group=None):
    n_out = src_ref.shape[0]
    padc = KERNEL // 4
    pad_ref[...] = jnp.full(pad_ref.shape, jnp.inf, jnp.float32)
    pad_ref[padc:padc + n_out] = src_ref[...]
    lane = lax.broadcasted_iota(jnp.int32, src_ref.shape[1:], 1)
    sub = lax.broadcasted_iota(jnp.int32, src_ref.shape[1:], 0)
    sub_z = (lane // 8) % 4
    sub_y = lane % 8

    lane3 = lax.broadcasted_iota(jnp.int32, (8,) + tuple(src_ref.shape[1:]), 2)
    sub_z3 = (lane3 // 8) % 4
    sub_y3 = lane3 % 8
    build_rotations(pad_ref, u_ref, 4, lambda r, here, after: jnp.where(
        sub_z3 + r < 4, pltpu.roll(here, 128 - 8 * r, 2), pltpu.roll(after, 32 - 8 * r, 2)))

    def q_range(g0, group):
        lo = max(0, padc - 1 - (g0 + group - 1))
        hi = padc + n_out - 1 - g0
        return lo, hi

    scan_offsets(u_ref, pen_z_ref, out_ref, n_out, 16, 4, q_range)

    def wbody(i, carry):
        a0 = pl.multiple_of(i * 8, 8)
        v = out_ref[pl.ds(a0, 8)]
        w_ref[0, pl.ds(a0, 8)] = v
        for r in range(1, 8):
            w_ref[r, pl.ds(a0, 8)] = jnp.where(sub_y3 + r < 8, pltpu.roll(v, 128 - r, 2),
                                               pltpu.roll(pltpu.roll(v, 8 - r, 2), 7, 1))
        return carry

    lax.fori_loop(0, n_out // 8, wbody, 0)
    if before_y is not None:
        before_y()
    group = 8
    shifts = []
    for db in range(-8, 8):
        for dy in range(8):
            carry_in = (sub_y + dy >= 8).astype(jnp.int32)
            row = sub + db + carry_in
            valid = (row >= 0) & (row <= 7)
            shifts.append((db, dy, valid))

    def ybody(i, carry):
        a0 = pl.multiple_of(i * group, group)
        acc = [jnp.full(src_ref.shape[1:], jnp.inf, jnp.float32) for _ in range(group)]
        for db, dy, valid in shifts:
            penvec = jnp.where(valid, pen_y_ref[8 * db + dy + 64], jnp.inf)
            for g in range(group):
                v = w_ref[dy, a0 + g]
                if db % 8:
                    v = pltpu.roll(v, (8 - db) % 8, 0)
                acc[g] = jnp.minimum(acc[g], v + penvec)
        for g in range(group):
            out_ref[a0 + g] = acc[g]
        if after_group is not None:
            after_group(a0, group)
        return carry

    lax.fori_loop(0, n_out // group, ybody, 0)


class Exchange:
    def __init__(self, mid_ref, recv_ref, sems, grp_sems, count):
        self.n_gz, self.n_gy = lax.axis_size("gz"), lax.axis_size("gy")
        self.a, self.b = lax.axis_index("gz"), lax.axis_index("gy")
        self.mid_ref, self.recv_ref, self.sems = mid_ref, recv_ref, sems
        self.grp_sems, self.count = grp_sems, count
        self.barrier = pltpu.get_barrier_semaphore()

    def greet(self):
        a, b, n_gz, n_gy = self.a, self.b, self.n_gz, self.n_gy

        def greet_gy(k, carry):
            pl.semaphore_signal(self.barrier, inc=1, device_id=(a, lax.rem(b + k, n_gy)),
                                device_id_type=MESH)
            return carry

        def greet_gz(k, carry):
            pl.semaphore_signal(self.barrier, inc=1, device_id=(lax.rem(a + k, n_gz), b),
                                device_id_type=MESH)
            return carry

        lax.fori_loop(1, n_gy, greet_gy, 0)
        lax.fori_loop(1, n_gz, greet_gz, 0)

    def wait_greetings(self):
        pl.semaphore_wait(self.barrier, self.n_gy - 1 + self.n_gz - 1)

    def send_rows(self, tiles_ref, g, t0):
        a, b, n_gy, count = self.a, self.b, self.n_gy, self.count
        for k in range(1, n_gy):
            p = lax.rem(b + k, n_gy)
            pltpu.make_async_remote_copy(
                src_ref=tiles_ref.at[pl.ds(t0, count), pl.ds(p, 1)],
                dst_ref=self.mid_ref.at[pl.ds(t0, count), pl.ds(b, 1)], send_sem=self.sems.at[0],
                recv_sem=self.grp_sems.at[g], device_id=(a, p), device_id_type=MESH).start()
        own = pltpu.make_async_copy(tiles_ref.at[pl.ds(t0, count), pl.ds(b, 1)],
                                    self.mid_ref.at[pl.ds(t0, count), pl.ds(b, 1)], self.sems.at[2])
        own.start()
        own.wait()

    def forward_group(self, g, t0):
        a, b, n_gy, count = self.a, self.b, self.n_gy, self.count
        pltpu.make_async_remote_copy(
            src_ref=self.mid_ref.at[pl.ds(t0, count), pl.ds(0, n_gy - 1)],
            dst_ref=self.mid_ref.at[pl.ds(t0, count), pl.ds(0, n_gy - 1)], send_sem=self.sems.at[0],
            recv_sem=self.grp_sems.at[g], device_id=(a, lax.rem(b + 1, n_gy)),
            device_id_type=MESH).wait_recv()
        for j in range(count):
            p = t0 + j

            @pl.when(p != a)
            def _(p=p):
                pltpu.make_async_remote_copy(
                    src_ref=self.mid_ref.at[pl.ds(p, 1)], dst_ref=self.recv_ref.at[pl.ds(a, 1)],
                    send_sem=self.sems.at[3], recv_sem=self.sems.at[4], device_id=(p, b),
                    device_id_type=MESH).start()

    def finish(self, tiles_ref, out_ref, transpose=False):
        a, b, n_gz, n_gy = self.a, self.b, self.n_gz, self.n_gy
        mid_ref, recv_ref, sems = self.mid_ref, self.recv_ref, self.sems
        last = n_gz // self.count - 1
        self.forward_group(last, last * self.count)
        pltpu.make_async_remote_copy(
            src_ref=tiles_ref.at[:, pl.ds(0, n_gy - 1)], dst_ref=mid_ref.at[:, pl.ds(0, n_gy - 1)],
            send_sem=sems.at[0], recv_sem=sems.at[1], device_id=(a, lax.rem(b + 1, n_gy)),
            device_id_type=MESH).wait_send()
        own = pltpu.make_async_copy(mid_ref.at[pl.ds(a, 1)], recv_ref.at[pl.ds(a, 1)], sems.at[5])
        own.start()
        own.wait()
        total = pltpu.make_async_remote_copy(
            src_ref=mid_ref.at[pl.ds(0, n_gz - 1)], dst_ref=recv_ref.at[pl.ds(0, n_gz - 1)],
            send_sem=sems.at[3], recv_sem=sems.at[4], device_id=(lax.rem(a + 1, n_gz), b),
            device_id_type=MESH)
        total.wait_recv()
        total.wait_send()
        if transpose:
            out_ref[...] = recv_ref[...].reshape(out_ref.shape[::-1]).T
        else:
            out_ref[...] = recv_ref[...]


def exchange_scratch(tiles_shape, groups):
    return [pltpu.VMEM(tiles_shape, jnp.float32)] * 3 + [pltpu.SemaphoreType.DMA((6,)),
                                                         pltpu.SemaphoreType.DMA((groups,))]


def xpass_send_kernel(pen_ref, src_ref, out_ref, pad_ref, u_ref, tiles_ref, mid_ref, recv_ref, sems, grp_sems):
    ex = Exchange(mid_ref, recv_ref, sems, grp_sems, 16)
    ex.greet()

    def after_group(g0, group):
        assert group == ex.count
        g = g0 // group
        if g == 0:
            ex.wait_greetings()
        ex.send_rows(tiles_ref, g, g0)
        if g >= 1:
            ex.forward_group(g - 1, g0 - group)

    xpass_kernel(pen_ref, src_ref, tiles_ref, pad_ref, u_ref, after_group)
    ex.finish(tiles_ref, out_ref)


def zy_send_kernel(pen_z_ref, pen_y_ref, src_ref, out_ref, pad_ref, u_ref, w_ref, tiles_ref, mid_ref,
                   recv_ref, sems, grp_sems):
    ex = Exchange(mid_ref, recv_ref, sems, grp_sems, 8)
    ex.greet()

    def after_group(a0, group):
        assert group == ex.count
        g = a0 // group
        ex.send_rows(tiles_ref, g, a0)

        @pl.when(g >= 1)
        def _():
            ex.forward_group(g - 1, a0 - group)

    zy_kernel(pen_z_ref, pen_y_ref, src_ref, tiles_ref, pad_ref, u_ref, w_ref, ex.wait_greetings, after_group)
    ex.finish(tiles_ref, out_ref, transpose=True)


def regularize(current):
    levels, nz, ny, nx = current.shape
    lines = levels * nz * ny
    n_gz = lax.axis_size("gz")
    n_gy = lax.axis_size("gy")
    assert lines == 128 and ny == 8 and n_gy == 8 and n_gz * n_gy == nx
    smem = pl.BlockSpec(memory_space=pltpu.SMEM)
    vmem = pl.BlockSpec(memory_space=pltpu.VMEM)
    tiles = (n_gz, n_gy, lines)
    xq = (KERNEL + 7) // 8
    nxo = nx // 8
    pen_x = penalty_table(8 * (xq * 2 + 2), KERNEL)
    xu = -(-(nxo + 2 * xq + 2) // 8) * 8
    r1 = pl.pallas_call(
        xpass_send_kernel,
        out_shape=jax.ShapeDtypeStruct(tiles, jnp.float32),
        in_specs=[smem, vmem],
        out_specs=vmem,
        scratch_shapes=[pltpu.VMEM((xu + 8, 8, lines), jnp.float32),
                        pltpu.VMEM((8, xu, 8, lines), jnp.float32)] + exchange_scratch(tiles, n_gz // 16),
        compiler_params=pltpu.CompilerParams(collective_id=1, has_side_effects=True),
    )(pen_x, current.reshape(lines, nx))
    zq = KERNEL // 4
    pen_z = penalty_table(4 * (2 * zq + 2), KERNEL)
    zu = -(-(n_gz + 2 * zq + 2) // 8) * 8
    pen_y = penalty_table(8 * 2 * n_gy, 8 * n_gy)
    r2 = pl.pallas_call(
        zy_send_kernel,
        out_shape=jax.ShapeDtypeStruct((lines, nx), jnp.float32),
        in_specs=[smem, smem, vmem],
        out_specs=vmem,
        scratch_shapes=[pltpu.VMEM((zu + 8, 8, lines), jnp.float32),
                        pltpu.VMEM((4, zu, 8, lines), jnp.float32),
                        pltpu.VMEM((8, n_gz, 8, lines), jnp.float32)] + exchange_scratch(tiles, n_gz // 8),
        compiler_params=pltpu.CompilerParams(collective_id=2, has_side_effects=True),
    )(pen_z, pen_y, r1)
    return r2.reshape(current.shape)


def body(levels, ct_image, region_means):
    current = evolve_all(levels, ct_image, region_means)
    return (current, regularize(current))


def solution(mesh):
    return jax.shard_map(
        body,
        mesh=mesh,
        in_specs=(P(None, "gz", "gy", None), P("gz", "gy", None), P()),
        out_specs=(P(None, "gz", "gy", None), P(None, "gz", "gy", None)),
        check_vma=False,
    )
```

```python
import functools
import math

import jax
import numpy as np
import jax.numpy as jnp
from jax import lax
from jax.experimental import pallas as pl
from jax.experimental.pallas import tpu as pltpu
from jax.sharding import PartitionSpec as P

LEVELS = 4
PHASES = 16
UPDATES = 2
KERNEL = 200


PENALTY = 0.0005
STEP_SIZE = 0.5


def arctan(x):
    ax = jnp.abs(x)
    big = ax > 2.414213562373095
    mid = ax > 0.4142135623730950
    z_big = -1.0 / jnp.where(big, ax, 1.0)
    z_mid = (ax - 1.0) / (ax + 1.0)
    z = jnp.where(big, z_big, jnp.where(mid, z_mid, ax))
    base = jnp.where(big, math.pi / 2, jnp.where(mid, math.pi / 4, 0.0))
    zz = z * z
    poly = (((8.05374449538e-2 * zz - 1.38776856032e-1) * zz + 1.99777106478e-1) * zz
            - 3.33329491539e-1) * zz * z + z
    r = base + poly
    return jnp.where(x < 0, -r, r)


def compute_step(means_ref, cur_ref, zlo_ref, zhi_ref, ylo_ref, yhi_ref, ct_ref, out_ref):
    nz, ny, nx = cur_ref.shape[1], cur_ref.shape[2], cur_ref.shape[3]
    shape = (ny, nx)
    xi = lax.broadcasted_iota(jnp.int32, shape, 1)
    yi = lax.broadcasted_iota(jnp.int32, shape, 0)
    xa = pltpu.roll(xi, 1, 1)
    xb = pltpu.roll(xi, nx - 1, 1)
    xa_ok = jnp.abs(xa - xi) == 1
    xb_ok = jnp.abs(xb - xi) == 1
    ya = pltpu.roll(yi, 1, 0)
    yb = pltpu.roll(yi, ny - 1, 0)
    ya_ok = jnp.abs(ya - yi) == 1
    yb_ok = jnp.abs(yb - yi) == 1
    low_row = yi == 0
    means = [means_ref[p] for p in range(PHASES)]
    for z in range(nz):
        picture = ct_ref[z]
        energy = []
        for p in range(PHASES):
            differ = picture - means[p]
            energy.append(differ * differ)
        phis, lap, g1, g0, dl = [], [], [], [], []
        for k in range(LEVELS):
            c = cur_ref[k, z]
            zm = zlo_ref[k] if z == 0 else cur_ref[k, z - 1]
            zp = zhi_ref[k] if z == nz - 1 else cur_ref[k, z + 1]
            edge = jnp.where(low_row, ylo_ref[k, z], yhi_ref[k, z])
            ym = jnp.where(ya_ok, pltpu.roll(c, 1, 0), edge)
            yp = jnp.where(yb_ok, pltpu.roll(c, ny - 1, 0), edge)
            xm = jnp.where(xa_ok, pltpu.roll(c, 1, 1), 0.0)
            xp = jnp.where(xb_ok, pltpu.roll(c, nx - 1, 1), 0.0)
            lap.append(zm + zp + ym + yp + xm + xp - 6.0 * c)
            h = 0.5 + arctan(c) / math.pi
            g1.append(h)
            g0.append(1.0 - h)
            dl.append(1.0 / (math.pi * (1.0 + c * c)))
            phis.append(c)
        g = (g0, g1)
        pair_lo = {(a, b): g[a][0] * g[b][1] for a in (0, 1) for b in (0, 1)}
        pair_hi = {(a, b): g[a][2] * g[b][3] for a in (0, 1) for b in (0, 1)}
        for k in range(LEVELS):
            force = None
            for q in range(PHASES // 2):
                low = q & ((1 << k) - 1)
                high = (q >> k) << (k + 1)
                p0 = high | low
                p1 = p0 | (1 << k)
                bits = [(p0 >> j) & 1 for j in range(LEVELS)]
                if k == 0:
                    prod = g[bits[1]][1] * pair_hi[(bits[2], bits[3])]
                elif k == 1:
                    prod = g[bits[0]][0] * pair_hi[(bits[2], bits[3])]
                elif k == 2:
                    prod = pair_lo[(bits[0], bits[1])] * g[bits[3]][3]
                else:
                    prod = pair_lo[(bits[0], bits[1])] * g[bits[2]][2]
                term = (energy[p1] - energy[p0]) * prod
                force = term if force is None else force + term
            out_ref[k, z] = phis[k] + STEP_SIZE * dl[k] * (lap[k] - force)


MESH = pl.DeviceIdType.MESH


def evolve_kernel(means_ref, cur_ref, ct_ref, out_ref, mid_ref, zlo_buf, zhi_buf, ylo_buf, yhi_buf,
                  send_sem, recv_sem):
    nz, ny = cur_ref.shape[1], cur_ref.shape[2]
    gz, gy = lax.axis_index("gz"), lax.axis_index("gy")
    n_gz, n_gy = lax.axis_size("gz"), lax.axis_size("gy")
    peers = [(gz > 0, (gz - 1, gy)), (gz < n_gz - 1, (gz + 1, gy)),
             (gy > 0, (gz, gy - 1)), (gy < n_gy - 1, (gz, gy + 1))]
    barrier = pltpu.get_barrier_semaphore()
    for present, dev in peers:
        @pl.when(present)
        def _(dev=dev):
            pl.semaphore_signal(barrier, inc=1, device_id=dev, device_id_type=MESH)
    count = sum(present.astype(jnp.int32) for present, _ in peers)
    pl.semaphore_wait(barrier, count)

    def exchange(step, src_ref):
        plan = [
            (gz < n_gz - 1, gz > 0, src_ref.at[:, nz - 1], zlo_buf.at[step], (gz + 1, gy)),
            (gz > 0, gz < n_gz - 1, src_ref.at[:, 0], zhi_buf.at[step], (gz - 1, gy)),
            (gy < n_gy - 1, gy > 0, src_ref.at[:, :, pl.ds(ny - 1, 1)], ylo_buf.at[step], (gz, gy + 1)),
            (gy > 0, gy < n_gy - 1, src_ref.at[:, :, pl.ds(0, 1)], yhi_buf.at[step], (gz, gy - 1)),
        ]
        copies = []
        for d, (sends, receives, src, dst, target) in enumerate(plan):
            copy = pltpu.make_async_remote_copy(
                src_ref=src, dst_ref=dst, send_sem=send_sem.at[step, d],
                recv_sem=recv_sem.at[step, d], device_id=target, device_id_type=MESH)

            @pl.when(sends)
            def _(copy=copy):
                copy.start()

            @pl.when(jnp.logical_not(receives))
            def _(dst=dst):
                dst[...] = jnp.zeros(dst.shape, jnp.float32)

            copies.append((sends, receives, copy))
        return copies

    def finish(copies):
        for sends, receives, copy in copies:
            @pl.when(receives)
            def _(copy=copy):
                copy.wait_recv()

    def drain(copies):
        for sends, receives, copy in copies:
            @pl.when(sends)
            def _(copy=copy):
                copy.wait_send()

    first = exchange(0, cur_ref)
    finish(first)
    compute_step(means_ref, cur_ref, zlo_buf.at[0], zhi_buf.at[0], ylo_buf.at[0], yhi_buf.at[0], ct_ref, mid_ref)
    drain(first)
    second = exchange(1, mid_ref)
    finish(second)
    compute_step(means_ref, mid_ref, zlo_buf.at[1], zhi_buf.at[1], ylo_buf.at[1], yhi_buf.at[1], ct_ref, out_ref)
    drain(second)


def evolve_all(current, picture, region_means):
    levels, nz, ny, nx = current.shape
    vmem = pl.BlockSpec(memory_space=pltpu.VMEM)
    f32 = jnp.float32
    return pl.pallas_call(
        evolve_kernel,
        out_shape=jax.ShapeDtypeStruct(current.shape, current.dtype),
        in_specs=[pl.BlockSpec(memory_space=pltpu.SMEM), vmem, vmem],
        out_specs=vmem,
        scratch_shapes=[
            pltpu.VMEM(current.shape, f32),
            pltpu.VMEM((2, levels, ny, nx), f32),
            pltpu.VMEM((2, levels, ny, nx), f32),
            pltpu.VMEM((2, levels, nz, 1, nx), f32),
            pltpu.VMEM((2, levels, nz, 1, nx), f32),
            pltpu.SemaphoreType.DMA((2, 4)),
            pltpu.SemaphoreType.DMA((2, 4)),
        ],
        compiler_params=pltpu.CompilerParams(collective_id=0, has_side_effects=True),
    )(region_means, current, picture)


def penalty_table(count, offset):
    distance = (np.arange(count, dtype=np.int32) - offset).astype(np.float32)
    table = np.where(np.abs(distance) <= KERNEL, np.float32(PENALTY) * (distance * distance), np.float32(np.inf))
    return jnp.asarray(table.astype(np.float32))


def scan_offsets(u_ref, pen_ref, out_ref, n_out, group, nrot, q_range, after_group=None):
    for g0 in range(0, n_out, group):
        q_lo, q_hi = q_range(g0, group)
        q_hi = min(q_hi, pen_ref.shape[0] // nrot - 1, u_ref.shape[1] - g0 - group)

        def body(q, acc, g0=g0):
            for r in range(nrot):
                vals = u_ref[r, pl.ds(g0 + q, group)]
                acc = jnp.minimum(acc, vals + pen_ref[q * nrot + r])
            return acc

        init = jnp.full((group,) + tuple(out_ref.shape[1:]), jnp.inf, jnp.float32)
        out_ref[g0:g0 + group] = lax.fori_loop(q_lo, q_hi + 1, body, init, unroll=2)
        if after_group is not None:
            after_group(g0, group)


def build_rotations(pad_ref, u_ref, nrot, pick, chunk=8):
    def body(i, carry):
        b0 = pl.multiple_of(i * chunk, chunk)
        here = pad_ref[pl.ds(b0, chunk)]
        after = pad_ref[pl.ds(b0 + 1, chunk)]
        u_ref[0, pl.ds(b0, chunk)] = here
        for r in range(1, nrot):
            u_ref[r, pl.ds(b0, chunk)] = pick(r, here, after)
        return carry

    lax.fori_loop(0, u_ref.shape[1] // chunk, body, 0)


def xpass_kernel(pen_ref, src_ref, out_ref, pad_ref, u_ref, after_group=None):
    lines, nx = src_ref.shape
    reach = KERNEL
    padc = reach // 8
    pad_ref[...] = jnp.full(pad_ref.shape, jnp.inf, jnp.float32)
    pad_ref[padc:padc + nx // 8] = src_ref[...].T.reshape(nx // 8, 8, lines)
    sub = lax.broadcasted_iota(jnp.int32, (8, 8, lines), 1)
    build_rotations(pad_ref, u_ref, 8, lambda r, here, after: jnp.where(
        sub < 8 - r, pltpu.roll(here, 8 - r, 1), pltpu.roll(after, 8 - r, 1)))
    n_out = nx // 8

    def q_range(g0, group):
        lo = max(0, -((8 * (g0 + group - 1) + 14 - reach) // 8))
        hi = (reach + nx - 1 - 8 * g0) // 8
        return lo, hi

    scan_offsets(u_ref, pen_ref, out_ref, n_out, 16, 8, q_range, after_group)


def transpose_kernel(src_ref, out_ref):
    out_ref[...] = src_ref[...].T


def local_call(kernel, out_shape, scratch, *args):
    vmem = pl.BlockSpec(memory_space=pltpu.VMEM)
    smem = pl.BlockSpec(memory_space=pltpu.SMEM)
    specs = [smem if a.ndim == 1 else vmem for a in args]
    return pl.pallas_call(
        kernel,
        out_shape=jax.ShapeDtypeStruct(out_shape, jnp.float32),
        in_specs=specs,
        out_specs=vmem,
        scratch_shapes=[pltpu.VMEM(s, jnp.float32) for s in scratch],
    )(*args)


def zy_kernel(pen_z_ref, pen_y_ref, src_ref, out_ref, pad_ref, u_ref, w_ref, before_y=None, after_group=None):
    n_out = src_ref.shape[0]
    padc = KERNEL // 4
    pad_ref[...] = jnp.full(pad_ref.shape, jnp.inf, jnp.float32)
    pad_ref[padc:padc + n_out] = src_ref[...]
    lane = lax.broadcasted_iota(jnp.int32, src_ref.shape[1:], 1)
    sub = lax.broadcasted_iota(jnp.int32, src_ref.shape[1:], 0)
    sub_z = (lane // 8) % 4
    sub_y = lane % 8

    lane3 = lax.broadcasted_iota(jnp.int32, (8,) + tuple(src_ref.shape[1:]), 2)
    sub_z3 = (lane3 // 8) % 4
    sub_y3 = lane3 % 8
    build_rotations(pad_ref, u_ref, 4, lambda r, here, after: jnp.where(
        sub_z3 + r < 4, pltpu.roll(here, 128 - 8 * r, 2), pltpu.roll(after, 32 - 8 * r, 2)))

    def q_range(g0, group):
        lo = max(0, padc - 1 - (g0 + group - 1))
        hi = padc + n_out - 1 - g0
        return lo, hi

    scan_offsets(u_ref, pen_z_ref, out_ref, n_out, 16, 4, q_range)

    def wbody(i, carry):
        a0 = pl.multiple_of(i * 8, 8)
        v = out_ref[pl.ds(a0, 8)]
        w_ref[0, pl.ds(a0, 8)] = v
        for r in range(1, 8):
            w_ref[r, pl.ds(a0, 8)] = jnp.where(sub_y3 + r < 8, pltpu.roll(v, 128 - r, 2),
                                               pltpu.roll(pltpu.roll(v, 8 - r, 2), 7, 1))
        return carry

    lax.fori_loop(0, n_out // 8, wbody, 0)
    if before_y is not None:
        before_y()
    group = 8
    shifts = []
    for db in range(-8, 8):
        for dy in range(8):
            carry_in = (sub_y + dy >= 8).astype(jnp.int32)
            row = sub + db + carry_in
            valid = (row >= 0) & (row <= 7)
            shifts.append((db, dy, valid))

    def ybody(i, carry):
        a0 = pl.multiple_of(i * group, group)
        acc = [jnp.full(src_ref.shape[1:], jnp.inf, jnp.float32) for _ in range(group)]
        for db, dy, valid in shifts:
            penvec = jnp.where(valid, pen_y_ref[8 * db + dy + 64], jnp.inf)
            for g in range(group):
                v = w_ref[dy, a0 + g]
                if db % 8:
                    v = pltpu.roll(v, (8 - db) % 8, 0)
                acc[g] = jnp.minimum(acc[g], v + penvec)
        for g in range(group):
            out_ref[a0 + g] = acc[g]
        if after_group is not None:
            after_group(a0, group)
        return carry

    lax.fori_loop(0, n_out // group, ybody, 0)


class Exchange:
    def __init__(self, mid_ref, recv_ref, sems, grp_sems, count):
        self.n_gz, self.n_gy = lax.axis_size("gz"), lax.axis_size("gy")
        self.a, self.b = lax.axis_index("gz"), lax.axis_index("gy")
        self.mid_ref, self.recv_ref, self.sems = mid_ref, recv_ref, sems
        self.grp_sems, self.count = grp_sems, count
        self.barrier = pltpu.get_barrier_semaphore()

    def greet(self):
        a, b, n_gz, n_gy = self.a, self.b, self.n_gz, self.n_gy

        def greet_gy(k, carry):
            pl.semaphore_signal(self.barrier, inc=1, device_id=(a, lax.rem(b + k, n_gy)),
                                device_id_type=MESH)
            return carry

        def greet_gz(k, carry):
            pl.semaphore_signal(self.barrier, inc=1, device_id=(lax.rem(a + k, n_gz), b),
                                device_id_type=MESH)
            return carry

        lax.fori_loop(1, n_gy, greet_gy, 0)
        lax.fori_loop(1, n_gz, greet_gz, 0)

    def wait_greetings(self):
        pl.semaphore_wait(self.barrier, self.n_gy - 1 + self.n_gz - 1)

    def send_rows(self, tiles_ref, g, t0):
        a, b, n_gy, count = self.a, self.b, self.n_gy, self.count
        for k in range(1, n_gy):
            p = lax.rem(b + k, n_gy)
            pltpu.make_async_remote_copy(
                src_ref=tiles_ref.at[pl.ds(t0, count), pl.ds(p, 1)],
                dst_ref=self.mid_ref.at[pl.ds(t0, count), pl.ds(b, 1)], send_sem=self.sems.at[0],
                recv_sem=self.grp_sems.at[g], device_id=(a, p), device_id_type=MESH).start()
        own = pltpu.make_async_copy(tiles_ref.at[pl.ds(t0, count), pl.ds(b, 1)],
                                    self.mid_ref.at[pl.ds(t0, count), pl.ds(b, 1)], self.sems.at[2])
        own.start()
        own.wait()

    def forward_group(self, g, t0):
        a, b, n_gy, count = self.a, self.b, self.n_gy, self.count
        pltpu.make_async_remote_copy(
            src_ref=self.mid_ref.at[pl.ds(t0, count), pl.ds(0, n_gy - 1)],
            dst_ref=self.mid_ref.at[pl.ds(t0, count), pl.ds(0, n_gy - 1)], send_sem=self.sems.at[0],
            recv_sem=self.grp_sems.at[g], device_id=(a, lax.rem(b + 1, n_gy)),
            device_id_type=MESH).wait_recv()
        for j in range(count):
            p = t0 + j

            @pl.when(p != a)
            def _(p=p):
                pltpu.make_async_remote_copy(
                    src_ref=self.mid_ref.at[pl.ds(p, 1)], dst_ref=self.recv_ref.at[pl.ds(a, 1)],
                    send_sem=self.sems.at[3], recv_sem=self.sems.at[4], device_id=(p, b),
                    device_id_type=MESH).start()

    def finish(self, tiles_ref, out_ref, pending, transpose=False):
        a, b, n_gz, n_gy = self.a, self.b, self.n_gz, self.n_gy
        mid_ref, recv_ref, sems = self.mid_ref, self.recv_ref, self.sems
        groups = n_gz // self.count
        for g in range(groups - pending, groups):
            self.forward_group(g, g * self.count)
        pltpu.make_async_remote_copy(
            src_ref=tiles_ref.at[:, pl.ds(0, n_gy - 1)], dst_ref=mid_ref.at[:, pl.ds(0, n_gy - 1)],
            send_sem=sems.at[0], recv_sem=sems.at[1], device_id=(a, lax.rem(b + 1, n_gy)),
            device_id_type=MESH).wait_send()
        own = pltpu.make_async_copy(mid_ref.at[pl.ds(a, 1)], recv_ref.at[pl.ds(a, 1)], sems.at[5])
        own.start()
        own.wait()
        total = pltpu.make_async_remote_copy(
            src_ref=mid_ref.at[pl.ds(0, n_gz - 1)], dst_ref=recv_ref.at[pl.ds(0, n_gz - 1)],
            send_sem=sems.at[3], recv_sem=sems.at[4], device_id=(lax.rem(a + 1, n_gz), b),
            device_id_type=MESH)
        total.wait_recv()
        total.wait_send()
        if transpose:
            out_ref[...] = recv_ref[...].reshape(out_ref.shape[::-1]).T
        else:
            out_ref[...] = recv_ref[...]


def n_gz_groups(ex):
    return ex.n_gz // ex.count


def exchange_scratch(tiles_shape, groups):
    return [pltpu.VMEM(tiles_shape, jnp.float32)] * 3 + [pltpu.SemaphoreType.DMA((6,)),
                                                         pltpu.SemaphoreType.DMA((groups,))]


def xpass_send_kernel(pen_ref, src_ref, out_ref, pad_ref, u_ref, tiles_ref, mid_ref, recv_ref, sems, grp_sems):
    ex = Exchange(mid_ref, recv_ref, sems, grp_sems, 16)
    ex.greet()

    def after_group(g0, group):
        assert group == ex.count
        g = g0 // group
        if g == 0:
            ex.wait_greetings()
        ex.send_rows(tiles_ref, g, g0)
        if g >= 1:
            ex.forward_group(g - 1, g0 - group)

    xpass_kernel(pen_ref, src_ref, tiles_ref, pad_ref, u_ref, after_group)
    ex.finish(tiles_ref, out_ref, 1)


def zy_send_kernel(pen_z_ref, pen_y_ref, src_ref, out_ref, pad_ref, u_ref, w_ref, tiles_ref, mid_ref,
                   recv_ref, sems, grp_sems):
    ex = Exchange(mid_ref, recv_ref, sems, grp_sems, 8)
    ex.greet()

    def after_group(a0, group):
        assert group == ex.count
        g = a0 // group
        ex.send_rows(tiles_ref, g, a0)

    zy_kernel(pen_z_ref, pen_y_ref, src_ref, tiles_ref, pad_ref, u_ref, w_ref, ex.wait_greetings, after_group)
    ex.finish(tiles_ref, out_ref, n_gz_groups(ex), transpose=True)


def regularize(current):
    levels, nz, ny, nx = current.shape
    lines = levels * nz * ny
    n_gz = lax.axis_size("gz")
    n_gy = lax.axis_size("gy")
    assert lines == 128 and ny == 8 and n_gy == 8 and n_gz * n_gy == nx
    smem = pl.BlockSpec(memory_space=pltpu.SMEM)
    vmem = pl.BlockSpec(memory_space=pltpu.VMEM)
    tiles = (n_gz, n_gy, lines)
    xq = (KERNEL + 7) // 8
    nxo = nx // 8
    pen_x = penalty_table(8 * (xq * 2 + 2), KERNEL)
    xu = -(-(nxo + 2 * xq + 2) // 8) * 8
    r1 = pl.pallas_call(
        xpass_send_kernel,
        out_shape=jax.ShapeDtypeStruct(tiles, jnp.float32),
        in_specs=[smem, vmem],
        out_specs=vmem,
        scratch_shapes=[pltpu.VMEM((xu + 8, 8, lines), jnp.float32),
                        pltpu.VMEM((8, xu, 8, lines), jnp.float32)] + exchange_scratch(tiles, n_gz // 16),
        compiler_params=pltpu.CompilerParams(collective_id=1, has_side_effects=True),
    )(pen_x, current.reshape(lines, nx))
    zq = KERNEL // 4
    pen_z = penalty_table(4 * (2 * zq + 2), KERNEL)
    zu = -(-(n_gz + 2 * zq + 2) // 8) * 8
    pen_y = penalty_table(8 * 2 * n_gy, 8 * n_gy)
    r2 = pl.pallas_call(
        zy_send_kernel,
        out_shape=jax.ShapeDtypeStruct((lines, nx), jnp.float32),
        in_specs=[smem, smem, vmem],
        out_specs=vmem,
        scratch_shapes=[pltpu.VMEM((zu + 8, 8, lines), jnp.float32),
                        pltpu.VMEM((4, zu, 8, lines), jnp.float32),
                        pltpu.VMEM((8, n_gz, 8, lines), jnp.float32)] + exchange_scratch(tiles, n_gz // 8),
        compiler_params=pltpu.CompilerParams(collective_id=2, has_side_effects=True),
    )(pen_z, pen_y, r1)
    return r2.reshape(current.shape)


def body(levels, ct_image, region_means):
    current = evolve_all(levels, ct_image, region_means)
    return (current, regularize(current))


def solution(mesh):
    return jax.shard_map(
        body,
        mesh=mesh,
        in_specs=(P(None, "gz", "gy", None), P("gz", "gy", None), P()),
        out_specs=(P(None, "gz", "gy", None), P(None, "gz", "gy", None)),
        check_vma=False,
    )
```

```python
import functools
import math

import jax
import numpy as np
import jax.numpy as jnp
from jax import lax
from jax.experimental import pallas as pl
from jax.experimental.pallas import tpu as pltpu
from jax.sharding import PartitionSpec as P

LEVELS = 4
PHASES = 16
UPDATES = 2
KERNEL = 200


PENALTY = 0.0005
STEP_SIZE = 0.5


def arctan(x):
    ax = jnp.abs(x)
    big = ax > 2.414213562373095
    mid = ax > 0.4142135623730950
    z_big = -1.0 / jnp.where(big, ax, 1.0)
    z_mid = (ax - 1.0) / (ax + 1.0)
    z = jnp.where(big, z_big, jnp.where(mid, z_mid, ax))
    base = jnp.where(big, math.pi / 2, jnp.where(mid, math.pi / 4, 0.0))
    zz = z * z
    poly = (((8.05374449538e-2 * zz - 1.38776856032e-1) * zz + 1.99777106478e-1) * zz
            - 3.33329491539e-1) * zz * z + z
    r = base + poly
    return jnp.where(x < 0, -r, r)


def compute_step(means_ref, cur_ref, zlo_ref, zhi_ref, ylo_ref, yhi_ref, ct_ref, out_ref):
    nz, ny, nx = cur_ref.shape[1], cur_ref.shape[2], cur_ref.shape[3]
    shape = (ny, nx)
    xi = lax.broadcasted_iota(jnp.int32, shape, 1)
    yi = lax.broadcasted_iota(jnp.int32, shape, 0)
    xa = pltpu.roll(xi, 1, 1)
    xb = pltpu.roll(xi, nx - 1, 1)
    xa_ok = jnp.abs(xa - xi) == 1
    xb_ok = jnp.abs(xb - xi) == 1
    ya = pltpu.roll(yi, 1, 0)
    yb = pltpu.roll(yi, ny - 1, 0)
    ya_ok = jnp.abs(ya - yi) == 1
    yb_ok = jnp.abs(yb - yi) == 1
    low_row = yi == 0
    means = [means_ref[p] for p in range(PHASES)]
    for z in range(nz):
        picture = ct_ref[z]
        energy = []
        for p in range(PHASES):
            differ = picture - means[p]
            energy.append(differ * differ)
        phis, lap, g1, g0, dl = [], [], [], [], []
        for k in range(LEVELS):
            c = cur_ref[k, z]
            zm = zlo_ref[k] if z == 0 else cur_ref[k, z - 1]
            zp = zhi_ref[k] if z == nz - 1 else cur_ref[k, z + 1]
            edge = jnp.where(low_row, ylo_ref[k, z], yhi_ref[k, z])
            ym = jnp.where(ya_ok, pltpu.roll(c, 1, 0), edge)
            yp = jnp.where(yb_ok, pltpu.roll(c, ny - 1, 0), edge)
            xm = jnp.where(xa_ok, pltpu.roll(c, 1, 1), 0.0)
            xp = jnp.where(xb_ok, pltpu.roll(c, nx - 1, 1), 0.0)
            lap.append(zm + zp + ym + yp + xm + xp - 6.0 * c)
            h = 0.5 + arctan(c) / math.pi
            g1.append(h)
            g0.append(1.0 - h)
            dl.append(1.0 / (math.pi * (1.0 + c * c)))
            phis.append(c)
        g = (g0, g1)
        pair_lo = {(a, b): g[a][0] * g[b][1] for a in (0, 1) for b in (0, 1)}
        pair_hi = {(a, b): g[a][2] * g[b][3] for a in (0, 1) for b in (0, 1)}
        for k in range(LEVELS):
            force = None
            for q in range(PHASES // 2):
                low = q & ((1 << k) - 1)
                high = (q >> k) << (k + 1)
                p0 = high | low
                p1 = p0 | (1 << k)
                bits = [(p0 >> j) & 1 for j in range(LEVELS)]
                if k == 0:
                    prod = g[bits[1]][1] * pair_hi[(bits[2], bits[3])]
                elif k == 1:
                    prod = g[bits[0]][0] * pair_hi[(bits[2], bits[3])]
                elif k == 2:
                    prod = pair_lo[(bits[0], bits[1])] * g[bits[3]][3]
                else:
                    prod = pair_lo[(bits[0], bits[1])] * g[bits[2]][2]
                term = (energy[p1] - energy[p0]) * prod
                force = term if force is None else force + term
            out_ref[k, z] = phis[k] + STEP_SIZE * dl[k] * (lap[k] - force)


MESH = pl.DeviceIdType.MESH


def evolve_kernel(means_ref, cur_ref, ct_ref, out_ref, mid_ref, zlo_buf, zhi_buf, ylo_buf, yhi_buf,
                  send_sem, recv_sem):
    nz, ny = cur_ref.shape[1], cur_ref.shape[2]
    gz, gy = lax.axis_index("gz"), lax.axis_index("gy")
    n_gz, n_gy = lax.axis_size("gz"), lax.axis_size("gy")
    peers = [(gz > 0, (gz - 1, gy)), (gz < n_gz - 1, (gz + 1, gy)),
             (gy > 0, (gz, gy - 1)), (gy < n_gy - 1, (gz, gy + 1))]
    barrier = pltpu.get_barrier_semaphore()
    for present, dev in peers:
        @pl.when(present)
        def _(dev=dev):
            pl.semaphore_signal(barrier, inc=1, device_id=dev, device_id_type=MESH)
    count = sum(present.astype(jnp.int32) for present, _ in peers)
    pl.semaphore_wait(barrier, count)

    def exchange(step, src_ref):
        plan = [
            (gz < n_gz - 1, gz > 0, src_ref.at[:, nz - 1], zlo_buf.at[step], (gz + 1, gy)),
            (gz > 0, gz < n_gz - 1, src_ref.at[:, 0], zhi_buf.at[step], (gz - 1, gy)),
            (gy < n_gy - 1, gy > 0, src_ref.at[:, :, pl.ds(ny - 1, 1)], ylo_buf.at[step], (gz, gy + 1)),
            (gy > 0, gy < n_gy - 1, src_ref.at[:, :, pl.ds(0, 1)], yhi_buf.at[step], (gz, gy - 1)),
        ]
        copies = []
        for d, (sends, receives, src, dst, target) in enumerate(plan):
            copy = pltpu.make_async_remote_copy(
                src_ref=src, dst_ref=dst, send_sem=send_sem.at[step, d],
                recv_sem=recv_sem.at[step, d], device_id=target, device_id_type=MESH)

            @pl.when(sends)
            def _(copy=copy):
                copy.start()

            @pl.when(jnp.logical_not(receives))
            def _(dst=dst):
                dst[...] = jnp.zeros(dst.shape, jnp.float32)

            copies.append((sends, receives, copy))
        return copies

    def finish(copies):
        for sends, receives, copy in copies:
            @pl.when(receives)
            def _(copy=copy):
                copy.wait_recv()

    def drain(copies):
        for sends, receives, copy in copies:
            @pl.when(sends)
            def _(copy=copy):
                copy.wait_send()

    first = exchange(0, cur_ref)
    finish(first)
    compute_step(means_ref, cur_ref, zlo_buf.at[0], zhi_buf.at[0], ylo_buf.at[0], yhi_buf.at[0], ct_ref, mid_ref)
    drain(first)
    second = exchange(1, mid_ref)
    finish(second)
    compute_step(means_ref, mid_ref, zlo_buf.at[1], zhi_buf.at[1], ylo_buf.at[1], yhi_buf.at[1], ct_ref, out_ref)
    drain(second)


def evolve_all(current, picture, region_means):
    levels, nz, ny, nx = current.shape
    vmem = pl.BlockSpec(memory_space=pltpu.VMEM)
    f32 = jnp.float32
    return pl.pallas_call(
        evolve_kernel,
        out_shape=jax.ShapeDtypeStruct(current.shape, current.dtype),
        in_specs=[pl.BlockSpec(memory_space=pltpu.SMEM), vmem, vmem],
        out_specs=vmem,
        scratch_shapes=[
            pltpu.VMEM(current.shape, f32),
            pltpu.VMEM((2, levels, ny, nx), f32),
            pltpu.VMEM((2, levels, ny, nx), f32),
            pltpu.VMEM((2, levels, nz, 1, nx), f32),
            pltpu.VMEM((2, levels, nz, 1, nx), f32),
            pltpu.SemaphoreType.DMA((2, 4)),
            pltpu.SemaphoreType.DMA((2, 4)),
        ],
        compiler_params=pltpu.CompilerParams(collective_id=0, has_side_effects=True),
    )(region_means, current, picture)


def penalty_table(count, offset):
    distance = (np.arange(count, dtype=np.int32) - offset).astype(np.float32)
    table = np.where(np.abs(distance) <= KERNEL, np.float32(PENALTY) * (distance * distance), np.float32(np.inf))
    return jnp.asarray(table.astype(np.float32))


def scan_offsets(u_ref, pen_ref, out_ref, n_out, group, nrot, q_range, after_group=None):
    for g0 in range(0, n_out, group):
        q_lo, q_hi = q_range(g0, group)
        q_hi = min(q_hi, pen_ref.shape[0] // nrot - 1, u_ref.shape[1] - g0 - group)

        def body(q, acc, g0=g0):
            for r in range(nrot):
                vals = u_ref[r, pl.ds(g0 + q, group)]
                acc = jnp.minimum(acc, vals + pen_ref[q * nrot + r])
            return acc

        init = jnp.full((group,) + tuple(out_ref.shape[1:]), jnp.inf, jnp.float32)
        out_ref[g0:g0 + group] = lax.fori_loop(q_lo, q_hi + 1, body, init, unroll=2)
        if after_group is not None:
            after_group(g0, group)


def build_rotations(pad_ref, u_ref, nrot, pick, chunk=8):
    def body(i, carry):
        b0 = pl.multiple_of(i * chunk, chunk)
        here = pad_ref[pl.ds(b0, chunk)]
        after = pad_ref[pl.ds(b0 + 1, chunk)]
        u_ref[0, pl.ds(b0, chunk)] = here
        for r in range(1, nrot):
            u_ref[r, pl.ds(b0, chunk)] = pick(r, here, after)
        return carry

    lax.fori_loop(0, u_ref.shape[1] // chunk, body, 0)


def xpass_kernel(pen_ref, src_ref, out_ref, pad_ref, u_ref, after_group=None):
    lines, nx = src_ref.shape
    reach = KERNEL
    padc = reach // 8
    pad_ref[...] = jnp.full(pad_ref.shape, jnp.inf, jnp.float32)
    pad_ref[padc:padc + nx // 8] = src_ref[...].T.reshape(nx // 8, 8, lines)
    sub = lax.broadcasted_iota(jnp.int32, (8, 8, lines), 1)
    build_rotations(pad_ref, u_ref, 8, lambda r, here, after: jnp.where(
        sub < 8 - r, pltpu.roll(here, 8 - r, 1), pltpu.roll(after, 8 - r, 1)))
    n_out = nx // 8

    def q_range(g0, group):
        lo = max(0, -((8 * (g0 + group - 1) + 14 - reach) // 8))
        hi = (reach + nx - 1 - 8 * g0) // 8
        return lo, hi

    scan_offsets(u_ref, pen_ref, out_ref, n_out, 16, 8, q_range, after_group)


def transpose_kernel(src_ref, out_ref):
    out_ref[...] = src_ref[...].T


def local_call(kernel, out_shape, scratch, *args):
    vmem = pl.BlockSpec(memory_space=pltpu.VMEM)
    smem = pl.BlockSpec(memory_space=pltpu.SMEM)
    specs = [smem if a.ndim == 1 else vmem for a in args]
    return pl.pallas_call(
        kernel,
        out_shape=jax.ShapeDtypeStruct(out_shape, jnp.float32),
        in_specs=specs,
        out_specs=vmem,
        scratch_shapes=[pltpu.VMEM(s, jnp.float32) for s in scratch],
    )(*args)


def zy_kernel(pen_z_ref, pen_y_ref, src_ref, out_ref, pad_ref, u_ref, w_ref, before_y=None, after_group=None):
    n_out = src_ref.shape[0]
    padc = KERNEL // 4
    pad_ref[...] = jnp.full(pad_ref.shape, jnp.inf, jnp.float32)
    pad_ref[padc:padc + n_out] = src_ref[...]
    lane = lax.broadcasted_iota(jnp.int32, src_ref.shape[1:], 1)
    sub = lax.broadcasted_iota(jnp.int32, src_ref.shape[1:], 0)
    sub_z = (lane // 8) % 4
    sub_y = lane % 8

    lane3 = lax.broadcasted_iota(jnp.int32, (8,) + tuple(src_ref.shape[1:]), 2)
    sub_z3 = (lane3 // 8) % 4
    sub_y3 = lane3 % 8
    build_rotations(pad_ref, u_ref, 4, lambda r, here, after: jnp.where(
        sub_z3 + r < 4, pltpu.roll(here, 128 - 8 * r, 2), pltpu.roll(after, 32 - 8 * r, 2)))

    def q_range(g0, group):
        lo = max(0, padc - 1 - (g0 + group - 1))
        hi = padc + n_out - 1 - g0
        return lo, hi

    scan_offsets(u_ref, pen_z_ref, out_ref, n_out, 16, 4, q_range)

    def wbody(i, carry):
        a0 = pl.multiple_of(i * 8, 8)
        v = out_ref[pl.ds(a0, 8)]
        w_ref[0, pl.ds(a0, 8)] = v
        for r in range(1, 8):
            w_ref[r, pl.ds(a0, 8)] = jnp.where(sub_y3 + r < 8, pltpu.roll(v, 128 - r, 2),
                                               pltpu.roll(pltpu.roll(v, 8 - r, 2), 7, 1))
        return carry

    lax.fori_loop(0, n_out // 8, wbody, 0)
    if before_y is not None:
        before_y()
    group = 8
    shifts = []
    for db in range(-8, 8):
        for dy in range(8):
            carry_in = (sub_y + dy >= 8).astype(jnp.int32)
            row = sub + db + carry_in
            valid = (row >= 0) & (row <= 7)
            shifts.append((db, dy, valid))

    def ybody(i, carry):
        a0 = pl.multiple_of(i * group, group)
        acc = [jnp.full(src_ref.shape[1:], jnp.inf, jnp.float32) for _ in range(group)]
        for db, dy, valid in shifts:
            penvec = jnp.where(valid, pen_y_ref[8 * db + dy + 64], jnp.inf)
            for g in range(group):
                v = w_ref[dy, a0 + g]
                if db % 8:
                    v = pltpu.roll(v, (8 - db) % 8, 0)
                acc[g] = jnp.minimum(acc[g], v + penvec)
        for g in range(group):
            out_ref[a0 + g] = acc[g]
        if after_group is not None:
            after_group(a0, group)
        return carry

    lax.fori_loop(0, n_out // group, ybody, 0)


class Exchange:
    def __init__(self, mid_ref, recv_ref, sems, grp_sems, count):
        self.n_gz, self.n_gy = lax.axis_size("gz"), lax.axis_size("gy")
        self.a, self.b = lax.axis_index("gz"), lax.axis_index("gy")
        self.mid_ref, self.recv_ref, self.sems = mid_ref, recv_ref, sems
        self.grp_sems, self.count = grp_sems, count
        self.barrier = pltpu.get_barrier_semaphore()

    def greet(self):
        a, b, n_gz, n_gy = self.a, self.b, self.n_gz, self.n_gy

        def greet_gy(k, carry):
            pl.semaphore_signal(self.barrier, inc=1, device_id=(a, lax.rem(b + k, n_gy)),
                                device_id_type=MESH)
            return carry

        def greet_gz(k, carry):
            pl.semaphore_signal(self.barrier, inc=1, device_id=(lax.rem(a + k, n_gz), b),
                                device_id_type=MESH)
            return carry

        lax.fori_loop(1, n_gy, greet_gy, 0)
        lax.fori_loop(1, n_gz, greet_gz, 0)

    def wait_greetings(self):
        pl.semaphore_wait(self.barrier, self.n_gy - 1 + self.n_gz - 1)

    def send_rows(self, tiles_ref, g, t0):
        a, b, n_gy, count = self.a, self.b, self.n_gy, self.count
        for k in range(1, n_gy):
            p = lax.rem(b + k, n_gy)
            pltpu.make_async_remote_copy(
                src_ref=tiles_ref.at[pl.ds(t0, count), pl.ds(p, 1)],
                dst_ref=self.mid_ref.at[pl.ds(t0, count), pl.ds(b, 1)], send_sem=self.sems.at[0],
                recv_sem=self.grp_sems.at[g], device_id=(a, p), device_id_type=MESH).start()
        own = pltpu.make_async_copy(tiles_ref.at[pl.ds(t0, count), pl.ds(b, 1)],
                                    self.mid_ref.at[pl.ds(t0, count), pl.ds(b, 1)], self.sems.at[2])
        own.start()
        own.wait()

    def forward_group(self, g, t0):
        a, b, n_gy, count = self.a, self.b, self.n_gy, self.count
        pltpu.make_async_remote_copy(
            src_ref=self.mid_ref.at[pl.ds(t0, count), pl.ds(0, n_gy - 1)],
            dst_ref=self.mid_ref.at[pl.ds(t0, count), pl.ds(0, n_gy - 1)], send_sem=self.sems.at[0],
            recv_sem=self.grp_sems.at[g], device_id=(a, lax.rem(b + 1, n_gy)),
            device_id_type=MESH).wait_recv()
        for j in range(count):
            p = t0 + j

            @pl.when(p != a)
            def _(p=p):
                pltpu.make_async_remote_copy(
                    src_ref=self.mid_ref.at[pl.ds(p, 1)], dst_ref=self.recv_ref.at[pl.ds(a, 1)],
                    send_sem=self.sems.at[3], recv_sem=self.sems.at[4], device_id=(p, b),
                    device_id_type=MESH).start()

    def finish(self, tiles_ref, out_ref, pending, transpose=False):
        a, b, n_gz, n_gy = self.a, self.b, self.n_gz, self.n_gy
        mid_ref, recv_ref, sems = self.mid_ref, self.recv_ref, self.sems
        groups = n_gz // self.count
        if pending < groups:
            for g in range(groups - pending, groups):
                self.forward_group(g, g * self.count)
        else:
            for g in range(groups):
                t0 = g * self.count
                pltpu.make_async_remote_copy(
                    src_ref=mid_ref.at[pl.ds(t0, self.count), pl.ds(0, n_gy - 1)],
                    dst_ref=mid_ref.at[pl.ds(t0, self.count), pl.ds(0, n_gy - 1)], send_sem=sems.at[0],
                    recv_sem=self.grp_sems.at[g], device_id=(a, lax.rem(b + 1, n_gy)),
                    device_id_type=MESH).wait_recv()

            def send(k, carry):
                p = lax.rem(a + k, n_gz)
                pltpu.make_async_remote_copy(
                    src_ref=mid_ref.at[pl.ds(p, 1)], dst_ref=recv_ref.at[pl.ds(a, 1)], send_sem=sems.at[3],
                    recv_sem=sems.at[4], device_id=(p, b), device_id_type=MESH).start()
                return carry

            lax.fori_loop(1, n_gz, send, 0, unroll=4)
        pltpu.make_async_remote_copy(
            src_ref=tiles_ref.at[:, pl.ds(0, n_gy - 1)], dst_ref=mid_ref.at[:, pl.ds(0, n_gy - 1)],
            send_sem=sems.at[0], recv_sem=sems.at[1], device_id=(a, lax.rem(b + 1, n_gy)),
            device_id_type=MESH).wait_send()
        own = pltpu.make_async_copy(mid_ref.at[pl.ds(a, 1)], recv_ref.at[pl.ds(a, 1)], sems.at[5])
        own.start()
        own.wait()
        total = pltpu.make_async_remote_copy(
            src_ref=mid_ref.at[pl.ds(0, n_gz - 1)], dst_ref=recv_ref.at[pl.ds(0, n_gz - 1)],
            send_sem=sems.at[3], recv_sem=sems.at[4], device_id=(lax.rem(a + 1, n_gz), b),
            device_id_type=MESH)
        total.wait_recv()
        total.wait_send()
        if transpose:
            out_ref[...] = recv_ref[...].reshape(out_ref.shape[::-1]).T
        else:
            out_ref[...] = recv_ref[...]


def n_gz_groups(ex):
    return ex.n_gz // ex.count


def exchange_scratch(tiles_shape, groups):
    return [pltpu.VMEM(tiles_shape, jnp.float32)] * 3 + [pltpu.SemaphoreType.DMA((6,)),
                                                         pltpu.SemaphoreType.DMA((groups,))]


def xpass_send_kernel(pen_ref, src_ref, out_ref, pad_ref, u_ref, tiles_ref, mid_ref, recv_ref, sems, grp_sems):
    ex = Exchange(mid_ref, recv_ref, sems, grp_sems, 16)
    ex.greet()

    def after_group(g0, group):
        assert group == ex.count
        g = g0 // group
        if g == 0:
            ex.wait_greetings()
        ex.send_rows(tiles_ref, g, g0)
        if g >= 1:
            ex.forward_group(g - 1, g0 - group)

    xpass_kernel(pen_ref, src_ref, tiles_ref, pad_ref, u_ref, after_group)
    ex.finish(tiles_ref, out_ref, 1)


def zy_send_kernel(pen_z_ref, pen_y_ref, src_ref, out_ref, pad_ref, u_ref, w_ref, tiles_ref, mid_ref,
                   recv_ref, sems, grp_sems):
    ex = Exchange(mid_ref, recv_ref, sems, grp_sems, 8)
    ex.greet()

    def after_group(a0, group):
        assert group == ex.count
        g = a0 // group
        ex.send_rows(tiles_ref, g, a0)

    zy_kernel(pen_z_ref, pen_y_ref, src_ref, tiles_ref, pad_ref, u_ref, w_ref, ex.wait_greetings, after_group)
    ex.finish(tiles_ref, out_ref, n_gz_groups(ex), transpose=True)


def regularize(current):
    levels, nz, ny, nx = current.shape
    lines = levels * nz * ny
    n_gz = lax.axis_size("gz")
    n_gy = lax.axis_size("gy")
    assert lines == 128 and ny == 8 and n_gy == 8 and n_gz * n_gy == nx
    smem = pl.BlockSpec(memory_space=pltpu.SMEM)
    vmem = pl.BlockSpec(memory_space=pltpu.VMEM)
    tiles = (n_gz, n_gy, lines)
    xq = (KERNEL + 7) // 8
    nxo = nx // 8
    pen_x = penalty_table(8 * (xq * 2 + 2), KERNEL)
    xu = -(-(nxo + 2 * xq + 2) // 8) * 8
    r1 = pl.pallas_call(
        xpass_send_kernel,
        out_shape=jax.ShapeDtypeStruct(tiles, jnp.float32),
        in_specs=[smem, vmem],
        out_specs=vmem,
        scratch_shapes=[pltpu.VMEM((xu + 8, 8, lines), jnp.float32),
                        pltpu.VMEM((8, xu, 8, lines), jnp.float32)] + exchange_scratch(tiles, n_gz // 16),
        compiler_params=pltpu.CompilerParams(collective_id=1, has_side_effects=True),
    )(pen_x, current.reshape(lines, nx))
    zq = KERNEL // 4
    pen_z = penalty_table(4 * (2 * zq + 2), KERNEL)
    zu = -(-(n_gz + 2 * zq + 2) // 8) * 8
    pen_y = penalty_table(8 * 2 * n_gy, 8 * n_gy)
    r2 = pl.pallas_call(
        zy_send_kernel,
        out_shape=jax.ShapeDtypeStruct((lines, nx), jnp.float32),
        in_specs=[smem, smem, vmem],
        out_specs=vmem,
        scratch_shapes=[pltpu.VMEM((zu + 8, 8, lines), jnp.float32),
                        pltpu.VMEM((4, zu, 8, lines), jnp.float32),
                        pltpu.VMEM((8, n_gz, 8, lines), jnp.float32)] + exchange_scratch(tiles, n_gz // 8),
        compiler_params=pltpu.CompilerParams(collective_id=2, has_side_effects=True),
    )(pen_z, pen_y, r1)
    return r2.reshape(current.shape)


def body(levels, ct_image, region_means):
    current = evolve_all(levels, ct_image, region_means)
    return (current, regularize(current))


def solution(mesh):
    return jax.shard_map(
        body,
        mesh=mesh,
        in_specs=(P(None, "gz", "gy", None), P("gz", "gy", None), P()),
        out_specs=(P(None, "gz", "gy", None), P(None, "gz", "gy", None)),
        check_vma=False,
    )
```

```python
import functools
import math

import jax
import numpy as np
import jax.numpy as jnp
from jax import lax
from jax.experimental import pallas as pl
from jax.experimental.pallas import tpu as pltpu
from jax.sharding import PartitionSpec as P

LEVELS = 4
PHASES = 16
UPDATES = 2
KERNEL = 200


PENALTY = 0.0005
STEP_SIZE = 0.5


def arctan(x):
    ax = jnp.abs(x)
    big = ax > 2.414213562373095
    mid = ax > 0.4142135623730950
    z_big = -1.0 / jnp.where(big, ax, 1.0)
    z_mid = (ax - 1.0) / (ax + 1.0)
    z = jnp.where(big, z_big, jnp.where(mid, z_mid, ax))
    base = jnp.where(big, math.pi / 2, jnp.where(mid, math.pi / 4, 0.0))
    zz = z * z
    poly = (((8.05374449538e-2 * zz - 1.38776856032e-1) * zz + 1.99777106478e-1) * zz
            - 3.33329491539e-1) * zz * z + z
    r = base + poly
    return jnp.where(x < 0, -r, r)


def compute_step(means_ref, cur_ref, zlo_ref, zhi_ref, ylo_ref, yhi_ref, ct_ref, out_ref):
    nz, ny, nx = cur_ref.shape[1], cur_ref.shape[2], cur_ref.shape[3]
    shape = (ny, nx)
    xi = lax.broadcasted_iota(jnp.int32, shape, 1)
    yi = lax.broadcasted_iota(jnp.int32, shape, 0)
    xa = pltpu.roll(xi, 1, 1)
    xb = pltpu.roll(xi, nx - 1, 1)
    xa_ok = jnp.abs(xa - xi) == 1
    xb_ok = jnp.abs(xb - xi) == 1
    ya = pltpu.roll(yi, 1, 0)
    yb = pltpu.roll(yi, ny - 1, 0)
    ya_ok = jnp.abs(ya - yi) == 1
    yb_ok = jnp.abs(yb - yi) == 1
    low_row = yi == 0
    means = [means_ref[p] for p in range(PHASES)]
    for z in range(nz):
        picture = ct_ref[z]
        energy = []
        for p in range(PHASES):
            differ = picture - means[p]
            energy.append(differ * differ)
        phis, lap, g1, g0, dl = [], [], [], [], []
        for k in range(LEVELS):
            c = cur_ref[k, z]
            zm = zlo_ref[k] if z == 0 else cur_ref[k, z - 1]
            zp = zhi_ref[k] if z == nz - 1 else cur_ref[k, z + 1]
            edge = jnp.where(low_row, ylo_ref[k, z], yhi_ref[k, z])
            ym = jnp.where(ya_ok, pltpu.roll(c, 1, 0), edge)
            yp = jnp.where(yb_ok, pltpu.roll(c, ny - 1, 0), edge)
            xm = jnp.where(xa_ok, pltpu.roll(c, 1, 1), 0.0)
            xp = jnp.where(xb_ok, pltpu.roll(c, nx - 1, 1), 0.0)
            lap.append(zm + zp + ym + yp + xm + xp - 6.0 * c)
            h = 0.5 + arctan(c) / math.pi
            g1.append(h)
            g0.append(1.0 - h)
            dl.append(1.0 / (math.pi * (1.0 + c * c)))
            phis.append(c)
        g = (g0, g1)
        pair_lo = {(a, b): g[a][0] * g[b][1] for a in (0, 1) for b in (0, 1)}
        pair_hi = {(a, b): g[a][2] * g[b][3] for a in (0, 1) for b in (0, 1)}
        for k in range(LEVELS):
            force = None
            for q in range(PHASES // 2):
                low = q & ((1 << k) - 1)
                high = (q >> k) << (k + 1)
                p0 = high | low
                p1 = p0 | (1 << k)
                bits = [(p0 >> j) & 1 for j in range(LEVELS)]
                if k == 0:
                    prod = g[bits[1]][1] * pair_hi[(bits[2], bits[3])]
                elif k == 1:
                    prod = g[bits[0]][0] * pair_hi[(bits[2], bits[3])]
                elif k == 2:
                    prod = pair_lo[(bits[0], bits[1])] * g[bits[3]][3]
                else:
                    prod = pair_lo[(bits[0], bits[1])] * g[bits[2]][2]
                term = (energy[p1] - energy[p0]) * prod
                force = term if force is None else force + term
            out_ref[k, z] = phis[k] + STEP_SIZE * dl[k] * (lap[k] - force)


MESH = pl.DeviceIdType.MESH


def evolve_kernel(means_ref, cur_ref, ct_ref, out_ref, mid_ref, zlo_buf, zhi_buf, ylo_buf, yhi_buf,
                  send_sem, recv_sem):
    nz, ny = cur_ref.shape[1], cur_ref.shape[2]
    gz, gy = lax.axis_index("gz"), lax.axis_index("gy")
    n_gz, n_gy = lax.axis_size("gz"), lax.axis_size("gy")
    peers = [(gz > 0, (gz - 1, gy)), (gz < n_gz - 1, (gz + 1, gy)),
             (gy > 0, (gz, gy - 1)), (gy < n_gy - 1, (gz, gy + 1))]
    barrier = pltpu.get_barrier_semaphore()
    for present, dev in peers:
        @pl.when(present)
        def _(dev=dev):
            pl.semaphore_signal(barrier, inc=1, device_id=dev, device_id_type=MESH)
    count = sum(present.astype(jnp.int32) for present, _ in peers)
    pl.semaphore_wait(barrier, count)

    def exchange(step, src_ref):
        plan = [
            (gz < n_gz - 1, gz > 0, src_ref.at[:, nz - 1], zlo_buf.at[step], (gz + 1, gy)),
            (gz > 0, gz < n_gz - 1, src_ref.at[:, 0], zhi_buf.at[step], (gz - 1, gy)),
            (gy < n_gy - 1, gy > 0, src_ref.at[:, :, pl.ds(ny - 1, 1)], ylo_buf.at[step], (gz, gy + 1)),
            (gy > 0, gy < n_gy - 1, src_ref.at[:, :, pl.ds(0, 1)], yhi_buf.at[step], (gz, gy - 1)),
        ]
        copies = []
        for d, (sends, receives, src, dst, target) in enumerate(plan):
            copy = pltpu.make_async_remote_copy(
                src_ref=src, dst_ref=dst, send_sem=send_sem.at[step, d],
                recv_sem=recv_sem.at[step, d], device_id=target, device_id_type=MESH)

            @pl.when(sends)
            def _(copy=copy):
                copy.start()

            @pl.when(jnp.logical_not(receives))
            def _(dst=dst):
                dst[...] = jnp.zeros(dst.shape, jnp.float32)

            copies.append((sends, receives, copy))
        return copies

    def finish(copies):
        for sends, receives, copy in copies:
            @pl.when(receives)
            def _(copy=copy):
                copy.wait_recv()

    def drain(copies):
        for sends, receives, copy in copies:
            @pl.when(sends)
            def _(copy=copy):
                copy.wait_send()

    first = exchange(0, cur_ref)
    finish(first)
    compute_step(means_ref, cur_ref, zlo_buf.at[0], zhi_buf.at[0], ylo_buf.at[0], yhi_buf.at[0], ct_ref, mid_ref)
    drain(first)
    second = exchange(1, mid_ref)
    finish(second)
    compute_step(means_ref, mid_ref, zlo_buf.at[1], zhi_buf.at[1], ylo_buf.at[1], yhi_buf.at[1], ct_ref, out_ref)
    drain(second)


def evolve_all(current, picture, region_means):
    levels, nz, ny, nx = current.shape
    vmem = pl.BlockSpec(memory_space=pltpu.VMEM)
    f32 = jnp.float32
    return pl.pallas_call(
        evolve_kernel,
        out_shape=jax.ShapeDtypeStruct(current.shape, current.dtype),
        in_specs=[pl.BlockSpec(memory_space=pltpu.SMEM), vmem, vmem],
        out_specs=vmem,
        scratch_shapes=[
            pltpu.VMEM(current.shape, f32),
            pltpu.VMEM((2, levels, ny, nx), f32),
            pltpu.VMEM((2, levels, ny, nx), f32),
            pltpu.VMEM((2, levels, nz, 1, nx), f32),
            pltpu.VMEM((2, levels, nz, 1, nx), f32),
            pltpu.SemaphoreType.DMA((2, 4)),
            pltpu.SemaphoreType.DMA((2, 4)),
        ],
        compiler_params=pltpu.CompilerParams(collective_id=0, has_side_effects=True),
    )(region_means, current, picture)


def penalty_table(count, offset):
    distance = (np.arange(count, dtype=np.int32) - offset).astype(np.float32)
    table = np.where(np.abs(distance) <= KERNEL, np.float32(PENALTY) * (distance * distance), np.float32(np.inf))
    return jnp.asarray(table.astype(np.float32))


def scan_offsets(u_ref, pen_ref, out_ref, n_out, group, nrot, q_range, after_group=None):
    for g0 in range(0, n_out, group):
        q_lo, q_hi = q_range(g0, group)
        q_hi = min(q_hi, pen_ref.shape[0] // nrot - 1, u_ref.shape[1] - g0 - group)

        def body(q, acc, g0=g0):
            for r in range(nrot):
                vals = u_ref[r, pl.ds(g0 + q, group)]
                acc = jnp.minimum(acc, vals + pen_ref[q * nrot + r])
            return acc

        init = jnp.full((group,) + tuple(out_ref.shape[1:]), jnp.inf, jnp.float32)
        out_ref[g0:g0 + group] = lax.fori_loop(q_lo, q_hi + 1, body, init, unroll=2)
        if after_group is not None:
            after_group(g0, group)


def build_rotations(pad_ref, u_ref, nrot, pick, chunk=8):
    def body(i, carry):
        b0 = pl.multiple_of(i * chunk, chunk)
        here = pad_ref[pl.ds(b0, chunk)]
        after = pad_ref[pl.ds(b0 + 1, chunk)]
        u_ref[0, pl.ds(b0, chunk)] = here
        for r in range(1, nrot):
            u_ref[r, pl.ds(b0, chunk)] = pick(r, here, after)
        return carry

    lax.fori_loop(0, u_ref.shape[1] // chunk, body, 0)


def xpass_kernel(pen_ref, src_ref, out_ref, pad_ref, u_ref, after_group=None):
    lines, nx = src_ref.shape
    reach = KERNEL
    padc = reach // 8
    pad_ref[...] = jnp.full(pad_ref.shape, jnp.inf, jnp.float32)
    pad_ref[padc:padc + nx // 8] = src_ref[...].T.reshape(nx // 8, 8, lines)
    sub = lax.broadcasted_iota(jnp.int32, (8, 8, lines), 1)
    build_rotations(pad_ref, u_ref, 8, lambda r, here, after: jnp.where(
        sub < 8 - r, pltpu.roll(here, 8 - r, 1), pltpu.roll(after, 8 - r, 1)))
    n_out = nx // 8

    def q_range(g0, group):
        lo = max(0, -((8 * (g0 + group - 1) + 14 - reach) // 8))
        hi = (reach + nx - 1 - 8 * g0) // 8
        return lo, hi

    scan_offsets(u_ref, pen_ref, out_ref, n_out, 8, 8, q_range, after_group)


def transpose_kernel(src_ref, out_ref):
    out_ref[...] = src_ref[...].T


def local_call(kernel, out_shape, scratch, *args):
    vmem = pl.BlockSpec(memory_space=pltpu.VMEM)
    smem = pl.BlockSpec(memory_space=pltpu.SMEM)
    specs = [smem if a.ndim == 1 else vmem for a in args]
    return pl.pallas_call(
        kernel,
        out_shape=jax.ShapeDtypeStruct(out_shape, jnp.float32),
        in_specs=specs,
        out_specs=vmem,
        scratch_shapes=[pltpu.VMEM(s, jnp.float32) for s in scratch],
    )(*args)


def zy_kernel(pen_z_ref, pen_y_ref, src_ref, out_ref, pad_ref, u_ref, w_ref, before_y=None, after_group=None):
    n_out = src_ref.shape[0]
    padc = KERNEL // 4
    pad_ref[...] = jnp.full(pad_ref.shape, jnp.inf, jnp.float32)
    pad_ref[padc:padc + n_out] = src_ref[...]
    lane = lax.broadcasted_iota(jnp.int32, src_ref.shape[1:], 1)
    sub = lax.broadcasted_iota(jnp.int32, src_ref.shape[1:], 0)
    sub_z = (lane // 8) % 4
    sub_y = lane % 8

    lane3 = lax.broadcasted_iota(jnp.int32, (8,) + tuple(src_ref.shape[1:]), 2)
    sub_z3 = (lane3 // 8) % 4
    sub_y3 = lane3 % 8
    build_rotations(pad_ref, u_ref, 4, lambda r, here, after: jnp.where(
        sub_z3 + r < 4, pltpu.roll(here, 128 - 8 * r, 2), pltpu.roll(after, 32 - 8 * r, 2)))

    def q_range(g0, group):
        lo = max(0, padc - 1 - (g0 + group - 1))
        hi = padc + n_out - 1 - g0
        return lo, hi

    scan_offsets(u_ref, pen_z_ref, out_ref, n_out, 16, 4, q_range)

    def wbody(i, carry):
        a0 = pl.multiple_of(i * 8, 8)
        v = out_ref[pl.ds(a0, 8)]
        w_ref[0, pl.ds(a0, 8)] = v
        for r in range(1, 8):
            w_ref[r, pl.ds(a0, 8)] = jnp.where(sub_y3 + r < 8, pltpu.roll(v, 128 - r, 2),
                                               pltpu.roll(pltpu.roll(v, 8 - r, 2), 7, 1))
        return carry

    lax.fori_loop(0, n_out // 8, wbody, 0)
    if before_y is not None:
        before_y()
    group = 8
    shifts = []
    for db in range(-8, 8):
        for dy in range(8):
            carry_in = (sub_y + dy >= 8).astype(jnp.int32)
            row = sub + db + carry_in
            valid = (row >= 0) & (row <= 7)
            shifts.append((db, dy, valid))

    def ybody(i, carry):
        a0 = pl.multiple_of(i * group, group)
        acc = [jnp.full(src_ref.shape[1:], jnp.inf, jnp.float32) for _ in range(group)]
        for db, dy, valid in shifts:
            penvec = jnp.where(valid, pen_y_ref[8 * db + dy + 64], jnp.inf)
            for g in range(group):
                v = w_ref[dy, a0 + g]
                if db % 8:
                    v = pltpu.roll(v, (8 - db) % 8, 0)
                acc[g] = jnp.minimum(acc[g], v + penvec)
        for g in range(group):
            out_ref[a0 + g] = acc[g]
        if after_group is not None:
            after_group(a0, group)
        return carry

    lax.fori_loop(0, n_out // group, ybody, 0)


class Exchange:
    def __init__(self, mid_ref, recv_ref, sems, grp_sems, count):
        self.n_gz, self.n_gy = lax.axis_size("gz"), lax.axis_size("gy")
        self.a, self.b = lax.axis_index("gz"), lax.axis_index("gy")
        self.mid_ref, self.recv_ref, self.sems = mid_ref, recv_ref, sems
        self.grp_sems, self.count = grp_sems, count
        self.barrier = pltpu.get_barrier_semaphore()

    def greet(self):
        a, b, n_gz, n_gy = self.a, self.b, self.n_gz, self.n_gy

        def greet_gy(k, carry):
            pl.semaphore_signal(self.barrier, inc=1, device_id=(a, lax.rem(b + k, n_gy)),
                                device_id_type=MESH)
            return carry

        def greet_gz(k, carry):
            pl.semaphore_signal(self.barrier, inc=1, device_id=(lax.rem(a + k, n_gz), b),
                                device_id_type=MESH)
            return carry

        lax.fori_loop(1, n_gy, greet_gy, 0)
        lax.fori_loop(1, n_gz, greet_gz, 0)

    def wait_greetings(self):
        pl.semaphore_wait(self.barrier, self.n_gy - 1 + self.n_gz - 1)

    def send_rows(self, tiles_ref, g, t0):
        a, b, n_gy, count = self.a, self.b, self.n_gy, self.count
        for k in range(1, n_gy):
            p = lax.rem(b + k, n_gy)
            pltpu.make_async_remote_copy(
                src_ref=tiles_ref.at[pl.ds(t0, count), pl.ds(p, 1)],
                dst_ref=self.mid_ref.at[pl.ds(t0, count), pl.ds(b, 1)], send_sem=self.sems.at[0],
                recv_sem=self.grp_sems.at[g], device_id=(a, p), device_id_type=MESH).start()
        own = pltpu.make_async_copy(tiles_ref.at[pl.ds(t0, count), pl.ds(b, 1)],
                                    self.mid_ref.at[pl.ds(t0, count), pl.ds(b, 1)], self.sems.at[2])
        own.start()
        own.wait()

    def forward_group(self, g, t0):
        a, b, n_gy, count = self.a, self.b, self.n_gy, self.count
        pltpu.make_async_remote_copy(
            src_ref=self.mid_ref.at[pl.ds(t0, count), pl.ds(0, n_gy - 1)],
            dst_ref=self.mid_ref.at[pl.ds(t0, count), pl.ds(0, n_gy - 1)], send_sem=self.sems.at[0],
            recv_sem=self.grp_sems.at[g], device_id=(a, lax.rem(b + 1, n_gy)),
            device_id_type=MESH).wait_recv()
        for j in range(count):
            p = t0 + j

            @pl.when(p != a)
            def _(p=p):
                pltpu.make_async_remote_copy(
                    src_ref=self.mid_ref.at[pl.ds(p, 1)], dst_ref=self.recv_ref.at[pl.ds(a, 1)],
                    send_sem=self.sems.at[3], recv_sem=self.sems.at[4], device_id=(p, b),
                    device_id_type=MESH).start()

    def finish(self, tiles_ref, out_ref, pending, transpose=False):
        a, b, n_gz, n_gy = self.a, self.b, self.n_gz, self.n_gy
        mid_ref, recv_ref, sems = self.mid_ref, self.recv_ref, self.sems
        groups = n_gz // self.count
        for g in range(groups - pending, groups):
            self.forward_group(g, g * self.count)
        pltpu.make_async_remote_copy(
            src_ref=tiles_ref.at[:, pl.ds(0, n_gy - 1)], dst_ref=mid_ref.at[:, pl.ds(0, n_gy - 1)],
            send_sem=sems.at[0], recv_sem=sems.at[1], device_id=(a, lax.rem(b + 1, n_gy)),
            device_id_type=MESH).wait_send()
        own = pltpu.make_async_copy(mid_ref.at[pl.ds(a, 1)], recv_ref.at[pl.ds(a, 1)], sems.at[5])
        own.start()
        own.wait()
        total = pltpu.make_async_remote_copy(
            src_ref=mid_ref.at[pl.ds(0, n_gz - 1)], dst_ref=recv_ref.at[pl.ds(0, n_gz - 1)],
            send_sem=sems.at[3], recv_sem=sems.at[4], device_id=(lax.rem(a + 1, n_gz), b),
            device_id_type=MESH)
        total.wait_recv()
        total.wait_send()
        if transpose:
            out_ref[...] = recv_ref[...].reshape(out_ref.shape[::-1]).T
        else:
            out_ref[...] = recv_ref[...]


def n_gz_groups(ex):
    return ex.n_gz // ex.count


def exchange_scratch(tiles_shape, groups):
    return [pltpu.VMEM(tiles_shape, jnp.float32)] * 3 + [pltpu.SemaphoreType.DMA((6,)),
                                                         pltpu.SemaphoreType.DMA((groups,))]


def xpass_send_kernel(pen_ref, src_ref, out_ref, pad_ref, u_ref, tiles_ref, mid_ref, recv_ref, sems, grp_sems):
    ex = Exchange(mid_ref, recv_ref, sems, grp_sems, 8)
    ex.greet()

    def after_group(g0, group):
        assert group == ex.count
        g = g0 // group
        if g == 0:
            ex.wait_greetings()
        ex.send_rows(tiles_ref, g, g0)
        if g >= 2:
            ex.forward_group(g - 2, g0 - 2 * group)

    xpass_kernel(pen_ref, src_ref, tiles_ref, pad_ref, u_ref, after_group)
    ex.finish(tiles_ref, out_ref, 2)


def zy_send_kernel(pen_z_ref, pen_y_ref, src_ref, out_ref, pad_ref, u_ref, w_ref, tiles_ref, mid_ref,
                   recv_ref, sems, grp_sems):
    ex = Exchange(mid_ref, recv_ref, sems, grp_sems, 8)
    ex.greet()

    def after_group(a0, group):
        assert group == ex.count
        g = a0 // group
        ex.send_rows(tiles_ref, g, a0)

    zy_kernel(pen_z_ref, pen_y_ref, src_ref, tiles_ref, pad_ref, u_ref, w_ref, ex.wait_greetings, after_group)
    ex.finish(tiles_ref, out_ref, n_gz_groups(ex), transpose=True)


def regularize(current):
    levels, nz, ny, nx = current.shape
    lines = levels * nz * ny
    n_gz = lax.axis_size("gz")
    n_gy = lax.axis_size("gy")
    assert lines == 128 and ny == 8 and n_gy == 8 and n_gz * n_gy == nx
    smem = pl.BlockSpec(memory_space=pltpu.SMEM)
    vmem = pl.BlockSpec(memory_space=pltpu.VMEM)
    tiles = (n_gz, n_gy, lines)
    xq = (KERNEL + 7) // 8
    nxo = nx // 8
    pen_x = penalty_table(8 * (xq * 2 + 2), KERNEL)
    xu = -(-(nxo + 2 * xq + 2) // 8) * 8
    r1 = pl.pallas_call(
        xpass_send_kernel,
        out_shape=jax.ShapeDtypeStruct(tiles, jnp.float32),
        in_specs=[smem, vmem],
        out_specs=vmem,
        scratch_shapes=[pltpu.VMEM((xu + 8, 8, lines), jnp.float32),
                        pltpu.VMEM((8, xu, 8, lines), jnp.float32)] + exchange_scratch(tiles, n_gz // 8),
        compiler_params=pltpu.CompilerParams(collective_id=1, has_side_effects=True),
    )(pen_x, current.reshape(lines, nx))
    zq = KERNEL // 4
    pen_z = penalty_table(4 * (2 * zq + 2), KERNEL)
    zu = -(-(n_gz + 2 * zq + 2) // 8) * 8
    pen_y = penalty_table(8 * 2 * n_gy, 8 * n_gy)
    r2 = pl.pallas_call(
        zy_send_kernel,
        out_shape=jax.ShapeDtypeStruct((lines, nx), jnp.float32),
        in_specs=[smem, smem, vmem],
        out_specs=vmem,
        scratch_shapes=[pltpu.VMEM((zu + 8, 8, lines), jnp.float32),
                        pltpu.VMEM((4, zu, 8, lines), jnp.float32),
                        pltpu.VMEM((8, n_gz, 8, lines), jnp.float32)] + exchange_scratch(tiles, n_gz // 8),
        compiler_params=pltpu.CompilerParams(collective_id=2, has_side_effects=True),
    )(pen_z, pen_y, r1)
    return r2.reshape(current.shape)


def body(levels, ct_image, region_means):
    current = evolve_all(levels, ct_image, region_means)
    return (current, regularize(current))


def solution(mesh):
    return jax.shard_map(
        body,
        mesh=mesh,
        in_specs=(P(None, "gz", "gy", None), P("gz", "gy", None), P()),
        out_specs=(P(None, "gz", "gy", None), P(None, "gz", "gy", None)),
        check_vma=False,
    )
```

```python
import functools
import math

import jax
import numpy as np
import jax.numpy as jnp
from jax import lax
from jax.experimental import pallas as pl
from jax.experimental.pallas import tpu as pltpu
from jax.sharding import PartitionSpec as P

LEVELS = 4
PHASES = 16
UPDATES = 2
KERNEL = 200


PENALTY = 0.0005
STEP_SIZE = 0.5


def arctan(x):
    ax = jnp.abs(x)
    big = ax > 2.414213562373095
    mid = ax > 0.4142135623730950
    num = jnp.where(big, -1.0, jnp.where(mid, ax - 1.0, ax))
    den = jnp.where(big, ax, jnp.where(mid, ax + 1.0, 1.0))
    z = num / den
    base = jnp.where(big, math.pi / 2, jnp.where(mid, math.pi / 4, 0.0))
    zz = z * z
    poly = (((8.05374449538e-2 * zz - 1.38776856032e-1) * zz + 1.99777106478e-1) * zz
            - 3.33329491539e-1) * zz * z + z
    r = base + poly
    return jnp.where(x < 0, -r, r)


def compute_step(means_ref, cur_ref, zlo_ref, zhi_ref, ylo_ref, yhi_ref, ct_ref, out_ref):
    nz, ny, nx = cur_ref.shape[1], cur_ref.shape[2], cur_ref.shape[3]
    shape = (ny, nx)
    xi = lax.broadcasted_iota(jnp.int32, shape, 1)
    yi = lax.broadcasted_iota(jnp.int32, shape, 0)
    xa = pltpu.roll(xi, 1, 1)
    xb = pltpu.roll(xi, nx - 1, 1)
    xa_ok = jnp.abs(xa - xi) == 1
    xb_ok = jnp.abs(xb - xi) == 1
    ya = pltpu.roll(yi, 1, 0)
    yb = pltpu.roll(yi, ny - 1, 0)
    ya_ok = jnp.abs(ya - yi) == 1
    yb_ok = jnp.abs(yb - yi) == 1
    low_row = yi == 0
    means = [means_ref[p] for p in range(PHASES)]
    for z in range(nz):
        picture = ct_ref[z]
        energy = []
        for p in range(PHASES):
            differ = picture - means[p]
            energy.append(differ * differ)
        phis, lap, g1, g0, dl = [], [], [], [], []
        for k in range(LEVELS):
            c = cur_ref[k, z]
            zm = zlo_ref[k] if z == 0 else cur_ref[k, z - 1]
            zp = zhi_ref[k] if z == nz - 1 else cur_ref[k, z + 1]
            edge = jnp.where(low_row, ylo_ref[k, z], yhi_ref[k, z])
            ym = jnp.where(ya_ok, pltpu.roll(c, 1, 0), edge)
            yp = jnp.where(yb_ok, pltpu.roll(c, ny - 1, 0), edge)
            xm = jnp.where(xa_ok, pltpu.roll(c, 1, 1), 0.0)
            xp = jnp.where(xb_ok, pltpu.roll(c, nx - 1, 1), 0.0)
            lap.append(zm + zp + ym + yp + xm + xp - 6.0 * c)
            h = 0.5 + arctan(c) / math.pi
            g1.append(h)
            g0.append(1.0 - h)
            dl.append(1.0 / (math.pi * (1.0 + c * c)))
            phis.append(c)
        g = (g0, g1)
        pair_lo = {(a, b): g[a][0] * g[b][1] for a in (0, 1) for b in (0, 1)}
        pair_hi = {(a, b): g[a][2] * g[b][3] for a in (0, 1) for b in (0, 1)}
        for k in range(LEVELS):
            force = None
            for q in range(PHASES // 2):
                low = q & ((1 << k) - 1)
                high = (q >> k) << (k + 1)
                p0 = high | low
                p1 = p0 | (1 << k)
                bits = [(p0 >> j) & 1 for j in range(LEVELS)]
                if k == 0:
                    prod = g[bits[1]][1] * pair_hi[(bits[2], bits[3])]
                elif k == 1:
                    prod = g[bits[0]][0] * pair_hi[(bits[2], bits[3])]
                elif k == 2:
                    prod = pair_lo[(bits[0], bits[1])] * g[bits[3]][3]
                else:
                    prod = pair_lo[(bits[0], bits[1])] * g[bits[2]][2]
                term = (energy[p1] - energy[p0]) * prod
                force = term if force is None else force + term
            out_ref[k, z] = phis[k] + STEP_SIZE * dl[k] * (lap[k] - force)


MESH = pl.DeviceIdType.MESH


def evolve_kernel(means_ref, cur_ref, ct_ref, out_ref, mid_ref, zlo_buf, zhi_buf, ylo_buf, yhi_buf,
                  send_sem, recv_sem):
    nz, ny = cur_ref.shape[1], cur_ref.shape[2]
    gz, gy = lax.axis_index("gz"), lax.axis_index("gy")
    n_gz, n_gy = lax.axis_size("gz"), lax.axis_size("gy")
    peers = [(gz > 0, (gz - 1, gy)), (gz < n_gz - 1, (gz + 1, gy)),
             (gy > 0, (gz, gy - 1)), (gy < n_gy - 1, (gz, gy + 1))]
    barrier = pltpu.get_barrier_semaphore()
    for present, dev in peers:
        @pl.when(present)
        def _(dev=dev):
            pl.semaphore_signal(barrier, inc=1, device_id=dev, device_id_type=MESH)
    count = sum(present.astype(jnp.int32) for present, _ in peers)
    pl.semaphore_wait(barrier, count)

    def exchange(step, src_ref):
        plan = [
            (gz < n_gz - 1, gz > 0, src_ref.at[:, nz - 1], zlo_buf.at[step], (gz + 1, gy)),
            (gz > 0, gz < n_gz - 1, src_ref.at[:, 0], zhi_buf.at[step], (gz - 1, gy)),
            (gy < n_gy - 1, gy > 0, src_ref.at[:, :, pl.ds(ny - 1, 1)], ylo_buf.at[step], (gz, gy + 1)),
            (gy > 0, gy < n_gy - 1, src_ref.at[:, :, pl.ds(0, 1)], yhi_buf.at[step], (gz, gy - 1)),
        ]
        copies = []
        for d, (sends, receives, src, dst, target) in enumerate(plan):
            copy = pltpu.make_async_remote_copy(
                src_ref=src, dst_ref=dst, send_sem=send_sem.at[step, d],
                recv_sem=recv_sem.at[step, d], device_id=target, device_id_type=MESH)

            @pl.when(sends)
            def _(copy=copy):
                copy.start()

            @pl.when(jnp.logical_not(receives))
            def _(dst=dst):
                dst[...] = jnp.zeros(dst.shape, jnp.float32)

            copies.append((sends, receives, copy))
        return copies

    def finish(copies):
        for sends, receives, copy in copies:
            @pl.when(receives)
            def _(copy=copy):
                copy.wait_recv()

    def drain(copies):
        for sends, receives, copy in copies:
            @pl.when(sends)
            def _(copy=copy):
                copy.wait_send()

    first = exchange(0, cur_ref)
    finish(first)
    compute_step(means_ref, cur_ref, zlo_buf.at[0], zhi_buf.at[0], ylo_buf.at[0], yhi_buf.at[0], ct_ref, mid_ref)
    drain(first)
    second = exchange(1, mid_ref)
    finish(second)
    compute_step(means_ref, mid_ref, zlo_buf.at[1], zhi_buf.at[1], ylo_buf.at[1], yhi_buf.at[1], ct_ref, out_ref)
    drain(second)


def evolve_all(current, picture, region_means):
    levels, nz, ny, nx = current.shape
    vmem = pl.BlockSpec(memory_space=pltpu.VMEM)
    f32 = jnp.float32
    return pl.pallas_call(
        evolve_kernel,
        out_shape=jax.ShapeDtypeStruct(current.shape, current.dtype),
        in_specs=[pl.BlockSpec(memory_space=pltpu.SMEM), vmem, vmem],
        out_specs=vmem,
        scratch_shapes=[
            pltpu.VMEM(current.shape, f32),
            pltpu.VMEM((2, levels, ny, nx), f32),
            pltpu.VMEM((2, levels, ny, nx), f32),
            pltpu.VMEM((2, levels, nz, 1, nx), f32),
            pltpu.VMEM((2, levels, nz, 1, nx), f32),
            pltpu.SemaphoreType.DMA((2, 4)),
            pltpu.SemaphoreType.DMA((2, 4)),
        ],
        compiler_params=pltpu.CompilerParams(collective_id=0, has_side_effects=True),
    )(region_means, current, picture)


def penalty_table(count, offset):
    distance = (np.arange(count, dtype=np.int32) - offset).astype(np.float32)
    table = np.where(np.abs(distance) <= KERNEL, np.float32(PENALTY) * (distance * distance), np.float32(np.inf))
    return jnp.asarray(table.astype(np.float32))


def scan_offsets(u_ref, pen_ref, out_ref, n_out, group, nrot, q_range, after_group=None):
    for g0 in range(0, n_out, group):
        q_lo, q_hi = q_range(g0, group)
        q_hi = min(q_hi, pen_ref.shape[0] // nrot - 1, u_ref.shape[1] - g0 - group)

        def body(q, acc, g0=g0):
            for r in range(nrot):
                vals = u_ref[r, pl.ds(g0 + q, group)]
                acc = jnp.minimum(acc, vals + pen_ref[q * nrot + r])
            return acc

        init = jnp.full((group,) + tuple(out_ref.shape[1:]), jnp.inf, jnp.float32)
        out_ref[g0:g0 + group] = lax.fori_loop(q_lo, q_hi + 1, body, init, unroll=2)
        if after_group is not None:
            after_group(g0, group)


def build_rotations(pad_ref, u_ref, nrot, pick, chunk=8):
    def body(i, carry):
        b0 = pl.multiple_of(i * chunk, chunk)
        here = pad_ref[pl.ds(b0, chunk)]
        after = pad_ref[pl.ds(b0 + 1, chunk)]
        u_ref[0, pl.ds(b0, chunk)] = here
        for r in range(1, nrot):
            u_ref[r, pl.ds(b0, chunk)] = pick(r, here, after)
        return carry

    lax.fori_loop(0, u_ref.shape[1] // chunk, body, 0)


def xpass_kernel(pen_ref, src_ref, out_ref, pad_ref, u_ref, after_group=None):
    lines, nx = src_ref.shape
    reach = KERNEL
    padc = reach // 8
    pad_ref[...] = jnp.full(pad_ref.shape, jnp.inf, jnp.float32)
    pad_ref[padc:padc + nx // 8] = src_ref[...].T.reshape(nx // 8, 8, lines)
    sub = lax.broadcasted_iota(jnp.int32, (8, 8, lines), 1)
    build_rotations(pad_ref, u_ref, 8, lambda r, here, after: jnp.where(
        sub < 8 - r, pltpu.roll(here, 8 - r, 1), pltpu.roll(after, 8 - r, 1)))
    n_out = nx // 8

    def q_range(g0, group):
        lo = max(0, -((8 * (g0 + group - 1) + 14 - reach) // 8))
        hi = (reach + nx - 1 - 8 * g0) // 8
        return lo, hi

    scan_offsets(u_ref, pen_ref, out_ref, n_out, 16, 8, q_range, after_group)


def transpose_kernel(src_ref, out_ref):
    out_ref[...] = src_ref[...].T


def local_call(kernel, out_shape, scratch, *args):
    vmem = pl.BlockSpec(memory_space=pltpu.VMEM)
    smem = pl.BlockSpec(memory_space=pltpu.SMEM)
    specs = [smem if a.ndim == 1 else vmem for a in args]
    return pl.pallas_call(
        kernel,
        out_shape=jax.ShapeDtypeStruct(out_shape, jnp.float32),
        in_specs=specs,
        out_specs=vmem,
        scratch_shapes=[pltpu.VMEM(s, jnp.float32) for s in scratch],
    )(*args)


def zy_kernel(pen_z_ref, pen_y_ref, src_ref, out_ref, pad_ref, u_ref, w_ref, before_y=None, after_group=None):
    n_out = src_ref.shape[0]
    padc = KERNEL // 4
    pad_ref[...] = jnp.full(pad_ref.shape, jnp.inf, jnp.float32)
    pad_ref[padc:padc + n_out] = src_ref[...]
    lane = lax.broadcasted_iota(jnp.int32, src_ref.shape[1:], 1)
    sub = lax.broadcasted_iota(jnp.int32, src_ref.shape[1:], 0)
    sub_z = (lane // 8) % 4
    sub_y = lane % 8

    lane3 = lax.broadcasted_iota(jnp.int32, (8,) + tuple(src_ref.shape[1:]), 2)
    sub_z3 = (lane3 // 8) % 4
    sub_y3 = lane3 % 8
    build_rotations(pad_ref, u_ref, 4, lambda r, here, after: jnp.where(
        sub_z3 + r < 4, pltpu.roll(here, 128 - 8 * r, 2), pltpu.roll(after, 32 - 8 * r, 2)))

    def q_range(g0, group):
        lo = max(0, padc - 1 - (g0 + group - 1))
        hi = padc + n_out - 1 - g0
        return lo, hi

    scan_offsets(u_ref, pen_z_ref, out_ref, n_out, 16, 4, q_range)

    def wbody(i, carry):
        a0 = pl.multiple_of(i * 8, 8)
        v = out_ref[pl.ds(a0, 8)]
        w_ref[0, pl.ds(a0, 8)] = v
        for r in range(1, 8):
            w_ref[r, pl.ds(a0, 8)] = jnp.where(sub_y3 + r < 8, pltpu.roll(v, 128 - r, 2),
                                               pltpu.roll(pltpu.roll(v, 8 - r, 2), 7, 1))
        return carry

    lax.fori_loop(0, n_out // 8, wbody, 0)
    if before_y is not None:
        before_y()
    group = 8
    shifts = []
    for db in range(-8, 8):
        for dy in range(8):
            carry_in = (sub_y + dy >= 8).astype(jnp.int32)
            row = sub + db + carry_in
            valid = (row >= 0) & (row <= 7)
            shifts.append((db, dy, valid))

    def ybody(i, carry):
        a0 = pl.multiple_of(i * group, group)
        acc = [jnp.full(src_ref.shape[1:], jnp.inf, jnp.float32) for _ in range(group)]
        for db, dy, valid in shifts:
            penvec = jnp.where(valid, pen_y_ref[8 * db + dy + 64], jnp.inf)
            for g in range(group):
                v = w_ref[dy, a0 + g]
                if db % 8:
                    v = pltpu.roll(v, (8 - db) % 8, 0)
                acc[g] = jnp.minimum(acc[g], v + penvec)
        for g in range(group):
            out_ref[a0 + g] = acc[g]
        if after_group is not None:
            after_group(a0, group)
        return carry

    lax.fori_loop(0, n_out // group, ybody, 0)


class Exchange:
    def __init__(self, mid_ref, recv_ref, sems, grp_sems, count):
        self.n_gz, self.n_gy = lax.axis_size("gz"), lax.axis_size("gy")
        self.a, self.b = lax.axis_index("gz"), lax.axis_index("gy")
        self.mid_ref, self.recv_ref, self.sems = mid_ref, recv_ref, sems
        self.grp_sems, self.count = grp_sems, count
        self.barrier = pltpu.get_barrier_semaphore()

    def greet(self):
        a, b, n_gz, n_gy = self.a, self.b, self.n_gz, self.n_gy

        def greet_gy(k, carry):
            pl.semaphore_signal(self.barrier, inc=1, device_id=(a, lax.rem(b + k, n_gy)),
                                device_id_type=MESH)
            return carry

        def greet_gz(k, carry):
            pl.semaphore_signal(self.barrier, inc=1, device_id=(lax.rem(a + k, n_gz), b),
                                device_id_type=MESH)
            return carry

        lax.fori_loop(1, n_gy, greet_gy, 0)
        lax.fori_loop(1, n_gz, greet_gz, 0)

    def wait_greetings(self):
        pl.semaphore_wait(self.barrier, self.n_gy - 1 + self.n_gz - 1)

    def send_rows(self, tiles_ref, g, t0):
        a, b, n_gy, count = self.a, self.b, self.n_gy, self.count
        for k in range(1, n_gy):
            p = lax.rem(b + k, n_gy)
            pltpu.make_async_remote_copy(
                src_ref=tiles_ref.at[pl.ds(t0, count), pl.ds(p, 1)],
                dst_ref=self.mid_ref.at[pl.ds(t0, count), pl.ds(b, 1)], send_sem=self.sems.at[0],
                recv_sem=self.grp_sems.at[g], device_id=(a, p), device_id_type=MESH).start()
        own = pltpu.make_async_copy(tiles_ref.at[pl.ds(t0, count), pl.ds(b, 1)],
                                    self.mid_ref.at[pl.ds(t0, count), pl.ds(b, 1)], self.sems.at[2])
        own.start()
        own.wait()

    def forward_group(self, g, t0):
        a, b, n_gy, count = self.a, self.b, self.n_gy, self.count
        pltpu.make_async_remote_copy(
            src_ref=self.mid_ref.at[pl.ds(t0, count), pl.ds(0, n_gy - 1)],
            dst_ref=self.mid_ref.at[pl.ds(t0, count), pl.ds(0, n_gy - 1)], send_sem=self.sems.at[0],
            recv_sem=self.grp_sems.at[g], device_id=(a, lax.rem(b + 1, n_gy)),
            device_id_type=MESH).wait_recv()
        for j in range(count):
            p = t0 + j

            @pl.when(p != a)
            def _(p=p):
                pltpu.make_async_remote_copy(
                    src_ref=self.mid_ref.at[pl.ds(p, 1)], dst_ref=self.recv_ref.at[pl.ds(a, 1)],
                    send_sem=self.sems.at[3], recv_sem=self.sems.at[4], device_id=(p, b),
                    device_id_type=MESH).start()

    def finish(self, tiles_ref, out_ref, pending, transpose=False):
        a, b, n_gz, n_gy = self.a, self.b, self.n_gz, self.n_gy
        mid_ref, recv_ref, sems = self.mid_ref, self.recv_ref, self.sems
        groups = n_gz // self.count
        for g in range(groups - pending, groups):
            self.forward_group(g, g * self.count)
        pltpu.make_async_remote_copy(
            src_ref=tiles_ref.at[:, pl.ds(0, n_gy - 1)], dst_ref=mid_ref.at[:, pl.ds(0, n_gy - 1)],
            send_sem=sems.at[0], recv_sem=sems.at[1], device_id=(a, lax.rem(b + 1, n_gy)),
            device_id_type=MESH).wait_send()
        own = pltpu.make_async_copy(mid_ref.at[pl.ds(a, 1)], recv_ref.at[pl.ds(a, 1)], sems.at[5])
        own.start()
        own.wait()
        total = pltpu.make_async_remote_copy(
            src_ref=mid_ref.at[pl.ds(0, n_gz - 1)], dst_ref=recv_ref.at[pl.ds(0, n_gz - 1)],
            send_sem=sems.at[3], recv_sem=sems.at[4], device_id=(lax.rem(a + 1, n_gz), b),
            device_id_type=MESH)
        total.wait_recv()
        total.wait_send()
        if transpose:
            out_ref[...] = recv_ref[...].reshape(out_ref.shape[::-1]).T
        else:
            out_ref[...] = recv_ref[...]


def n_gz_groups(ex):
    return ex.n_gz // ex.count


def exchange_scratch(tiles_shape, groups):
    return [pltpu.VMEM(tiles_shape, jnp.float32)] * 3 + [pltpu.SemaphoreType.DMA((6,)),
                                                         pltpu.SemaphoreType.DMA((groups,))]


def xpass_send_kernel(pen_ref, src_ref, out_ref, pad_ref, u_ref, tiles_ref, mid_ref, recv_ref, sems, grp_sems):
    ex = Exchange(mid_ref, recv_ref, sems, grp_sems, 16)
    ex.greet()

    def after_group(g0, group):
        assert group == ex.count
        g = g0 // group
        if g == 0:
            ex.wait_greetings()
        ex.send_rows(tiles_ref, g, g0)
        if g >= 1:
            ex.forward_group(g - 1, g0 - group)

    xpass_kernel(pen_ref, src_ref, tiles_ref, pad_ref, u_ref, after_group)
    ex.finish(tiles_ref, out_ref, 1)


def zy_send_kernel(pen_z_ref, pen_y_ref, src_ref, out_ref, pad_ref, u_ref, w_ref, tiles_ref, mid_ref,
                   recv_ref, sems, grp_sems):
    ex = Exchange(mid_ref, recv_ref, sems, grp_sems, 8)
    ex.greet()

    def after_group(a0, group):
        assert group == ex.count
        g = a0 // group
        ex.send_rows(tiles_ref, g, a0)

    zy_kernel(pen_z_ref, pen_y_ref, src_ref, tiles_ref, pad_ref, u_ref, w_ref, ex.wait_greetings, after_group)
    ex.finish(tiles_ref, out_ref, n_gz_groups(ex), transpose=True)


def regularize(current):
    levels, nz, ny, nx = current.shape
    lines = levels * nz * ny
    n_gz = lax.axis_size("gz")
    n_gy = lax.axis_size("gy")
    assert lines == 128 and ny == 8 and n_gy == 8 and n_gz * n_gy == nx
    smem = pl.BlockSpec(memory_space=pltpu.SMEM)
    vmem = pl.BlockSpec(memory_space=pltpu.VMEM)
    tiles = (n_gz, n_gy, lines)
    xq = (KERNEL + 7) // 8
    nxo = nx // 8
    pen_x = penalty_table(8 * (xq * 2 + 2), KERNEL)
    xu = -(-(nxo + 2 * xq + 2) // 8) * 8
    r1 = pl.pallas_call(
        xpass_send_kernel,
        out_shape=jax.ShapeDtypeStruct(tiles, jnp.float32),
        in_specs=[smem, vmem],
        out_specs=vmem,
        scratch_shapes=[pltpu.VMEM((xu + 8, 8, lines), jnp.float32),
                        pltpu.VMEM((8, xu, 8, lines), jnp.float32)] + exchange_scratch(tiles, n_gz // 16),
        compiler_params=pltpu.CompilerParams(collective_id=1, has_side_effects=True),
    )(pen_x, current.reshape(lines, nx))
    zq = KERNEL // 4
    pen_z = penalty_table(4 * (2 * zq + 2), KERNEL)
    zu = -(-(n_gz + 2 * zq + 2) // 8) * 8
    pen_y = penalty_table(8 * 2 * n_gy, 8 * n_gy)
    r2 = pl.pallas_call(
        zy_send_kernel,
        out_shape=jax.ShapeDtypeStruct((lines, nx), jnp.float32),
        in_specs=[smem, smem, vmem],
        out_specs=vmem,
        scratch_shapes=[pltpu.VMEM((zu + 8, 8, lines), jnp.float32),
                        pltpu.VMEM((4, zu, 8, lines), jnp.float32),
                        pltpu.VMEM((8, n_gz, 8, lines), jnp.float32)] + exchange_scratch(tiles, n_gz // 8),
        compiler_params=pltpu.CompilerParams(collective_id=2, has_side_effects=True),
    )(pen_z, pen_y, r1)
    return r2.reshape(current.shape)


def body(levels, ct_image, region_means):
    current = evolve_all(levels, ct_image, region_means)
    return (current, regularize(current))


def solution(mesh):
    return jax.shard_map(
        body,
        mesh=mesh,
        in_specs=(P(None, "gz", "gy", None), P("gz", "gy", None), P()),
        out_specs=(P(None, "gz", "gy", None), P(None, "gz", "gy", None)),
        check_vma=False,
    )
```

```python
import functools
import math

import jax
import numpy as np
import jax.numpy as jnp
from jax import lax
from jax.experimental import pallas as pl
from jax.experimental.pallas import tpu as pltpu
from jax.sharding import PartitionSpec as P

LEVELS = 4
PHASES = 16
UPDATES = 2
KERNEL = 200


PENALTY = 0.0005
STEP_SIZE = 0.5


def arctan(x):
    ax = jnp.abs(x)
    big = ax > 2.414213562373095
    mid = ax > 0.4142135623730950
    z_big = -1.0 / jnp.where(big, ax, 1.0)
    z_mid = (ax - 1.0) / (ax + 1.0)
    z = jnp.where(big, z_big, jnp.where(mid, z_mid, ax))
    base = jnp.where(big, math.pi / 2, jnp.where(mid, math.pi / 4, 0.0))
    zz = z * z
    poly = (((8.05374449538e-2 * zz - 1.38776856032e-1) * zz + 1.99777106478e-1) * zz
            - 3.33329491539e-1) * zz * z + z
    r = base + poly
    return jnp.where(x < 0, -r, r)


def compute_step(means_ref, cur_ref, zlo_ref, zhi_ref, ylo_ref, yhi_ref, ct_ref, out_ref):
    nz, ny, nx = cur_ref.shape[1], cur_ref.shape[2], cur_ref.shape[3]
    shape = (ny, nx)
    xi = lax.broadcasted_iota(jnp.int32, shape, 1)
    yi = lax.broadcasted_iota(jnp.int32, shape, 0)
    xa = pltpu.roll(xi, 1, 1)
    xb = pltpu.roll(xi, nx - 1, 1)
    xa_ok = jnp.abs(xa - xi) == 1
    xb_ok = jnp.abs(xb - xi) == 1
    ya = pltpu.roll(yi, 1, 0)
    yb = pltpu.roll(yi, ny - 1, 0)
    ya_ok = jnp.abs(ya - yi) == 1
    yb_ok = jnp.abs(yb - yi) == 1
    low_row = yi == 0
    means = [means_ref[p] for p in range(PHASES)]
    for z in range(nz):
        picture = ct_ref[z]
        energy = []
        for p in range(PHASES):
            differ = picture - means[p]
            energy.append(differ * differ)
        phis, lap, g1, g0, dl = [], [], [], [], []
        for k in range(LEVELS):
            c = cur_ref[k, z]
            zm = zlo_ref[k] if z == 0 else cur_ref[k, z - 1]
            zp = zhi_ref[k] if z == nz - 1 else cur_ref[k, z + 1]
            edge = jnp.where(low_row, ylo_ref[k, z], yhi_ref[k, z])
            ym = jnp.where(ya_ok, pltpu.roll(c, 1, 0), edge)
            yp = jnp.where(yb_ok, pltpu.roll(c, ny - 1, 0), edge)
            xm = jnp.where(xa_ok, pltpu.roll(c, 1, 1), 0.0)
            xp = jnp.where(xb_ok, pltpu.roll(c, nx - 1, 1), 0.0)
            lap.append(zm + zp + ym + yp + xm + xp - 6.0 * c)
            h = 0.5 + arctan(c) / math.pi
            g1.append(h)
            g0.append(1.0 - h)
            dl.append(1.0 / (math.pi * (1.0 + c * c)))
            phis.append(c)
        g = (g0, g1)
        pair_lo = {(a, b): g[a][0] * g[b][1] for a in (0, 1) for b in (0, 1)}
        pair_hi = {(a, b): g[a][2] * g[b][3] for a in (0, 1) for b in (0, 1)}
        for k in range(LEVELS):
            force = None
            for q in range(PHASES // 2):
                low = q & ((1 << k) - 1)
                high = (q >> k) << (k + 1)
                p0 = high | low
                p1 = p0 | (1 << k)
                bits = [(p0 >> j) & 1 for j in range(LEVELS)]
                if k == 0:
                    prod = g[bits[1]][1] * pair_hi[(bits[2], bits[3])]
                elif k == 1:
                    prod = g[bits[0]][0] * pair_hi[(bits[2], bits[3])]
                elif k == 2:
                    prod = pair_lo[(bits[0], bits[1])] * g[bits[3]][3]
                else:
                    prod = pair_lo[(bits[0], bits[1])] * g[bits[2]][2]
                term = (energy[p1] - energy[p0]) * prod
                force = term if force is None else force + term
            out_ref[k, z] = phis[k] + STEP_SIZE * dl[k] * (lap[k] - force)


MESH = pl.DeviceIdType.MESH


def evolve_kernel(means_ref, cur_ref, ct_ref, out_ref, mid_ref, zlo_buf, zhi_buf, ylo_buf, yhi_buf,
                  send_sem, recv_sem):
    nz, ny = cur_ref.shape[1], cur_ref.shape[2]
    gz, gy = lax.axis_index("gz"), lax.axis_index("gy")
    n_gz, n_gy = lax.axis_size("gz"), lax.axis_size("gy")
    peers = [(gz > 0, (gz - 1, gy)), (gz < n_gz - 1, (gz + 1, gy)),
             (gy > 0, (gz, gy - 1)), (gy < n_gy - 1, (gz, gy + 1))]
    barrier = pltpu.get_barrier_semaphore()
    for present, dev in peers:
        @pl.when(present)
        def _(dev=dev):
            pl.semaphore_signal(barrier, inc=1, device_id=dev, device_id_type=MESH)
    count = sum(present.astype(jnp.int32) for present, _ in peers)
    pl.semaphore_wait(barrier, count)

    def exchange(step, src_ref):
        plan = [
            (gz < n_gz - 1, gz > 0, src_ref.at[:, nz - 1], zlo_buf.at[step], (gz + 1, gy)),
            (gz > 0, gz < n_gz - 1, src_ref.at[:, 0], zhi_buf.at[step], (gz - 1, gy)),
            (gy < n_gy - 1, gy > 0, src_ref.at[:, :, pl.ds(ny - 1, 1)], ylo_buf.at[step], (gz, gy + 1)),
            (gy > 0, gy < n_gy - 1, src_ref.at[:, :, pl.ds(0, 1)], yhi_buf.at[step], (gz, gy - 1)),
        ]
        copies = []
        for d, (sends, receives, src, dst, target) in enumerate(plan):
            copy = pltpu.make_async_remote_copy(
                src_ref=src, dst_ref=dst, send_sem=send_sem.at[step, d],
                recv_sem=recv_sem.at[step, d], device_id=target, device_id_type=MESH)

            @pl.when(sends)
            def _(copy=copy):
                copy.start()

            @pl.when(jnp.logical_not(receives))
            def _(dst=dst):
                dst[...] = jnp.zeros(dst.shape, jnp.float32)

            copies.append((sends, receives, copy))
        return copies

    def finish(copies):
        for sends, receives, copy in copies:
            @pl.when(receives)
            def _(copy=copy):
                copy.wait_recv()

    def drain(copies):
        for sends, receives, copy in copies:
            @pl.when(sends)
            def _(copy=copy):
                copy.wait_send()

    first = exchange(0, cur_ref)
    finish(first)
    compute_step(means_ref, cur_ref, zlo_buf.at[0], zhi_buf.at[0], ylo_buf.at[0], yhi_buf.at[0], ct_ref, mid_ref)
    drain(first)
    second = exchange(1, mid_ref)
    finish(second)
    compute_step(means_ref, mid_ref, zlo_buf.at[1], zhi_buf.at[1], ylo_buf.at[1], yhi_buf.at[1], ct_ref, out_ref)
    drain(second)


def evolve_all(current, picture, region_means):
    levels, nz, ny, nx = current.shape
    vmem = pl.BlockSpec(memory_space=pltpu.VMEM)
    f32 = jnp.float32
    return pl.pallas_call(
        evolve_kernel,
        out_shape=jax.ShapeDtypeStruct(current.shape, current.dtype),
        in_specs=[pl.BlockSpec(memory_space=pltpu.SMEM), vmem, vmem],
        out_specs=vmem,
        scratch_shapes=[
            pltpu.VMEM(current.shape, f32),
            pltpu.VMEM((2, levels, ny, nx), f32),
            pltpu.VMEM((2, levels, ny, nx), f32),
            pltpu.VMEM((2, levels, nz, 1, nx), f32),
            pltpu.VMEM((2, levels, nz, 1, nx), f32),
            pltpu.SemaphoreType.DMA((2, 4)),
            pltpu.SemaphoreType.DMA((2, 4)),
        ],
        compiler_params=pltpu.CompilerParams(collective_id=0, has_side_effects=True),
    )(region_means, current, picture)


def penalty_table(count, offset):
    distance = (np.arange(count, dtype=np.int32) - offset).astype(np.float32)
    table = np.where(np.abs(distance) <= KERNEL, np.float32(PENALTY) * (distance * distance), np.float32(np.inf))
    return jnp.asarray(table.astype(np.float32))


def scan_offsets(u_ref, pen_ref, out_ref, n_out, group, nrot, q_range, after_group=None):
    for g0 in range(0, n_out, group):
        q_lo, q_hi = q_range(g0, group)
        q_hi = min(q_hi, pen_ref.shape[0] // nrot - 1, u_ref.shape[1] - g0 - group)

        def body(q, acc, g0=g0):
            for r in range(nrot):
                vals = u_ref[r, pl.ds(g0 + q, group)]
                acc = jnp.minimum(acc, vals + pen_ref[q * nrot + r])
            return acc

        init = jnp.full((group,) + tuple(out_ref.shape[1:]), jnp.inf, jnp.float32)
        out_ref[g0:g0 + group] = lax.fori_loop(q_lo, q_hi + 1, body, init, unroll=2)
        if after_group is not None:
            after_group(g0, group)


def build_rotations(pad_ref, u_ref, nrot, pick, chunk=8):
    def body(i, carry):
        b0 = pl.multiple_of(i * chunk, chunk)
        here = pad_ref[pl.ds(b0, chunk)]
        after = pad_ref[pl.ds(b0 + 1, chunk)]
        u_ref[0, pl.ds(b0, chunk)] = here
        for r in range(1, nrot):
            u_ref[r, pl.ds(b0, chunk)] = pick(r, here, after)
        return carry

    lax.fori_loop(0, u_ref.shape[1] // chunk, body, 0)


def xpass_kernel(pen_ref, src_ref, out_ref, pad_ref, u_ref, after_group=None):
    lines, nx = src_ref.shape
    reach = KERNEL
    padc = reach // 8
    pad_ref[...] = jnp.full(pad_ref.shape, jnp.inf, jnp.float32)
    pad_ref[padc:padc + nx // 8] = src_ref[...].T.reshape(nx // 8, 8, lines)
    sub = lax.broadcasted_iota(jnp.int32, (8, 8, lines), 1)
    build_rotations(pad_ref, u_ref, 8, lambda r, here, after: jnp.where(
        sub < 8 - r, pltpu.roll(here, 8 - r, 1), pltpu.roll(after, 8 - r, 1)))
    n_out = nx // 8

    def q_range(g0, group):
        lo = max(0, -((8 * (g0 + group - 1) + 14 - reach) // 8))
        hi = (reach + nx - 1 - 8 * g0) // 8
        return lo, hi

    scan_offsets(u_ref, pen_ref, out_ref, n_out, 16, 8, q_range, after_group)


def transpose_kernel(src_ref, out_ref):
    out_ref[...] = src_ref[...].T


def local_call(kernel, out_shape, scratch, *args):
    vmem = pl.BlockSpec(memory_space=pltpu.VMEM)
    smem = pl.BlockSpec(memory_space=pltpu.SMEM)
    specs = [smem if a.ndim == 1 else vmem for a in args]
    return pl.pallas_call(
        kernel,
        out_shape=jax.ShapeDtypeStruct(out_shape, jnp.float32),
        in_specs=specs,
        out_specs=vmem,
        scratch_shapes=[pltpu.VMEM(s, jnp.float32) for s in scratch],
    )(*args)


def zy_kernel(pen_z_ref, pen_y_ref, src_ref, out_ref, pad_ref, u_ref, w_ref, before_y=None, after_group=None):
    n_out = src_ref.shape[0]
    padc = KERNEL // 4
    pad_ref[...] = jnp.full(pad_ref.shape, jnp.inf, jnp.float32)
    pad_ref[padc:padc + n_out] = src_ref[...]
    lane = lax.broadcasted_iota(jnp.int32, src_ref.shape[1:], 1)
    sub = lax.broadcasted_iota(jnp.int32, src_ref.shape[1:], 0)
    sub_z = (lane // 8) % 4
    sub_y = lane % 8

    lane3 = lax.broadcasted_iota(jnp.int32, (8,) + tuple(src_ref.shape[1:]), 2)
    sub_z3 = (lane3 // 8) % 4
    sub_y3 = lane3 % 8
    build_rotations(pad_ref, u_ref, 4, lambda r, here, after: jnp.where(
        sub_z3 + r < 4, pltpu.roll(here, 128 - 8 * r, 2), pltpu.roll(after, 32 - 8 * r, 2)))

    def q_range(g0, group):
        lo = max(0, padc - 1 - (g0 + group - 1))
        hi = padc + n_out - 1 - g0
        return lo, hi

    scan_offsets(u_ref, pen_z_ref, out_ref, n_out, 16, 4, q_range)

    def wbody(i, carry):
        a0 = pl.multiple_of(i * 8, 8)
        v = out_ref[pl.ds(a0, 8)]
        w_ref[0, pl.ds(a0, 8)] = v
        for r in range(1, 8):
            w_ref[r, pl.ds(a0, 8)] = jnp.where(sub_y3 + r < 8, pltpu.roll(v, 128 - r, 2),
                                               pltpu.roll(pltpu.roll(v, 8 - r, 2), 7, 1))
        return carry

    lax.fori_loop(0, n_out // 8, wbody, 0)
    if before_y is not None:
        before_y()
    group = 16
    shifts = []
    for db in range(-8, 8):
        for dy in range(8):
            carry_in = (sub_y + dy >= 8).astype(jnp.int32)
            row = sub + db + carry_in
            valid = (row >= 0) & (row <= 7)
            shifts.append((db, dy, valid))

    def ybody(i, carry):
        a0 = pl.multiple_of(i * group, group)
        acc = [jnp.full(src_ref.shape[1:], jnp.inf, jnp.float32) for _ in range(group)]
        for db, dy, valid in shifts:
            penvec = jnp.where(valid, pen_y_ref[8 * db + dy + 64], jnp.inf)
            for g in range(group):
                v = w_ref[dy, a0 + g]
                if db % 8:
                    v = pltpu.roll(v, (8 - db) % 8, 0)
                acc[g] = jnp.minimum(acc[g], v + penvec)
        for g in range(group):
            out_ref[a0 + g] = acc[g]
        if after_group is not None:
            after_group(a0, group)
        return carry

    lax.fori_loop(0, n_out // group, ybody, 0)


class Exchange:
    def __init__(self, mid_ref, recv_ref, sems, grp_sems, count):
        self.n_gz, self.n_gy = lax.axis_size("gz"), lax.axis_size("gy")
        self.a, self.b = lax.axis_index("gz"), lax.axis_index("gy")
        self.mid_ref, self.recv_ref, self.sems = mid_ref, recv_ref, sems
        self.grp_sems, self.count = grp_sems, count
        self.barrier = pltpu.get_barrier_semaphore()

    def greet(self):
        a, b, n_gz, n_gy = self.a, self.b, self.n_gz, self.n_gy

        def greet_gy(k, carry):
            pl.semaphore_signal(self.barrier, inc=1, device_id=(a, lax.rem(b + k, n_gy)),
                                device_id_type=MESH)
            return carry

        def greet_gz(k, carry):
            pl.semaphore_signal(self.barrier, inc=1, device_id=(lax.rem(a + k, n_gz), b),
                                device_id_type=MESH)
            return carry

        lax.fori_loop(1, n_gy, greet_gy, 0)
        lax.fori_loop(1, n_gz, greet_gz, 0)

    def wait_greetings(self):
        pl.semaphore_wait(self.barrier, self.n_gy - 1 + self.n_gz - 1)

    def send_rows(self, tiles_ref, g, t0):
        a, b, n_gy, count = self.a, self.b, self.n_gy, self.count
        for k in range(1, n_gy):
            p = lax.rem(b + k, n_gy)
            pltpu.make_async_remote_copy(
                src_ref=tiles_ref.at[pl.ds(t0, count), pl.ds(p, 1)],
                dst_ref=self.mid_ref.at[pl.ds(t0, count), pl.ds(b, 1)], send_sem=self.sems.at[0],
                recv_sem=self.grp_sems.at[g], device_id=(a, p), device_id_type=MESH).start()
        own = pltpu.make_async_copy(tiles_ref.at[pl.ds(t0, count), pl.ds(b, 1)],
                                    self.mid_ref.at[pl.ds(t0, count), pl.ds(b, 1)], self.sems.at[2])
        own.start()
        own.wait()

    def forward_group(self, g, t0):
        a, b, n_gy, count = self.a, self.b, self.n_gy, self.count
        pltpu.make_async_remote_copy(
            src_ref=self.mid_ref.at[pl.ds(t0, count), pl.ds(0, n_gy - 1)],
            dst_ref=self.mid_ref.at[pl.ds(t0, count), pl.ds(0, n_gy - 1)], send_sem=self.sems.at[0],
            recv_sem=self.grp_sems.at[g], device_id=(a, lax.rem(b + 1, n_gy)),
            device_id_type=MESH).wait_recv()
        for j in range(count):
            p = t0 + j

            @pl.when(p != a)
            def _(p=p):
                pltpu.make_async_remote_copy(
                    src_ref=self.mid_ref.at[pl.ds(p, 1)], dst_ref=self.recv_ref.at[pl.ds(a, 1)],
                    send_sem=self.sems.at[3], recv_sem=self.sems.at[4], device_id=(p, b),
                    device_id_type=MESH).start()

    def finish(self, tiles_ref, out_ref, pending, transpose=False):
        a, b, n_gz, n_gy = self.a, self.b, self.n_gz, self.n_gy
        mid_ref, recv_ref, sems = self.mid_ref, self.recv_ref, self.sems
        groups = n_gz // self.count
        for g in range(groups - pending, groups):
            self.forward_group(g, g * self.count)
        pltpu.make_async_remote_copy(
            src_ref=tiles_ref.at[:, pl.ds(0, n_gy - 1)], dst_ref=mid_ref.at[:, pl.ds(0, n_gy - 1)],
            send_sem=sems.at[0], recv_sem=sems.at[1], device_id=(a, lax.rem(b + 1, n_gy)),
            device_id_type=MESH).wait_send()
        own = pltpu.make_async_copy(mid_ref.at[pl.ds(a, 1)], recv_ref.at[pl.ds(a, 1)], sems.at[5])
        own.start()
        own.wait()
        total = pltpu.make_async_remote_copy(
            src_ref=mid_ref.at[pl.ds(0, n_gz - 1)], dst_ref=recv_ref.at[pl.ds(0, n_gz - 1)],
            send_sem=sems.at[3], recv_sem=sems.at[4], device_id=(lax.rem(a + 1, n_gz), b),
            device_id_type=MESH)
        total.wait_recv()
        total.wait_send()
        if transpose:
            out_ref[...] = recv_ref[...].reshape(out_ref.shape[::-1]).T
        else:
            out_ref[...] = recv_ref[...]


def n_gz_groups(ex):
    return ex.n_gz // ex.count


def exchange_scratch(tiles_shape, groups):
    return [pltpu.VMEM(tiles_shape, jnp.float32)] * 3 + [pltpu.SemaphoreType.DMA((6,)),
                                                         pltpu.SemaphoreType.DMA((groups,))]


def xpass_send_kernel(pen_ref, src_ref, out_ref, pad_ref, u_ref, tiles_ref, mid_ref, recv_ref, sems, grp_sems):
    ex = Exchange(mid_ref, recv_ref, sems, grp_sems, 16)
    ex.greet()

    def after_group(g0, group):
        assert group == ex.count
        g = g0 // group
        if g == 0:
            ex.wait_greetings()
        ex.send_rows(tiles_ref, g, g0)
        if g >= 1:
            ex.forward_group(g - 1, g0 - group)

    xpass_kernel(pen_ref, src_ref, tiles_ref, pad_ref, u_ref, after_group)
    ex.finish(tiles_ref, out_ref, 1)


def zy_send_kernel(pen_z_ref, pen_y_ref, src_ref, out_ref, pad_ref, u_ref, w_ref, tiles_ref, mid_ref,
                   recv_ref, sems, grp_sems):
    ex = Exchange(mid_ref, recv_ref, sems, grp_sems, 16)
    ex.greet()

    def after_group(a0, group):
        assert group == ex.count
        g = a0 // group
        ex.send_rows(tiles_ref, g, a0)

    zy_kernel(pen_z_ref, pen_y_ref, src_ref, tiles_ref, pad_ref, u_ref, w_ref, ex.wait_greetings, after_group)
    ex.finish(tiles_ref, out_ref, n_gz_groups(ex), transpose=True)


def regularize(current):
    levels, nz, ny, nx = current.shape
    lines = levels * nz * ny
    n_gz = lax.axis_size("gz")
    n_gy = lax.axis_size("gy")
    assert lines == 128 and ny == 8 and n_gy == 8 and n_gz * n_gy == nx
    smem = pl.BlockSpec(memory_space=pltpu.SMEM)
    vmem = pl.BlockSpec(memory_space=pltpu.VMEM)
    tiles = (n_gz, n_gy, lines)
    xq = (KERNEL + 7) // 8
    nxo = nx // 8
    pen_x = penalty_table(8 * (xq * 2 + 2), KERNEL)
    xu = -(-(nxo + 2 * xq + 2) // 8) * 8
    r1 = pl.pallas_call(
        xpass_send_kernel,
        out_shape=jax.ShapeDtypeStruct(tiles, jnp.float32),
        in_specs=[smem, vmem],
        out_specs=vmem,
        scratch_shapes=[pltpu.VMEM((xu + 8, 8, lines), jnp.float32),
                        pltpu.VMEM((8, xu, 8, lines), jnp.float32)] + exchange_scratch(tiles, n_gz // 16),
        compiler_params=pltpu.CompilerParams(collective_id=1, has_side_effects=True),
    )(pen_x, current.reshape(lines, nx))
    zq = KERNEL // 4
    pen_z = penalty_table(4 * (2 * zq + 2), KERNEL)
    zu = -(-(n_gz + 2 * zq + 2) // 8) * 8
    pen_y = penalty_table(8 * 2 * n_gy, 8 * n_gy)
    r2 = pl.pallas_call(
        zy_send_kernel,
        out_shape=jax.ShapeDtypeStruct((lines, nx), jnp.float32),
        in_specs=[smem, smem, vmem],
        out_specs=vmem,
        scratch_shapes=[pltpu.VMEM((zu + 8, 8, lines), jnp.float32),
                        pltpu.VMEM((4, zu, 8, lines), jnp.float32),
                        pltpu.VMEM((8, n_gz, 8, lines), jnp.float32)] + exchange_scratch(tiles, n_gz // 16),
        compiler_params=pltpu.CompilerParams(collective_id=2, has_side_effects=True),
    )(pen_z, pen_y, r1)
    return r2.reshape(current.shape)


def body(levels, ct_image, region_means):
    current = evolve_all(levels, ct_image, region_means)
    return (current, regularize(current))


def solution(mesh):
    return jax.shard_map(
        body,
        mesh=mesh,
        in_specs=(P(None, "gz", "gy", None), P("gz", "gy", None), P()),
        out_specs=(P(None, "gz", "gy", None), P(None, "gz", "gy", None)),
        check_vma=False,
    )
```

```python
import functools
import math

import jax
import numpy as np
import jax.numpy as jnp
from jax import lax
from jax.experimental import pallas as pl
from jax.experimental.pallas import tpu as pltpu
from jax.sharding import PartitionSpec as P

LEVELS = 4
PHASES = 16
UPDATES = 2
KERNEL = 200


PENALTY = 0.0005
STEP_SIZE = 0.5


def arctan(x):
    ax = jnp.abs(x)
    big = ax > 2.414213562373095
    mid = ax > 0.4142135623730950
    z_big = -1.0 / jnp.where(big, ax, 1.0)
    z_mid = (ax - 1.0) / (ax + 1.0)
    z = jnp.where(big, z_big, jnp.where(mid, z_mid, ax))
    base = jnp.where(big, math.pi / 2, jnp.where(mid, math.pi / 4, 0.0))
    zz = z * z
    poly = (((8.05374449538e-2 * zz - 1.38776856032e-1) * zz + 1.99777106478e-1) * zz
            - 3.33329491539e-1) * zz * z + z
    r = base + poly
    return jnp.where(x < 0, -r, r)


def compute_step(means_ref, cur_ref, zlo_ref, zhi_ref, ylo_ref, yhi_ref, ct_ref, out_ref):
    nz, ny, nx = cur_ref.shape[1], cur_ref.shape[2], cur_ref.shape[3]
    shape = (ny, nx)
    xi = lax.broadcasted_iota(jnp.int32, shape, 1)
    yi = lax.broadcasted_iota(jnp.int32, shape, 0)
    xa = pltpu.roll(xi, 1, 1)
    xb = pltpu.roll(xi, nx - 1, 1)
    xa_ok = jnp.abs(xa - xi) == 1
    xb_ok = jnp.abs(xb - xi) == 1
    ya = pltpu.roll(yi, 1, 0)
    yb = pltpu.roll(yi, ny - 1, 0)
    ya_ok = jnp.abs(ya - yi) == 1
    yb_ok = jnp.abs(yb - yi) == 1
    low_row = yi == 0
    means = [means_ref[p] for p in range(PHASES)]
    for z in range(nz):
        picture = ct_ref[z]
        energy = []
        for p in range(PHASES):
            differ = picture - means[p]
            energy.append(differ * differ)
        phis, lap, g1, g0, dl = [], [], [], [], []
        for k in range(LEVELS):
            c = cur_ref[k, z]
            zm = zlo_ref[k] if z == 0 else cur_ref[k, z - 1]
            zp = zhi_ref[k] if z == nz - 1 else cur_ref[k, z + 1]
            edge = jnp.where(low_row, ylo_ref[k, z], yhi_ref[k, z])
            ym = jnp.where(ya_ok, pltpu.roll(c, 1, 0), edge)
            yp = jnp.where(yb_ok, pltpu.roll(c, ny - 1, 0), edge)
            xm = jnp.where(xa_ok, pltpu.roll(c, 1, 1), 0.0)
            xp = jnp.where(xb_ok, pltpu.roll(c, nx - 1, 1), 0.0)
            lap.append(zm + zp + ym + yp + xm + xp - 6.0 * c)
            h = 0.5 + arctan(c) / math.pi
            g1.append(h)
            g0.append(1.0 - h)
            dl.append(1.0 / (math.pi * (1.0 + c * c)))
            phis.append(c)
        g = (g0, g1)
        pair_lo = {(a, b): g[a][0] * g[b][1] for a in (0, 1) for b in (0, 1)}
        pair_hi = {(a, b): g[a][2] * g[b][3] for a in (0, 1) for b in (0, 1)}
        for k in range(LEVELS):
            force = None
            for q in range(PHASES // 2):
                low = q & ((1 << k) - 1)
                high = (q >> k) << (k + 1)
                p0 = high | low
                p1 = p0 | (1 << k)
                bits = [(p0 >> j) & 1 for j in range(LEVELS)]
                if k == 0:
                    prod = g[bits[1]][1] * pair_hi[(bits[2], bits[3])]
                elif k == 1:
                    prod = g[bits[0]][0] * pair_hi[(bits[2], bits[3])]
                elif k == 2:
                    prod = pair_lo[(bits[0], bits[1])] * g[bits[3]][3]
                else:
                    prod = pair_lo[(bits[0], bits[1])] * g[bits[2]][2]
                term = (energy[p1] - energy[p0]) * prod
                force = term if force is None else force + term
            out_ref[k, z] = phis[k] + STEP_SIZE * dl[k] * (lap[k] - force)


MESH = pl.DeviceIdType.MESH


def evolve_kernel(means_ref, cur_ref, ct_ref, out_ref, mid_ref, zlo_buf, zhi_buf, ylo_buf, yhi_buf,
                  send_sem, recv_sem):
    nz, ny = cur_ref.shape[1], cur_ref.shape[2]
    gz, gy = lax.axis_index("gz"), lax.axis_index("gy")
    n_gz, n_gy = lax.axis_size("gz"), lax.axis_size("gy")
    peers = [(gz > 0, (gz - 1, gy)), (gz < n_gz - 1, (gz + 1, gy)),
             (gy > 0, (gz, gy - 1)), (gy < n_gy - 1, (gz, gy + 1))]
    barrier = pltpu.get_barrier_semaphore()
    for present, dev in peers:
        @pl.when(present)
        def _(dev=dev):
            pl.semaphore_signal(barrier, inc=1, device_id=dev, device_id_type=MESH)
    count = sum(present.astype(jnp.int32) for present, _ in peers)
    pl.semaphore_wait(barrier, count)

    def exchange(step, src_ref):
        plan = [
            (gz < n_gz - 1, gz > 0, src_ref.at[:, nz - 1], zlo_buf.at[step], (gz + 1, gy)),
            (gz > 0, gz < n_gz - 1, src_ref.at[:, 0], zhi_buf.at[step], (gz - 1, gy)),
            (gy < n_gy - 1, gy > 0, src_ref.at[:, :, pl.ds(ny - 1, 1)], ylo_buf.at[step], (gz, gy + 1)),
            (gy > 0, gy < n_gy - 1, src_ref.at[:, :, pl.ds(0, 1)], yhi_buf.at[step], (gz, gy - 1)),
        ]
        copies = []
        for d, (sends, receives, src, dst, target) in enumerate(plan):
            copy = pltpu.make_async_remote_copy(
                src_ref=src, dst_ref=dst, send_sem=send_sem.at[step, d],
                recv_sem=recv_sem.at[step, d], device_id=target, device_id_type=MESH)

            @pl.when(sends)
            def _(copy=copy):
                copy.start()

            @pl.when(jnp.logical_not(receives))
            def _(dst=dst):
                dst[...] = jnp.zeros(dst.shape, jnp.float32)

            copies.append((sends, receives, copy))
        return copies

    def finish(copies):
        for sends, receives, copy in copies:
            @pl.when(receives)
            def _(copy=copy):
                copy.wait_recv()

    def drain(copies):
        for sends, receives, copy in copies:
            @pl.when(sends)
            def _(copy=copy):
                copy.wait_send()

    first = exchange(0, cur_ref)
    finish(first)
    compute_step(means_ref, cur_ref, zlo_buf.at[0], zhi_buf.at[0], ylo_buf.at[0], yhi_buf.at[0], ct_ref, mid_ref)
    drain(first)
    second = exchange(1, mid_ref)
    finish(second)
    compute_step(means_ref, mid_ref, zlo_buf.at[1], zhi_buf.at[1], ylo_buf.at[1], yhi_buf.at[1], ct_ref, out_ref)
    drain(second)


def evolve_all(current, picture, region_means):
    levels, nz, ny, nx = current.shape
    vmem = pl.BlockSpec(memory_space=pltpu.VMEM)
    f32 = jnp.float32
    return pl.pallas_call(
        evolve_kernel,
        out_shape=jax.ShapeDtypeStruct(current.shape, current.dtype),
        in_specs=[pl.BlockSpec(memory_space=pltpu.SMEM), vmem, vmem],
        out_specs=vmem,
        scratch_shapes=[
            pltpu.VMEM(current.shape, f32),
            pltpu.VMEM((2, levels, ny, nx), f32),
            pltpu.VMEM((2, levels, ny, nx), f32),
            pltpu.VMEM((2, levels, nz, 1, nx), f32),
            pltpu.VMEM((2, levels, nz, 1, nx), f32),
            pltpu.SemaphoreType.DMA((2, 4)),
            pltpu.SemaphoreType.DMA((2, 4)),
        ],
        compiler_params=pltpu.CompilerParams(collective_id=0, has_side_effects=True),
    )(region_means, current, picture)


def penalty_table(count, offset):
    distance = (np.arange(count, dtype=np.int32) - offset).astype(np.float32)
    table = np.where(np.abs(distance) <= KERNEL, np.float32(PENALTY) * (distance * distance), np.float32(np.inf))
    return jnp.asarray(table.astype(np.float32))


def scan_offsets(u_ref, pen_ref, out_ref, n_out, group, nrot, q_range, after_group=None):
    for g0 in range(0, n_out, group):
        q_lo, q_hi = q_range(g0, group)
        q_hi = min(q_hi, pen_ref.shape[0] // nrot - 1, u_ref.shape[1] - g0 - group)

        def body(q, acc, g0=g0):
            for r in range(nrot):
                vals = u_ref[r, pl.ds(g0 + q, group)]
                acc = jnp.minimum(acc, vals + pen_ref[q * nrot + r])
            return acc

        init = jnp.full((group,) + tuple(out_ref.shape[1:]), jnp.inf, jnp.float32)
        out_ref[g0:g0 + group] = lax.fori_loop(q_lo, q_hi + 1, body, init, unroll=2)
        if after_group is not None:
            after_group(g0, group)


def build_rotations(pad_ref, u_ref, nrot, pick, chunk=8):
    def body(i, carry):
        b0 = pl.multiple_of(i * chunk, chunk)
        here = pad_ref[pl.ds(b0, chunk)]
        after = pad_ref[pl.ds(b0 + 1, chunk)]
        u_ref[0, pl.ds(b0, chunk)] = here
        for r in range(1, nrot):
            u_ref[r, pl.ds(b0, chunk)] = pick(r, here, after)
        return carry

    lax.fori_loop(0, u_ref.shape[1] // chunk, body, 0)


def xpass_kernel(pen_ref, src_ref, out_ref, pad_ref, u_ref, after_group=None):
    lines, nx = src_ref.shape
    reach = KERNEL
    padc = reach // 8
    pad_ref[...] = jnp.full(pad_ref.shape, jnp.inf, jnp.float32)
    pad_ref[padc:padc + nx // 8] = src_ref[...].T.reshape(nx // 8, 8, lines)
    sub = lax.broadcasted_iota(jnp.int32, (8, 8, lines), 1)
    build_rotations(pad_ref, u_ref, 8, lambda r, here, after: jnp.where(
        sub < 8 - r, pltpu.roll(here, 8 - r, 1), pltpu.roll(after, 8 - r, 1)))
    n_out = nx // 8

    def q_range(g0, group):
        lo = max(0, -((8 * (g0 + group - 1) + 14 - reach) // 8))
        hi = (reach + nx - 1 - 8 * g0) // 8
        return lo, hi

    scan_offsets(u_ref, pen_ref, out_ref, n_out, 16, 8, q_range, after_group)


def transpose_kernel(src_ref, out_ref):
    out_ref[...] = src_ref[...].T


def local_call(kernel, out_shape, scratch, *args):
    vmem = pl.BlockSpec(memory_space=pltpu.VMEM)
    smem = pl.BlockSpec(memory_space=pltpu.SMEM)
    specs = [smem if a.ndim == 1 else vmem for a in args]
    return pl.pallas_call(
        kernel,
        out_shape=jax.ShapeDtypeStruct(out_shape, jnp.float32),
        in_specs=specs,
        out_specs=vmem,
        scratch_shapes=[pltpu.VMEM(s, jnp.float32) for s in scratch],
    )(*args)


def zy_kernel(pen_z_ref, pen_y_ref, src_ref, out_ref, pad_ref, u_ref, w_ref, before_y=None, after_group=None):
    n_out = src_ref.shape[0]
    padc = KERNEL // 4
    pad_ref[...] = jnp.full(pad_ref.shape, jnp.inf, jnp.float32)
    pad_ref[padc:padc + n_out] = src_ref[...]
    lane = lax.broadcasted_iota(jnp.int32, src_ref.shape[1:], 1)
    sub = lax.broadcasted_iota(jnp.int32, src_ref.shape[1:], 0)
    sub_z = (lane // 8) % 4
    sub_y = lane % 8

    lane3 = lax.broadcasted_iota(jnp.int32, (8,) + tuple(src_ref.shape[1:]), 2)
    sub_z3 = (lane3 // 8) % 4
    sub_y3 = lane3 % 8
    build_rotations(pad_ref, u_ref, 4, lambda r, here, after: jnp.where(
        sub_z3 + r < 4, pltpu.roll(here, 128 - 8 * r, 2), pltpu.roll(after, 32 - 8 * r, 2)))

    def q_range(g0, group):
        lo = max(0, padc - 1 - (g0 + group - 1))
        hi = padc + n_out - 1 - g0
        return lo, hi

    scan_offsets(u_ref, pen_z_ref, out_ref, n_out, 16, 4, q_range)

    def wbody(i, carry):
        a0 = pl.multiple_of(i * 8, 8)
        v = out_ref[pl.ds(a0, 8)]
        w_ref[0, pl.ds(a0, 8)] = v
        for r in range(1, 8):
            w_ref[r, pl.ds(a0, 8)] = jnp.where(sub_y3 + r < 8, pltpu.roll(v, 128 - r, 2),
                                               pltpu.roll(pltpu.roll(v, 8 - r, 2), 7, 1))
        return carry

    lax.fori_loop(0, n_out // 8, wbody, 0)
    if before_y is not None:
        before_y()
    group = 8
    shifts = []
    for db in range(-8, 8):
        for dy in range(8):
            carry_in = (sub_y + dy >= 8).astype(jnp.int32)
            row = sub + db + carry_in
            valid = (row >= 0) & (row <= 7)
            shifts.append((db, dy, valid))

    def ybody(i, carry):
        a0 = pl.multiple_of(i * group, group)
        acc = [jnp.full(src_ref.shape[1:], jnp.inf, jnp.float32) for _ in range(group)]
        for db, dy, valid in shifts:
            penvec = jnp.where(valid, pen_y_ref[8 * db + dy + 64], jnp.inf)
            for g in range(group):
                v = w_ref[dy, a0 + g]
                if db % 8:
                    v = pltpu.roll(v, (8 - db) % 8, 0)
                acc[g] = jnp.minimum(acc[g], v + penvec)
        for g in range(group):
            out_ref[a0 + g] = acc[g]
        if after_group is not None:
            after_group(a0, group)
        return carry

    lax.fori_loop(0, n_out // group, ybody, 0)


class Exchange:
    def __init__(self, mid_ref, recv_ref, sems, grp_sems, count):
        self.n_gz, self.n_gy = lax.axis_size("gz"), lax.axis_size("gy")
        self.a, self.b = lax.axis_index("gz"), lax.axis_index("gy")
        self.mid_ref, self.recv_ref, self.sems = mid_ref, recv_ref, sems
        self.grp_sems, self.count = grp_sems, count
        self.barrier = pltpu.get_barrier_semaphore()

    def greet(self):
        a, b, n_gz, n_gy = self.a, self.b, self.n_gz, self.n_gy

        def greet_gy(k, carry):
            pl.semaphore_signal(self.barrier, inc=1, device_id=(a, lax.rem(b + k, n_gy)),
                                device_id_type=MESH)
            return carry

        def greet_gz(k, carry):
            pl.semaphore_signal(self.barrier, inc=1, device_id=(lax.rem(a + k, n_gz), b),
                                device_id_type=MESH)
            return carry

        lax.fori_loop(1, n_gy, greet_gy, 0)
        lax.fori_loop(1, n_gz, greet_gz, 0)

    def wait_greetings(self):
        pl.semaphore_wait(self.barrier, self.n_gy - 1 + self.n_gz - 1)

    def send_rows(self, tiles_ref, g, t0):
        a, b, n_gy, count = self.a, self.b, self.n_gy, self.count
        for k in range(1, n_gy):
            p = lax.rem(b + k, n_gy)
            pltpu.make_async_remote_copy(
                src_ref=tiles_ref.at[pl.ds(t0, count), pl.ds(p, 1)],
                dst_ref=self.mid_ref.at[pl.ds(t0, count), pl.ds(b, 1)], send_sem=self.sems.at[0],
                recv_sem=self.grp_sems.at[g], device_id=(a, p), device_id_type=MESH).start()
        own = pltpu.make_async_copy(tiles_ref.at[pl.ds(t0, count), pl.ds(b, 1)],
                                    self.mid_ref.at[pl.ds(t0, count), pl.ds(b, 1)], self.sems.at[2])
        own.start()
        own.wait()

    def forward_group(self, g, t0):
        a, b, n_gy, count = self.a, self.b, self.n_gy, self.count
        pltpu.make_async_remote_copy(
            src_ref=self.mid_ref.at[pl.ds(t0, count), pl.ds(0, n_gy - 1)],
            dst_ref=self.mid_ref.at[pl.ds(t0, count), pl.ds(0, n_gy - 1)], send_sem=self.sems.at[0],
            recv_sem=self.grp_sems.at[g], device_id=(a, lax.rem(b + 1, n_gy)),
            device_id_type=MESH).wait_recv()
        for j in range(count):
            p = t0 + j

            @pl.when(p != a)
            def _(p=p):
                pltpu.make_async_remote_copy(
                    src_ref=self.mid_ref.at[pl.ds(p, 1)], dst_ref=self.recv_ref.at[pl.ds(a, 1)],
                    send_sem=self.sems.at[3], recv_sem=self.sems.at[4], device_id=(p, b),
                    device_id_type=MESH).start()

    def finish(self, tiles_ref, out_ref, pending, transpose=False):
        a, b, n_gz, n_gy = self.a, self.b, self.n_gz, self.n_gy
        mid_ref, recv_ref, sems = self.mid_ref, self.recv_ref, self.sems
        groups = n_gz // self.count
        for g in range(groups - pending, groups):
            self.forward_group(g, g * self.count)
        pltpu.make_async_remote_copy(
            src_ref=tiles_ref.at[:, pl.ds(0, n_gy - 1)], dst_ref=mid_ref.at[:, pl.ds(0, n_gy - 1)],
            send_sem=sems.at[0], recv_sem=sems.at[1], device_id=(a, lax.rem(b + 1, n_gy)),
            device_id_type=MESH).wait_send()
        own = pltpu.make_async_copy(mid_ref.at[pl.ds(a, 1)], recv_ref.at[pl.ds(a, 1)], sems.at[5])
        own.start()
        own.wait()
        total = pltpu.make_async_remote_copy(
            src_ref=mid_ref.at[pl.ds(0, n_gz - 1)], dst_ref=recv_ref.at[pl.ds(0, n_gz - 1)],
            send_sem=sems.at[3], recv_sem=sems.at[4], device_id=(lax.rem(a + 1, n_gz), b),
            device_id_type=MESH)
        total.wait_recv()
        total.wait_send()
        if transpose:
            out_ref[...] = recv_ref[...].reshape(out_ref.shape[::-1]).T
        else:
            out_ref[...] = recv_ref[...]


def n_gz_groups(ex):
    return ex.n_gz // ex.count


def exchange_scratch(tiles_shape, groups):
    return [pltpu.VMEM(tiles_shape, jnp.float32)] * 3 + [pltpu.SemaphoreType.DMA((6,)),
                                                         pltpu.SemaphoreType.DMA((groups,))]


def xpass_send_kernel(pen_ref, src_ref, out_ref, pad_ref, u_ref, tiles_ref, mid_ref, recv_ref, sems, grp_sems):
    ex = Exchange(mid_ref, recv_ref, sems, grp_sems, 16)
    ex.greet()

    def after_group(g0, group):
        assert group == ex.count
        g = g0 // group
        if g == 0:
            ex.wait_greetings()
        ex.send_rows(tiles_ref, g, g0)
        if g >= 1:
            ex.forward_group(g - 1, g0 - group)

    xpass_kernel(pen_ref, src_ref, tiles_ref, pad_ref, u_ref, after_group)
    ex.finish(tiles_ref, out_ref, 1)


def zy_send_kernel(pen_z_ref, pen_y_ref, src_ref, out_ref, pad_ref, u_ref, w_ref, tiles_ref, mid_ref,
                   recv_ref, sems, grp_sems):
    ex = Exchange(mid_ref, recv_ref, sems, grp_sems, 8)
    ex.greet()

    def after_group(a0, group):
        assert group == ex.count
        g = a0 // group
        ex.send_rows(tiles_ref, g, a0)

        @pl.when(g >= 4)
        def _():
            ex.forward_group(g - 4, a0 - 4 * group)

    zy_kernel(pen_z_ref, pen_y_ref, src_ref, tiles_ref, pad_ref, u_ref, w_ref, ex.wait_greetings, after_group)
    ex.finish(tiles_ref, out_ref, 4, transpose=True)


def regularize(current):
    levels, nz, ny, nx = current.shape
    lines = levels * nz * ny
    n_gz = lax.axis_size("gz")
    n_gy = lax.axis_size("gy")
    assert lines == 128 and ny == 8 and n_gy == 8 and n_gz * n_gy == nx
    smem = pl.BlockSpec(memory_space=pltpu.SMEM)
    vmem = pl.BlockSpec(memory_space=pltpu.VMEM)
    tiles = (n_gz, n_gy, lines)
    xq = (KERNEL + 7) // 8
    nxo = nx // 8
    pen_x = penalty_table(8 * (xq * 2 + 2), KERNEL)
    xu = -(-(nxo + 2 * xq + 2) // 8) * 8
    r1 = pl.pallas_call(
        xpass_send_kernel,
        out_shape=jax.ShapeDtypeStruct(tiles, jnp.float32),
        in_specs=[smem, vmem],
        out_specs=vmem,
        scratch_shapes=[pltpu.VMEM((xu + 8, 8, lines), jnp.float32),
                        pltpu.VMEM((8, xu, 8, lines), jnp.float32)] + exchange_scratch(tiles, n_gz // 16),
        compiler_params=pltpu.CompilerParams(collective_id=1, has_side_effects=True),
    )(pen_x, current.reshape(lines, nx))
    zq = KERNEL // 4
    pen_z = penalty_table(4 * (2 * zq + 2), KERNEL)
    zu = -(-(n_gz + 2 * zq + 2) // 8) * 8
    pen_y = penalty_table(8 * 2 * n_gy, 8 * n_gy)
    r2 = pl.pallas_call(
        zy_send_kernel,
        out_shape=jax.ShapeDtypeStruct((lines, nx), jnp.float32),
        in_specs=[smem, smem, vmem],
        out_specs=vmem,
        scratch_shapes=[pltpu.VMEM((zu + 8, 8, lines), jnp.float32),
                        pltpu.VMEM((4, zu, 8, lines), jnp.float32),
                        pltpu.VMEM((8, n_gz, 8, lines), jnp.float32)] + exchange_scratch(tiles, n_gz // 8),
        compiler_params=pltpu.CompilerParams(collective_id=2, has_side_effects=True),
    )(pen_z, pen_y, r1)
    return r2.reshape(current.shape)


def body(levels, ct_image, region_means):
    current = evolve_all(levels, ct_image, region_means)
    return (current, regularize(current))


def solution(mesh):
    return jax.shard_map(
        body,
        mesh=mesh,
        in_specs=(P(None, "gz", "gy", None), P("gz", "gy", None), P()),
        out_specs=(P(None, "gz", "gy", None), P(None, "gz", "gy", None)),
        check_vma=False,
    )
```
